128 devices in a mesh: depth: 16 (over z, y), col: 8 (over x, core).
Axes of the slice: x: 4, y: 4, z: 4, core: 2. Of those that a mesh axis runs over, the one named last changes fastest.
Arguments:
- features: bfloat16 [16, 8, 8192, 256], P('depth', None, 'col'), may hold values from -6 to 6
- counts: int32 [16, 8192], P('depth', 'col'), may hold values from 0 to 8
- steps: float32 [16, 8192], P('depth', 'col'), may hold values from 0.01875 to 0.15
- target: float32 [8192, 512], P('col'), may hold values from -3 to 3
- w_in: bfloat16 [16, 256, 256], P('depth'), may hold values from -0.375 to 0.375
- w_density: bfloat16 [16, 256], P('depth'), may hold values from -0.375 to 0.375
- w_out: bfloat16 [16, 256, 512], P('depth'), may hold values from -0.375 to 0.375
Outputs:
- residual: float32 [8192, 512], P('col')
- density_grad: float32 [16, 8, 8192], P('depth', None, 'col')
- grad_in: float32 [16, 256, 256], P('depth', 'col')
- grad_density: float32 [16, 256], P('depth', 'col')
- grad_out: float32 [16, 256, 512], P('depth', 'col')
The draws below stay inside these ranges and needn't reach their ends.
Inputs may be any that keep to these rules, and one draw needn't show every extreme that they name: `counts`: a count of 0 means that the ray misses the brick.
All inputs are finite; a program needn't handle non-finite values.
Results may differ from the reference program's by a relative error of at most 0.0019.
Values sent between devices are 32-bit elements; how exact they have to be, the bound alone decides.
A program may use at most 128 MiB of HBM per device.

```python
import math
import jax
import jax.numpy as jnp
from jax import lax

DIN = 256
HID = 256
C = 512
S = 8
BRICKS = 16
RAYS_TOT = 8192


def touch_ends(drawn, stream_key, least, largest):
    index_at = [jax.random.randint(jax.random.fold_in(stream_key, axis), (), 0, length) for axis, length in enumerate(drawn.shape)]
    longest = drawn.shape.index(max(drawn.shape))
    next_to = index_at[:longest] + [(index_at[longest] + 1) % drawn.shape[longest]] + index_at[longest + 1:]
    return drawn.at[tuple(index_at)].set(least).at[tuple(next_to)].set(largest)


def shard_levels(stream_key, shape, cuts, low, largest):
    level = 1.0
    for dim, parts in cuts:
        heights = jax.random.uniform(jax.random.fold_in(jax.random.fold_in(stream_key, 6), dim), (parts,), jnp.float32, low / len(cuts), largest / len(cuts))
        level = level * jnp.repeat(jnp.exp(heights), shape[dim] // parts).reshape((-1,) + (1,) * (len(shape) - 1 - dim))
    return level


def gaussian(stream_key, extent, deviation, bound, split=(), dtype=jnp.bfloat16):
    level = shard_levels(stream_key, extent, split, -0.22, 0.18) if split else 1.0
    values = jax.random.normal(stream_key, extent, jnp.float32) * deviation * level
    return jnp.minimum(jnp.maximum(values, -bound), bound).astype(dtype)


def setup_inputs(seed: int = 0) -> dict:
    key_list = jax.random.split(jax.random.key(seed), 8)
    features = gaussian(key_list[0], (BRICKS, S, RAYS_TOT, DIN), 1.0, 6.0, ((0, 16), (2, 8)))
    counts = touch_ends(jax.random.randint(key_list[1], (BRICKS, RAYS_TOT), 0, S + 1), jax.random.fold_in(key_list[1], 1), 0, S).astype(jnp.int32)
    steps = jnp.clip(jnp.exp(math.log(0.15) - 2.0794415 * jax.random.uniform(key_list[2], (BRICKS, RAYS_TOT), jnp.float32) ** shard_levels(key_list[2], (BRICKS, RAYS_TOT), ((0, 16), (1, 8)), -0.2, 0.2)), 0.01875, 0.15)
    target = gaussian(key_list[3], (RAYS_TOT, C), 0.5, 3.0, ((0, 8),), jnp.float32)
    w_in = gaussian(key_list[4], (BRICKS, DIN, HID), DIN ** -0.5, 0.375, ((0, 16),))
    w_density = gaussian(key_list[5], (BRICKS, HID), HID ** -0.5, 0.375, ((0, 16),))
    w_out = gaussian(key_list[6], (BRICKS, HID, C), HID ** -0.5, 0.375, ((0, 16),))
    return {"features": features, "counts": counts, "steps": steps, "target": target, "w_in": w_in, "w_density": w_density, "w_out": w_out}


def brick_forward(feat_b, w_in_b, w_den_b, w_out_b, count_b, step_b):
    rows = feat_b.reshape(-1, feat_b.shape[-1])
    pre = jnp.dot(rows, w_in_b, preferred_element_type=jnp.float32)
    hidden = jnp.maximum(pre, 0.0).astype(jnp.bfloat16)
    sig_pre = jnp.dot(hidden, w_den_b, preferred_element_type=jnp.float32).reshape(S, -1)
    valid = (lax.broadcasted_iota(jnp.int32, sig_pre.shape, 0) < count_b[None, :]).astype(jnp.float32)
    tau = jax.nn.softplus(sig_pre) * step_b[None, :] * valid
    return rows, pre, hidden, sig_pre, valid, tau


def exclusive(values):
    total = jnp.cumsum(values, 0)
    return jnp.concatenate([jnp.zeros_like(values[:1]), total[:-1]], 0)


def reference(features, counts, steps, target, w_in, w_density, w_out):
    def first(args):
        feat_b, w_in_b, w_den_b, count_b, step_b = args
        return brick_forward(feat_b, w_in_b, w_den_b, None, count_b, step_b)[5]

    taus = lax.map(first, (features, w_in, w_density, counts, steps))
    before_all = exclusive(jnp.sum(taus, 1))

    def weights_of(tau, before_b):
        inner = exclusive(tau)
        trans = jnp.exp(-(before_b[None, :] + inner))
        keep = jnp.exp(-tau)
        return trans, keep, trans * (1.0 - keep)

    def second(carry, args):
        feat_b, w_in_b, w_den_b, w_out_b, count_b, step_b, before_b = args
        rows, pre, hidden, sig_pre, valid, tau = brick_forward(feat_b, w_in_b, w_den_b, w_out_b, count_b, step_b)
        feat = jnp.dot(hidden, w_out_b, preferred_element_type=jnp.float32).reshape(S, -1, C)
        trans, keep, wgt = weights_of(tau, before_b)
        return carry + jnp.sum(wgt[:, :, None] * feat, 0), None

    pixel, _ = lax.scan(second, jnp.zeros((features.shape[2], C), jnp.float32),
                        (features, w_in, w_density, w_out, counts, steps, before_all))
    residual = pixel - target

    def third(args):
        feat_b, w_in_b, w_den_b, w_out_b, count_b, step_b, before_b = args
        rows, pre, hidden, sig_pre, valid, tau = brick_forward(feat_b, w_in_b, w_den_b, w_out_b, count_b, step_b)
        feat = jnp.dot(hidden, w_out_b, preferred_element_type=jnp.float32).reshape(S, -1, C)
        trans, keep, wgt = weights_of(tau, before_b)
        emission = jnp.sum(feat * residual[None], 2)
        return jnp.sum(wgt * emission, 0)

    owns = lax.map(third, (features, w_in, w_density, w_out, counts, steps, before_all))
    after_all = jnp.flip(exclusive(jnp.flip(owns, 0)), 0)

    def fourth(args):
        feat_b, w_in_b, w_den_b, w_out_b, count_b, step_b, before_b, after_b = args
        rows, pre, hidden, sig_pre, valid, tau = brick_forward(feat_b, w_in_b, w_den_b, w_out_b, count_b, step_b)
        feat = jnp.dot(hidden, w_out_b, preferred_element_type=jnp.float32).reshape(S, -1, C)
        trans, keep, wgt = weights_of(tau, before_b)
        emission = jnp.sum(feat * residual[None], 2)
        part = wgt * emission
        later_local = jnp.flip(exclusive(jnp.flip(part, 0)), 0)
        dens = (trans * keep * emission - (later_local + after_b[None, :])) * step_b[None, :] * valid
        dsig = dens * jax.nn.sigmoid(sig_pre)
        dfeat = (wgt[:, :, None] * residual[None]).astype(jnp.bfloat16).reshape(-1, C)
        dhid = jnp.einsum("nc,hc->nh", dfeat.astype(jnp.float32), w_out_b.astype(jnp.float32))
        dhid = dhid + dsig.reshape(-1)[:, None] * w_den_b.astype(jnp.float32)[None, :]
        dpre = jnp.where(pre > 0, dhid, 0.0).astype(jnp.bfloat16)
        g_out = jnp.einsum("nh,nc->hc", hidden.astype(jnp.float32), dfeat.astype(jnp.float32))
        g_in = jnp.einsum("nd,nh->dh", rows.astype(jnp.float32), dpre.astype(jnp.float32))
        g_den = jnp.dot(dsig.reshape(-1), hidden.astype(jnp.float32))
        return dens, g_in, g_den, g_out

    dens, g_in, g_den, g_out = lax.map(fourth, (features, w_in, w_density, w_out, counts, steps, before_all, after_all))
    return residual, dens, g_in, g_den, g_out
```

```python
import jax
import jax.numpy as jnp
from jax import lax
from jax.sharding import PartitionSpec as P


def sent_to_all(shard, axis):
    count = lax.axis_size(axis)
    return lax.all_to_all(
        jnp.broadcast_to(shard[None], (count, *shard.shape)), axis, 0, 0, tiled=True
    )


def combined_pairwise(pieces, combine):
    while len(jax.tree.leaves(pieces)[0]) > 1:
        pieces = jax.vmap(combine)(*(pieces[side::2] for side in (0, 1)))
    return pieces[0]


def carried_in(shard, axis, combine, identity, reverse):
    count, index = (lax.axis_size(axis), lax.axis_index(axis))
    passed = jnp.arange(count) > index if reverse else jnp.arange(count) < index

    def kept(part, zero, own):
        part = jnp.where(
            passed.reshape(-1, *(1 for _ in own.shape)), part, jnp.asarray(zero, own.dtype)
        )
        return part[::-1] if reverse else part

    pieces = sent_to_all(shard, axis)
    return combined_pairwise(kept(pieces, identity, shard), combine)


def split_up(shard, dim, count):
    dims = shard.shape
    tiles = shard.reshape(*dims[:dim], count, dims[dim] // count, *dims[dim + 1 :])
    return jnp.moveaxis(tiles, dim, 0)


def sent_and_summed(shard, axis, dim):
    count = lax.axis_size(axis)
    tiles = lax.all_to_all(split_up(shard, dim, count), axis, 0, 0, tiled=True)
    return jnp.sum(tiles, axis=0)


def joined_along(tiles, dim):
    dims = list(tiles.shape[1:])
    dims[dim] *= tiles.shape[0]
    return jnp.moveaxis(tiles, 0, dim).reshape(dims)


def gathered_copies(shard, axis, dim):
    return joined_along(sent_to_all(shard, axis), dim)


def in_one_piece(arrays, axis, dim, along):
    both = jnp.concatenate(arrays, axis=along)
    result, at, outs = (lax.psum_scatter(both, axis, scatter_dimension=dim, tiled=True), 0, [])
    for a in arrays:
        outs.append(lax.slice_in_dim(result, at, at + a.shape[along], axis=along))
        at += a.shape[along]
    return tuple(outs)


def exclusive(values):
    total = jnp.cumsum(values, 0)
    return jnp.concatenate([jnp.zeros_like(values[:1]), total[:-1]], 0)


def adding(earlier, later_val):
    return earlier + later_val


def split_two(x):
    high = lax.reduce_precision(x, 8, 7)
    low = x - high
    return high.astype(jnp.bfloat16), low.astype(jnp.bfloat16)


def dot_of(a, b, dims):
    return lax.dot_general(a, b, (dims, ((), ())), preferred_element_type=jnp.float32)


def per_device(features, counts, steps, target, w_in, w_density, w_out):
    smp = features.shape[1]
    nray = features.shape[2]
    rows = features.reshape(smp * nray, features.shape[3])
    pre = jnp.dot(rows, w_in[0], preferred_element_type=jnp.float32)
    hidden = jnp.maximum(pre, 0.0).astype(jnp.bfloat16)
    sig_pre = jnp.dot(hidden, w_density[0], preferred_element_type=jnp.float32).reshape(smp, nray)
    valid = (lax.broadcasted_iota(jnp.int32, (smp, nray), 0) < counts[0][None, :]).astype(
        jnp.float32
    )
    step_row = steps[0][None, :]
    tau = jax.nn.softplus(sig_pre) * step_row * valid
    inner = exclusive(tau)
    brick_total = jnp.sum(tau, 0)
    position = lax.axis_index("depth")
    before = carried_in(brick_total, "depth", adding, jnp.zeros_like(brick_total), False)
    keep = jnp.exp(-tau)
    trans = jnp.exp(-(before[None, :] + inner))
    wgt = trans * (1.0 - keep)
    hid3 = hidden.reshape(smp, nray, -1)
    hbar = jnp.sum(wgt[:, :, None] * hid3, 0)
    hb_hi, hb_lo = split_two(hbar)
    by_cols = ((1,), (0,))
    partial_value = dot_of(hb_hi, w_out[0], by_cols) + dot_of(hb_lo, w_out[0], by_cols)
    share = sent_and_summed(partial_value, "depth", 0)
    owned = share.shape[0]
    mine = lax.dynamic_slice_in_dim(target, position * owned, owned, 0)
    residual = gathered_copies(share - mine, "depth", 0)
    re_hi, re_lo = split_two(residual)
    v = dot_of(re_hi, w_out[0], ((1,), (1,))) + dot_of(re_lo, w_out[0], ((1,), (1,)))
    emission = jnp.sum(hid3 * v[None], 2)
    part = wgt * emission
    own = jnp.sum(part, 0)
    after = carried_in(own, "depth", adding, jnp.zeros_like(own), True)
    later_local = jnp.flip(exclusive(jnp.flip(part, 0)), 0)
    dens = (trans * keep * emission - (later_local + after[None, :])) * step_row * valid
    dsig = dens * jax.nn.sigmoid(sig_pre)
    dhid = wgt[:, :, None] * v[None] + dsig[:, :, None] * w_density[0].astype(jnp.float32)
    dpre = jnp.where(hid3 > 0, dhid, 0.0).astype(jnp.bfloat16).reshape(smp * nray, -1)
    first = ((0,), (0,))
    g_out = dot_of(hb_hi, re_hi, first) + dot_of(hb_lo, re_hi, first) + dot_of(hb_hi, re_lo, first)
    g_in = dot_of(rows, dpre, first)
    g_den = jnp.sum(dsig.reshape(-1)[:, None] * hidden.astype(jnp.float32), 0)
    tiles = lax.all_to_all(jnp.concatenate([g_in, g_out, jnp.broadcast_to(g_den[:, None], (256, 128))], 1), "col", 0, 0, tiled=True)
    got = jnp.sum(tiles.reshape(8, 32, -1), 0)
    return (residual, dens[None], got[None, :, :256], got[None, :, 768], got[None, :, 256:768])


def solution(mesh):
    return jax.shard_map(
        per_device,
        mesh=mesh,
        in_specs=(
            P("depth", None, "col", None),
            P("depth", "col"),
            P("depth", "col"),
            P("col", None),
            P("depth", None, None),
            P("depth", None),
            P("depth", None, None),
        ),
        out_specs=(
            P("col", None),
            P("depth", None, "col"),
            P("depth", "col", None),
            P("depth", "col"),
            P("depth", "col", None),
        ),
        check_vma=False,
    )
```

```python
import functools

import jax
import jax.numpy as jnp
from jax import lax
from jax.experimental import pallas as pl
from jax.experimental.pallas import tpu as pltpu
from jax.sharding import PartitionSpec as P

STREAMS = 2
PARTS = 4
BLOCKS = 16
LANES = 128
F32 = jnp.float32
BF16 = jnp.bfloat16
NT = (((1,), (1,)), ((), ()))
TN = (((0,), (0,)), ((), ()))
NN = (((1,), (0,)), ((), ()))


def mm(a, b, dims):
    return lax.dot_general(a, b, dims, preferred_element_type=F32)


def halves(x):
    high = x.astype(BF16)
    return high, (x - high.astype(F32)).astype(BF16)


def place(part, block):
    at = 0
    for turn in range(4):
        at = at * 2 + (block // 2 ** ((part + turn) % 4)) % 2
    return at


def block_at(part, at):
    block = 0
    for turn in range(4):
        block = block + (at // 2 ** (3 - turn)) % 2 * 2 ** ((part + turn) % 4)
    return block


def running(x, reverse):
    rows = x.shape[0]
    row = lax.broadcasted_iota(jnp.int32, x.shape, 0)
    total = x
    hop = 1
    while hop < rows:
        moved = pltpu.roll(total, rows - hop if reverse else hop, 0)
        total = total + jnp.where(row < rows - hop if reverse else row >= hop, moved, 0.0)
        hop *= 2
    edge = row < rows - 1 if reverse else row >= 1
    return jnp.where(edge, pltpu.roll(total, rows - 1 if reverse else 1, 0), 0.0)


def body(f_hbm, cnt_ref, step_ref, tgt_hbm, win_ref, wden_ref, wout_ref,
         res_hbm, dens_ref, gin_ref, gden_ref, gout_ref,
         f_ref, hid_ref, lwt_ref, hbar_ref, p_ref, acc_ref, recv_ref, r_ref, res_ref, tgt_ref,
         t_all, own_all, ecol_ref, keep_ref, v_ref, emt_ref, wt_ref, dt_ref, dpre_ref,
         gi_ref, go_ref, gi_recv, go_recv,
         f_sem, tgt_sem, res_sem, s_sem, r_sem, as_sem, ar_sem, ts_sem, tr_sem, os_sem, or_sem,
         gs_sem, gr_sem):
    smp, ray, rows = f_ref.shape[1], f_ref.shape[2], f_ref.shape[2] // BLOCKS
    hid = win_ref.shape[1]
    slab = gin_ref.shape[0]
    me = lax.axis_index("depth")
    col = lax.axis_index("col")
    y, z = me % 4, me // 4
    bits = ((y // 2 + y % 2) % 2, y // 2, (z // 2 + z % 2) % 2, z // 2)
    partners = (z * 4 + y + 1 - 2 * (y % 2), z * 4 + 3 - y,
                (z + 1 - 2 * (z % 2)) * 4 + y, (3 - z) * 4 + y)
    home = bits[0] + 2 * bits[1] + 4 * bits[2] + 8 * bits[3]
    mesh_id = pl.DeviceIdType.MESH

    barrier = pltpu.get_barrier_semaphore()

    def greet_depth(j, _):
        pl.semaphore_signal(barrier, inc=1, device_id={"depth": (me + j) % BLOCKS}, device_id_type=mesh_id)
        return 0

    def greet_col(j, _):
        pl.semaphore_signal(barrier, inc=1, device_id={"col": (col + j) % 8}, device_id_type=mesh_id)
        return 0

    lax.fori_loop(1, BLOCKS, greet_depth, 0)
    lax.fori_loop(1, 8, greet_col, 0)

    def fetch(s, i):
        return pltpu.make_async_copy(
            f_hbm.at[i, pl.ds(s * ray, ray)], f_ref.at[s, i], f_sem.at[s, i])

    def fetch_target(s):
        return pltpu.make_async_copy(
            tgt_hbm.at[s, home], tgt_ref.at[s], tgt_sem.at[s])

    for s in range(STREAMS):
        for i in range(smp):
            fetch(s, i).start()
    for s in range(STREAMS):
        fetch_target(s).start()

    def to_depth(src, dst, send, recv, who):
        return pltpu.make_async_remote_copy(
            src_ref=src, dst_ref=dst, send_sem=send, recv_sem=recv,
            device_id={"depth": who}, device_id_type=mesh_id)

    def spread(store, s, send, recv, j):
        return to_depth(store.at[s, me], store.at[s, me], send.at[s, j], recv.at[s, j], (me + j) % BLOCKS)

    def spread_start(store, s, send, recv):
        def one(j, _):
            spread(store, s, send, recv, j).start()
            return 0
        lax.fori_loop(1, BLOCKS, one, 0)

    def spread_wait(store, s, send, recv):
        def one(j, _):
            spread(store, s, send, recv, j).wait()
            return 0
        lax.fori_loop(1, BLOCKS, one, 0)

    recv_at = (0, 8, 12, 14)

    def span(p, turn):
        at = 0
        for t in range(turn):
            at = at + bits[(p + t) % 4] * (8 >> t)
        return at

    def reduce_copy(s, p, turn):
        half = 8 >> turn
        d = (p + turn) % 4
        away = (1 - bits[d]) * half
        if turn == 0:
            src = p_ref.at[s, p, pl.ds(away, half)]
        else:
            base = span(p, turn) - span(p, 1)
            src = acc_ref.at[s, p, pl.ds(base + away, half)]
        return to_depth(src, recv_ref.at[s, p, pl.ds(recv_at[turn], half)],
                        s_sem.at[s, p, turn], r_sem.at[s, p, turn], partners[d])

    def gather_copy(s, p, turn):
        half = 8 >> turn
        d = (p + turn) % 4
        mine = r_ref.at[s, p, pl.ds(span(p, turn + 1), half)]
        return to_depth(mine, mine, as_sem.at[s, p, turn], ar_sem.at[s, p, turn], partners[d])

    wden = jnp.broadcast_to(wden_ref[...].astype(F32), (smp, hid))
    sample = lax.broadcasted_iota(jnp.int32, (smp, hid), 0)

    def forward(s):
        sig = jnp.zeros((smp, ray), F32)
        for i in range(smp):
            fetch(s, i).wait()
            pre = mm(f_ref[s, i], win_ref[...], NN)
            h = jnp.maximum(pre, 0.0).astype(BF16)
            hid_ref[s, i] = h
            sig = sig + mm(jnp.where(sample == i, wden, 0.0).astype(BF16), h, NT)
        here = pl.ds(s * ray, ray)
        row = lax.broadcasted_iota(jnp.int32, (smp, ray), 0)
        gate = jnp.where(row < cnt_ref[:, here], jnp.broadcast_to(step_ref[:, here], (smp, ray)), 0.0)
        soft = jnp.maximum(sig, 0.0) + jnp.log1p(jnp.exp(-jnp.abs(sig)))
        tau = soft * gate
        inner = running(tau, False)
        t_all[s, me] = (inner + tau)[smp - 1:smp]
        keep = jnp.exp(-tau)
        light = jnp.exp(-inner)
        lw = light * (1.0 - keep)
        keep_ref[s, 0] = lw
        keep_ref[s, 1] = light * keep
        keep_ref[s, 2] = sig
        keep_ref[s, 3] = gate
        lwt_ref[...] = lw.T

    def weigh(s):
        def tile(t, _):
            at = pl.ds(pl.multiple_of(t * 64, 64), 64)
            w = lwt_ref[at]
            total = jnp.zeros((64, hid), F32)
            for i in range(smp):
                total = total + w[:, i:i + 1] * hid_ref[s, i, at].astype(F32)
            hbar_ref[s, at] = total
            return 0
        lax.fori_loop(0, ray // 64, tile, 0)
        high, low = halves(hbar_ref[s])
        value = mm(high, wout_ref[...], NN) + mm(low, wout_ref[...], NN)
        for n in range(BLOCKS):
            for p in range(PARTS):
                p_ref[s, p, place(p, n)] = value[n * rows:(n + 1) * rows, p * LANES:(p + 1) * LANES]

    def depths(s):
        spread_wait(t_all, s, ts_sem, tr_sem)
        whole = t_all[s]
        brick = lax.broadcasted_iota(jnp.int32, whole.shape, 0)
        out = [jnp.exp(-jnp.sum(jnp.where(brick < who, whole, 0.0), 0)) for who in (me, *partners)]
        row = lax.broadcasted_iota(jnp.int32, (smp, ray), 0)
        table = jnp.zeros((smp, ray), F32)
        for i, e in enumerate(out):
            table = jnp.where(row == i, jnp.broadcast_to(e, (smp, ray)), table)
        keep_ref[s, 4] = jnp.broadcast_to(out[0], (smp, ray))
        ecol_ref[s] = table.T.reshape(BLOCKS, rows, smp)

    def combine_first(s, p):
        first = span(p, 1)

        def one(i, _):
            e = ecol_ref[s, block_at(p, first + i)]
            acc_ref[s, p, i] = (e[:, :1] * p_ref[s, p, first + i]
                                + e[:, p + 1:p + 2] * recv_ref[s, p, i])
            return 0
        lax.fori_loop(0, 8, one, 0, unroll=True)

    def combine(s, p, turn):
        base = span(p, turn + 1) - span(p, 1)
        half = 8 >> turn
        here = pl.ds(base, half)
        acc_ref[s, p, here] = acc_ref[s, p, here] + recv_ref[s, p, pl.ds(recv_at[turn], half)]

    def reduce_turn(s, turn):
        for p in range(PARTS):
            reduce_copy(s, p, turn).wait()
            if turn == 0:
                combine_first(s, p)
            else:
                combine(s, p, turn)
            if turn < 3:
                reduce_copy(s, p, turn + 1).start()
            else:
                if p == 0:
                    fetch_target(s).wait()
                at = span(p, 4)
                r_ref[s, p, at] = (acc_ref[s, p, at - span(p, 1)]
                                   - tgt_ref[s, :, p * LANES:(p + 1) * LANES])
                gather_copy(s, p, 3).start()

    def gather_turn(s, turn):
        for p in range(PARTS):
            gather_copy(s, p, turn).wait()
            if turn > 0:
                gather_copy(s, p, turn - 1).start()

    def put_residual(s):
        return pltpu.make_async_copy(res_ref.at[s], res_hbm.at[s], res_sem.at[s])

    def own_terms(s):
        def one(n, _):
            here = pl.ds(pl.multiple_of(n * rows, rows), rows)
            total = jnp.zeros((rows, LANES), F32)
            for p in range(PARTS):
                at = place(p, n)
                r = r_ref[s, p, at]
                res_ref[s, here, p * LANES:(p + 1) * LANES] = r
                total = total + r * p_ref[s, p, at]
            emt_ref[here] = total
            return 0
        lax.fori_loop(0, BLOCKS, one, 0)
        put_residual(s).start()
        high, low = halves(emt_ref[...])
        ones = jnp.ones((smp, LANES), BF16)
        own = (mm(ones, high, NT) + mm(ones, low, NT)) * keep_ref[s, 4]
        own_all[s, me] = own[:1]
        spread_start(own_all, s, os_sem, or_sem)

    def emissions(s):
        r_high, r_low = halves(res_ref[s])
        v_ref[s] = mm(r_high, wout_ref[...], NT) + mm(r_low, wout_ref[...], NT)
        scaled = hbar_ref[s] * jnp.concatenate(
            [ecol_ref[s, n][:, :1] for n in range(BLOCKS)], 0)
        b_high, b_low = halves(scaled)
        out = mm(b_high, r_high, TN) + mm(b_low, r_high, TN) + mm(b_high, r_low, TN)
        for c in range(8):
            mine = out[c * slab:(c + 1) * slab]
            go_ref[c] = mine if s == 0 else go_ref[c] + mine

        def tile(t, _):
            at = pl.ds(pl.multiple_of(t * 64, 64), 64)
            v = v_ref[s, at]
            lane = lax.broadcasted_iota(jnp.int32, (64, smp), 1)
            found = jnp.zeros((64, smp), F32)
            for i in range(smp):
                e = jnp.sum(v * hid_ref[s, i, at].astype(F32), 1, keepdims=True)
                found = jnp.where(lane == i, e, found)
            wt_ref[at] = found
            return 0
        lax.fori_loop(0, ray // 64, tile, 0)
        keep_ref[s, 5] = wt_ref[...].T

    def gradients(s):
        spread_wait(own_all, s, os_sem, or_sem)
        whole = own_all[s]
        brick = lax.broadcasted_iota(jnp.int32, whole.shape, 0)
        after = jnp.sum(jnp.where(brick > me, whole, 0.0), 0)
        e = keep_ref[s, 4]
        em = keep_ref[s, 5]
        wgt = keep_ref[s, 0] * e
        later = running(wgt * em, True) + after
        dens = (keep_ref[s, 1] * e * em - later) * keep_ref[s, 3]
        dens_ref[:, pl.ds(s * ray, ray)] = dens
        dsig = dens / (1.0 + jnp.exp(-keep_ref[s, 2]))
        wt_ref[...] = wgt.T
        dt_ref[...] = dsig.T
        wden_row = wden_ref[...].astype(F32)

        def tile(t, _):
            at = pl.ds(pl.multiple_of(t * 32, 32), 32)
            v = v_ref[s, at]
            w = wt_ref[at]
            d = dt_ref[at]
            for i in range(smp):
                dh = w[:, i:i + 1] * v + d[:, i:i + 1] * wden_row
                h = hid_ref[s, i, at].astype(F32)
                dpre_ref[i, at] = jnp.where(h > 0.0, dh, 0.0).astype(BF16)
            return 0
        lax.fori_loop(0, ray // 32, tile, 0)
        g_in = mm(f_ref[s].reshape(smp * ray, -1), dpre_ref[...].reshape(smp * ray, hid), TN)
        d_high, d_low = halves(dsig)
        stacked = jnp.concatenate([d_high.astype(F32), d_low.astype(F32)], 0)
        row = lax.broadcasted_iota(jnp.int32, stacked.shape, 0)
        g_den = jnp.zeros((2 * smp, hid), F32)
        for i in range(smp):
            g_den = g_den + mm(jnp.where(row % smp == i, stacked, 0.0).astype(BF16), hid_ref[s, i], NN)
        g_den = g_den[:smp] + g_den[smp:]
        for c in range(8):
            mine = g_in[c * slab:(c + 1) * slab]
            if s == 0:
                gi_ref[c, :slab] = mine
                gi_ref[c, slab:] = g_den
            else:
                gi_ref[c, :slab] = gi_ref[c, :slab] + mine
                gi_ref[c, slab:] = gi_ref[c, slab:] + g_den

    def share(kind, j):
        src, dst = ((gi_ref, gi_recv), (go_ref, go_recv))[kind]
        to = (col + j) % 8
        return pltpu.make_async_remote_copy(
            src_ref=src.at[to], dst_ref=dst.at[j - 1], send_sem=gs_sem.at[kind, j],
            recv_sem=gr_sem.at[kind, j], device_id={"col": to}, device_id_type=mesh_id)

    def share_all(kind, wait):
        def one(j, _):
            if wait:
                share(kind, j).wait()
            else:
                share(kind, j).start()
            return 0
        lax.fori_loop(1, 8, one, 0)

    for s in range(STREAMS):
        forward(s)
        if s == 0:
            pl.semaphore_wait(barrier, BLOCKS - 1 + 7)
        spread_start(t_all, s, ts_sem, tr_sem)
        weigh(s)
        for p in range(PARTS):
            reduce_copy(s, p, 0).start()
    for turn in range(4):
        for s in range(STREAMS):
            if turn == 0:
                depths(s)
            reduce_turn(s, turn)
    for turn in (3, 2, 1):
        for s in range(STREAMS):
            gather_turn(s, turn)
    gather_turn(0, 0)
    own_terms(0)
    emissions(0)
    for s in range(1, STREAMS):
        gather_turn(s, 0)
        own_terms(s)
        gradients(s - 1)
        emissions(s)
    share_all(1, False)
    gradients(STREAMS - 1)
    share_all(0, False)
    share_all(1, True)
    total = go_ref[col]
    for j in range(7):
        total = total + go_recv[j]
    gout_ref[...] = total
    share_all(0, True)
    total = gi_ref[col]
    for j in range(7):
        total = total + gi_recv[j]
    gin_ref[...] = total[:slab]
    den = jnp.sum(total[slab:], 0, keepdims=True)
    mine = den[:, :slab]
    for c in range(1, 8):
        mine = jnp.where(col == c, den[:, c * slab:(c + 1) * slab], mine)
    gden_ref[...] = mine
    for s in range(STREAMS):
        put_residual(s).wait()


def per_device(features, counts, steps, target, w_in, w_density, w_out):
    _, smp, nray, din = features.shape
    hid, width = w_out.shape[1:]
    ray = nray // STREAMS
    rows = ray // BLOCKS
    slab = din // 8
    vmem = pl.BlockSpec(memory_space=pltpu.VMEM)
    hbm = pl.BlockSpec(memory_space=pl.ANY)
    dma = pltpu.SemaphoreType.DMA
    stage = (STREAMS, PARTS)
    scratch = [
        pltpu.VMEM((STREAMS, smp, ray, din), BF16),
        pltpu.VMEM((STREAMS, smp, ray, hid), BF16),
        pltpu.VMEM((ray, smp), F32),
        pltpu.VMEM((STREAMS, ray, hid), F32),
        pltpu.VMEM((*stage, BLOCKS, rows, LANES), F32),
        pltpu.VMEM((*stage, BLOCKS // 2, rows, LANES), F32),
        pltpu.VMEM((*stage, BLOCKS - 1, rows, LANES), F32),
        pltpu.VMEM((*stage, BLOCKS, rows, LANES), F32),
        pltpu.VMEM((STREAMS, ray, width), F32),
        pltpu.VMEM((STREAMS, rows, width), F32),
        pltpu.VMEM((STREAMS, BLOCKS, 1, ray), F32),
        pltpu.VMEM((STREAMS, BLOCKS, 1, ray), F32),
        pltpu.VMEM((STREAMS, BLOCKS, rows, smp), F32),
        pltpu.VMEM((STREAMS, 6, smp, ray), F32),
        pltpu.VMEM((STREAMS, ray, hid), F32),
        pltpu.VMEM((ray, LANES), F32),
        pltpu.VMEM((ray, smp), F32),
        pltpu.VMEM((ray, smp), F32),
        pltpu.VMEM((smp, ray, hid), BF16),
        pltpu.VMEM((8, slab + smp, hid), F32),
        pltpu.VMEM((8, slab, width), F32),
        pltpu.VMEM((7, slab + smp, hid), F32),
        pltpu.VMEM((7, slab, width), F32),
        dma((STREAMS, smp)), dma((STREAMS,)), dma((STREAMS,)),
        dma((*stage, 4)), dma((*stage, 4)), dma((*stage, 4)), dma((*stage, 4)),
        dma((STREAMS, BLOCKS)), dma((STREAMS, BLOCKS)), dma((STREAMS, BLOCKS)), dma((STREAMS, BLOCKS)),
        dma((2, 8)), dma((2, 8)),
    ]
    residual, dens, g_in, g_den, g_out = pl.pallas_call(
        body,
        out_shape=(
            jax.ShapeDtypeStruct((STREAMS, ray, width), F32),
            jax.ShapeDtypeStruct((smp, nray), F32),
            jax.ShapeDtypeStruct((slab, hid), F32),
            jax.ShapeDtypeStruct((1, slab), F32),
            jax.ShapeDtypeStruct((slab, width), F32),
        ),
        in_specs=[hbm, vmem, vmem, hbm, vmem, vmem, vmem],
        out_specs=(hbm, vmem, vmem, vmem, vmem),
        scratch_shapes=scratch,
        compiler_params=pltpu.CompilerParams(
            collective_id=0, has_side_effects=True, vmem_limit_bytes=60 * 1024 * 1024),
        name="brick_step",
    )(features[0], counts, steps, target.reshape(STREAMS, BLOCKS, rows, width),
      w_in[0], w_density, w_out[0])
    return residual.reshape(nray, width), dens[None], g_in[None], g_den, g_out[None]


def solution(mesh):
    return jax.shard_map(
        per_device,
        mesh=mesh,
        in_specs=(
            P("depth", None, "col", None),
            P("depth", "col"),
            P("depth", "col"),
            P("col", None),
            P("depth", None, None),
            P("depth", None),
            P("depth", None, None),
        ),
        out_specs=(
            P("col", None),
            P("depth", None, "col"),
            P("depth", "col", None),
            P("depth", "col"),
            P("depth", "col", None),
        ),
        check_vma=False,
    )
```

```python
import functools

import jax
import jax.numpy as jnp
from jax import lax
from jax.experimental import pallas as pl
from jax.experimental.pallas import tpu as pltpu
from jax.sharding import PartitionSpec as P

STREAMS = 4
RING = 4
BRICKS = 16
COLS = 8
ORDER = ((0, 0), (0, 1), (0, 2), (1, 0), (0, 3), (1, 1), (1, 2), (2, 0), (1, 3), (2, 1), (2, 2), (2, 3))
F32 = jnp.float32
BF16 = jnp.bfloat16
NT = (((1,), (1,)), ((), ()))
TN = (((0,), (0,)), ((), ()))
NN = (((1,), (0,)), ((), ()))


def mm(a, b, dims):
    return lax.dot_general(a, b, dims, preferred_element_type=F32)


def halves(x):
    high = x.astype(BF16)
    return high, (x - high.astype(F32)).astype(BF16)


def running(x, reverse):
    rows = x.shape[0]
    row = lax.broadcasted_iota(jnp.int32, x.shape, 0)
    total = x
    hop = 1
    while hop < rows:
        moved = pltpu.roll(total, rows - hop if reverse else hop, 0)
        total = total + jnp.where(row < rows - hop if reverse else row >= hop, moved, 0.0)
        hop *= 2
    edge = row < rows - 1 if reverse else row >= 1
    return jnp.where(edge, pltpu.roll(total, rows - 1 if reverse else 1, 0), 0.0)


def body(f_hbm, cnt_ref, step_ref, tgt_hbm, win_ref, wden_ref, wout_ref,
         res_hbm, dens_ref, gin_ref, gout_ref,
         f_ref, hid_ref, lwt_ref, hbar_ref, p_ref, ps_ref, acc_ref, recv1_ref, recv2_ref, r_ref, prod_ref, tgt_ref,
         t_all, e_all, own_all, ecol_ref, keep_ref, v_ref, wt_ref, dt_ref, dpre_ref,
         gi_ref, go_ref, gi_recv, go_recv,
         f_sem, tgt_sem, res_sem, s_sem, r_sem, ts_sem, tr_sem, os_sem, or_sem, gs_sem, gr_sem):
    smp, ray = f_ref.shape[1], f_ref.shape[2]
    hid, width = win_ref.shape[1], wout_ref.shape[1]
    part_rays = ray // 2
    quarter = part_rays // RING
    slab = gout_ref.shape[0]
    me = lax.axis_index("depth")
    col = lax.axis_index("col")
    y, z = me % RING, me // RING
    first, second = (y, z), (z, y)
    mesh_id = pl.DeviceIdType.MESH

    barrier = pltpu.get_barrier_semaphore()

    def greet_depth(j, _):
        pl.semaphore_signal(barrier, inc=1, device_id={"depth": (me + j) % BRICKS}, device_id_type=mesh_id)
        return 0

    def greet_col(j, _):
        pl.semaphore_signal(barrier, inc=1, device_id={"col": (col + j) % COLS}, device_id_type=mesh_id)
        return 0

    lax.fori_loop(1, BRICKS, greet_depth, 0)
    lax.fori_loop(1, COLS, greet_col, 0)

    def fetch(s, i):
        return pltpu.make_async_copy(
            f_hbm.at[i, pl.ds(s * ray, ray)], f_ref.at[s, i], f_sem.at[s, i])

    def fetch_target(s, part):
        return pltpu.make_async_copy(
            tgt_hbm.at[s, part, first[part], second[part]], tgt_ref.at[s, part], tgt_sem.at[s, part])

    for s in range(STREAMS):
        for i in range(smp):
            fetch(s, i).start()
    for s in range(STREAMS):
        for part in range(2):
            fetch_target(s, part).start()

    def to_depth(src, dst, send, recv, who):
        return pltpu.make_async_remote_copy(
            src_ref=src, dst_ref=dst, send_sem=send, recv_sem=recv,
            device_id={"depth": who}, device_id_type=mesh_id)

    def spread(store, s, send, recv, j):
        return to_depth(store.at[s, me], store.at[s, me], send.at[s, j], recv.at[s, j], (me + j) % BRICKS)

    def spread_start(store, s, send, recv):
        def one(j, _):
            spread(store, s, send, recv, j).start()
            return 0
        lax.fori_loop(1, BRICKS, one, 0)

    def spread_wait(store, s, send, recv):
        def one(j, _):
            spread(store, s, send, recv, j).wait()
            return 0
        lax.fori_loop(1, BRICKS, one, 0)

    def along(axis, j):
        at = (first[axis] + j) % RING
        return at, (z * RING + at if axis == 0 else at * RING + y)

    def hop(stage, s, part, j):
        near, far = first[part], second[part]
        at, who = along(part if stage in (0, 3) else 1 - part, j)
        if stage == 0:
            src, dst = p_ref.at[s, part, at], recv1_ref.at[s, part, j - 1]
        elif stage == 1:
            src, dst = acc_ref.at[s, part, at], recv2_ref.at[s, part, j - 1]
        elif stage == 2:
            src = dst = r_ref.at[s, part, near, far]
        else:
            src = dst = r_ref.at[s, part, near]
        return to_depth(src, dst, s_sem.at[stage, s, part, j], r_sem.at[stage, s, part, j], who)

    def hops(stage, s, part, what):
        for j in (2, 1, 3):
            getattr(hop(stage, s, part, j), what)()

    wden = jnp.broadcast_to(wden_ref[...].astype(F32), (smp, hid))
    sample = lax.broadcasted_iota(jnp.int32, (smp, hid), 0)

    def forward(s):
        sig = jnp.zeros((smp, ray), F32)
        for i in range(smp):
            fetch(s, i).wait()
            pre = mm(f_ref[s, i], win_ref[...], NN)
            h = jnp.maximum(pre, 0.0).astype(BF16)
            hid_ref[s, i] = h
            sig = sig + mm(jnp.where(sample == i, wden, 0.0).astype(BF16), h, NT)
        here = pl.ds(s * ray, ray)
        row = lax.broadcasted_iota(jnp.int32, (smp, ray), 0)
        gate = jnp.where(row < cnt_ref[:, here], jnp.broadcast_to(step_ref[:, here], (smp, ray)), 0.0)
        soft = jnp.maximum(sig, 0.0) + jnp.log1p(jnp.exp(-jnp.abs(sig)))
        tau = soft * gate
        inner = running(tau, False)
        t_all[s, me] = (inner + tau)[smp - 1:smp]
        keep = jnp.exp(-tau)
        light = jnp.exp(-inner)
        lw = light * (1.0 - keep)
        keep_ref[s, 0] = lw
        keep_ref[s, 1] = light * keep
        keep_ref[s, 2] = sig
        keep_ref[s, 3] = gate
        lwt_ref[...] = lw.T

    def weigh(s):
        def tile(t, _):
            at = pl.ds(pl.multiple_of(t * 64, 64), 64)
            w = lwt_ref[at]
            total = jnp.zeros((64, hid), F32)
            for i in range(smp):
                total = total + w[:, i:i + 1] * hid_ref[s, i, at].astype(F32)
            hbar_ref[s, at] = total
            return 0
        lax.fori_loop(0, ray // 64, tile, 0)
        high, low = halves(hbar_ref[s])
        value = mm(high, wout_ref[...], NN) + mm(low, wout_ref[...], NN)
        p_ref[s] = value.reshape(2, RING, quarter, width)

    def reduce_near(s):
        spread_wait(t_all, s, ts_sem, tr_sem)
        before = jnp.zeros((1, ray), F32)
        for b in range(BRICKS):
            e_all[s, b] = jnp.exp(-before)
            before = before + t_all[s, b]
        row = lax.broadcasted_iota(jnp.int32, (smp, ray), 0)
        table = jnp.broadcast_to(e_all[s, me], (smp, ray))
        for part in range(2):
            for j in range(1, RING):
                mine = e_all[s, along(part, RING - j)[1]]
                table = jnp.where(row == part * RING + j, jnp.broadcast_to(mine, (smp, ray)), table)
        ecol_ref[s] = table.T.reshape(2, RING, quarter, smp)
        for part in range(2):
            near = first[part]
            e = ecol_ref[s, part, near]
            hops(0, s, part, "wait_recv")
            total = None
            for j in range(RING):
                got = p_ref[s, part, near] if j == 0 else recv1_ref[s, part, j - 1]
                got = e[:, part * RING + j:part * RING + j + 1] * got
                ps_ref[s, part, j] = got
                total = got if j == 0 else total + got
            acc_ref[s, part] = total.reshape(RING, quarter // RING, width)
            hops(1, s, part, "start")

    def reduce_far(s):
        for part in range(2):
            fetch_target(s, part).wait()
            hops(1, s, part, "wait_recv")
            total = acc_ref[s, part, second[part]] - tgt_ref[s, part]
            for j in range(1, RING):
                total = total + recv2_ref[s, part, j - 1]
            r_ref[s, part, first[part], second[part]] = total
            hops(2, s, part, "start")

    def gather_far(s):
        for part in range(2):
            hops(2, s, part, "wait_recv")
            hops(3, s, part, "start")
        for part in range(2):
            r = r_ref[s, part, first[part]].reshape(quarter, width)
            for j in range(RING):
                prod_ref[pl.ds((part * RING + j) * quarter, quarter)] = ps_ref[s, part, j] * r
        high, low = halves(prod_ref[...])
        ones = jnp.ones((smp, width), BF16)
        own_all[s, me] = (mm(ones, high, NT) + mm(ones, low, NT))[:1]
        spread_start(own_all, s, os_sem, or_sem)

    def put_residual(s):
        return pltpu.make_async_copy(r_ref.at[s], res_hbm.at[s], res_sem.at[s])

    def gather_near(s):
        for part in range(2):
            hops(3, s, part, "wait_recv")
        put_residual(s).start()

    def emissions(s):
        r_high, r_low = halves(r_ref[s].reshape(ray, width))
        v_ref[...] = mm(r_high, wout_ref[...], NT) + mm(r_low, wout_ref[...], NT)
        scaled = hbar_ref[s] * ecol_ref[s].reshape(ray, smp)[:, :1]
        b_high, b_low = halves(scaled)
        out = mm(b_high, r_high, TN) + mm(b_low, r_high, TN) + mm(b_high, r_low, TN)
        out = out.reshape(COLS, slab, width)
        go_ref[...] = out if s == 0 else go_ref[...] + out

        def tile(t, _):
            at = pl.ds(pl.multiple_of(t * 64, 64), 64)
            v = v_ref[at]
            lane = lax.broadcasted_iota(jnp.int32, (64, smp), 1)
            found = jnp.zeros((64, smp), F32)
            for i in range(smp):
                e = jnp.sum(v * hid_ref[s, i, at].astype(F32), 1, keepdims=True)
                found = jnp.where(lane == i, e, found)
            wt_ref[at] = found
            return 0
        lax.fori_loop(0, ray // 64, tile, 0)
        return wt_ref[...].T

    def later_bricks(s):
        spread_wait(own_all, s, os_sem, or_sem)
        lane = lax.broadcasted_iota(jnp.int32, (1, part_rays), 1)
        slot = lane // quarter
        out = []
        for part in range(2):
            whole = jnp.zeros((1, part_rays), F32)
            for near in range(RING):
                total = jnp.zeros((1, part_rays), F32)
                for far in range(RING):
                    source = (near + RING * far, near * RING + far)[part]
                    from_near = (near - slot + RING) % RING
                    brick = (far * RING + from_near, from_near * RING + far)[part]
                    term = own_all[s, source][:, part * part_rays:(part + 1) * part_rays]
                    total = total + jnp.where(brick > me, term, 0.0)
                total = total + pltpu.roll(total, quarter, 1)
                total = total + pltpu.roll(total, 2 * quarter, 1)
                whole = jnp.where(slot == near, total, whole)
            out.append(whole)
        return jnp.concatenate(out, 1)

    def gradients(s, em):
        e = jnp.broadcast_to(e_all[s, me], (smp, ray))
        wgt = keep_ref[s, 0] * e
        later = running(wgt * em, True) + later_bricks(s)
        dens = (keep_ref[s, 1] * e * em - later) * keep_ref[s, 3]
        dens_ref[:, pl.ds(s * ray, ray)] = dens
        dsig = dens / (1.0 + jnp.exp(-keep_ref[s, 2]))
        wt_ref[...] = wgt.T
        dt_ref[...] = dsig.T
        wden_row = wden_ref[...].astype(F32)

        def tile(t, _):
            at = pl.ds(pl.multiple_of(t * 32, 32), 32)
            v = v_ref[at]
            w = wt_ref[at]
            d = dt_ref[at]
            for i in range(smp):
                dh = w[:, i:i + 1] * v + d[:, i:i + 1] * wden_row
                h = hid_ref[s, i, at].astype(F32)
                dpre_ref[i, at] = jnp.where(h > 0.0, dh, 0.0).astype(BF16)
            return 0
        lax.fori_loop(0, ray // 32, tile, 0)
        g_in = mm(f_ref[s].reshape(smp * ray, -1), dpre_ref[...].reshape(smp * ray, hid), TN)
        d_high, d_low = halves(dsig)
        stacked = jnp.concatenate([d_high.astype(F32), d_low.astype(F32)], 0)
        row = lax.broadcasted_iota(jnp.int32, stacked.shape, 0)
        g_den = jnp.zeros((2 * smp, hid), F32)
        for i in range(smp):
            g_den = g_den + mm(jnp.where(row % smp == i, stacked, 0.0).astype(BF16), hid_ref[s, i], NN)
        g_den = g_den[:smp] + g_den[smp:]
        for c in range(COLS):
            mine = g_in[c * slab:(c + 1) * slab]
            if s == 0:
                gi_ref[c, :slab] = mine
                gi_ref[c, slab:] = g_den
            else:
                gi_ref[c, :slab] = gi_ref[c, :slab] + mine
                gi_ref[c, slab:] = gi_ref[c, slab:] + g_den

    def share(kind, j):
        src, dst = ((gi_ref, gi_recv), (go_ref, go_recv))[kind]
        to = (col + j) % COLS
        return pltpu.make_async_remote_copy(
            src_ref=src.at[to], dst_ref=dst.at[j - 1], send_sem=gs_sem.at[kind, j],
            recv_sem=gr_sem.at[kind, j], device_id={"col": to}, device_id_type=mesh_id)

    def share_all(kind, wait):
        def one(j, _):
            if wait:
                share(kind, j).wait()
            else:
                share(kind, j).start()
            return 0
        lax.fori_loop(1, COLS, one, 0)

    for s in range(STREAMS):
        forward(s)
        if s == 0:
            pl.semaphore_wait(barrier, BRICKS - 1 + COLS - 1)
        spread_start(t_all, s, ts_sem, tr_sem)
        weigh(s)
        for part in range(2):
            hops(0, s, part, "start")
    for step, s in ORDER:
        (reduce_near, reduce_far, gather_far)[step](s)
    for s in range(STREAMS):
        gather_near(s)
        em = emissions(s)
        if s == STREAMS - 1:
            share_all(1, False)
        gradients(s, em)
    share_all(0, False)
    share_all(1, True)
    total = go_ref[col]
    for j in range(COLS - 1):
        total = total + go_recv[j]
    gout_ref[...] = total
    for s in range(STREAMS):
        for part in range(2):
            for stage in range(4):
                hops(stage, s, part, "wait_send")
        put_residual(s).wait()
    share_all(0, True)
    total = gi_ref[col]
    for j in range(COLS - 1):
        total = total + gi_recv[j]
    gin_ref[...] = total


def finish(res_in, dens_in, gin_in, gout_in, res_hbm, dens_ref, gin_ref, gden_ref, gout_ref, held, in_sem, out_sem):
    parts = res_in.shape[0]

    def take(i):
        return pltpu.make_async_copy(res_in.at[i], held.at[i], in_sem.at[i])

    def put(i):
        return pltpu.make_async_copy(held.at[i], res_hbm.at[i], out_sem.at[i])

    for i in range(parts):
        take(i).start()
    dens_ref[...] = dens_in[...]
    gout_ref[...] = gout_in[...]
    slab = gin_ref.shape[0]
    gin_ref[...] = gin_in[:slab]
    den = jnp.sum(gin_in[slab:], 0, keepdims=True)
    col = lax.axis_index("col")
    mine = den[:, :slab]
    for c in range(1, COLS):
        mine = jnp.where(col == c, den[:, c * slab:(c + 1) * slab], mine)
    gden_ref[...] = mine
    for i in range(parts):
        take(i).wait()
        put(i).start()
    for i in range(parts):
        put(i).wait()


def per_device(features, counts, steps, target, w_in, w_density, w_out):
    _, smp, nray, din = features.shape
    hid, width = w_out.shape[1:]
    ray = nray // STREAMS
    quarter = ray // 2 // RING
    piece = quarter // RING
    slab = din // COLS
    vmem = pl.BlockSpec(memory_space=pltpu.VMEM)
    hbm = pl.BlockSpec(memory_space=pl.ANY)
    dma = pltpu.SemaphoreType.DMA
    split = (STREAMS, 2, RING, RING, piece, width)
    scratch = [
        pltpu.VMEM((STREAMS, smp, ray, din), BF16),
        pltpu.VMEM((STREAMS, smp, ray, hid), BF16),
        pltpu.VMEM((ray, smp), F32),
        pltpu.VMEM((STREAMS, ray, hid), F32),
        pltpu.VMEM((STREAMS, 2, RING, quarter, width), F32),
        pltpu.VMEM((STREAMS, 2, RING, quarter, width), F32),
        pltpu.VMEM((STREAMS, 2, RING, piece, width), F32),
        pltpu.VMEM((STREAMS, 2, RING - 1, quarter, width), F32),
        pltpu.VMEM((STREAMS, 2, RING - 1, piece, width), F32),
        pltpu.VMEM(split, F32),
        pltpu.VMEM((ray, width), F32),
        pltpu.VMEM((STREAMS, 2, piece, width), F32),
        pltpu.VMEM((STREAMS, BRICKS, 1, ray), F32),
        pltpu.VMEM((STREAMS, BRICKS, 1, ray), F32),
        pltpu.VMEM((STREAMS, BRICKS, 1, ray), F32),
        pltpu.VMEM((STREAMS, 2, RING, quarter, smp), F32),
        pltpu.VMEM((STREAMS, 4, smp, ray), F32),
        pltpu.VMEM((ray, hid), F32),
        pltpu.VMEM((ray, smp), F32),
        pltpu.VMEM((ray, smp), F32),
        pltpu.VMEM((smp, ray, hid), BF16),
        pltpu.VMEM((COLS, slab + smp, hid), F32),
        pltpu.VMEM((COLS, slab, width), F32),
        pltpu.VMEM((COLS - 1, slab + smp, hid), F32),
        pltpu.VMEM((COLS - 1, slab, width), F32),
        dma((STREAMS, smp)), dma((STREAMS, 2)), dma((STREAMS,)),
        dma((4, STREAMS, 2, RING)), dma((4, STREAMS, 2, RING)),
        dma((STREAMS, BRICKS)), dma((STREAMS, BRICKS)), dma((STREAMS, BRICKS)), dma((STREAMS, BRICKS)),
        dma((2, COLS)), dma((2, COLS)),
    ]
    residual, dens, g_in, g_out = pl.pallas_call(
        body,
        out_shape=(
            jax.ShapeDtypeStruct(split, F32),
            jax.ShapeDtypeStruct((smp, nray), F32),
            jax.ShapeDtypeStruct((slab + smp, hid), F32),
            jax.ShapeDtypeStruct((slab, width), F32),
        ),
        in_specs=[hbm, vmem, vmem, hbm, vmem, vmem, vmem],
        out_specs=(hbm, vmem, vmem, vmem),
        scratch_shapes=scratch,
        compiler_params=pltpu.CompilerParams(
            collective_id=0, has_side_effects=True, vmem_limit_bytes=60 * 1024 * 1024),
        name="brick_step",
    )(features[0], counts, steps, target.reshape(split), w_in[0], w_density, w_out[0])
    residual, dens, g_in, g_den, g_out = pl.pallas_call(
        finish,
        out_shape=(
            jax.ShapeDtypeStruct((STREAMS, ray, width), F32),
            jax.ShapeDtypeStruct((smp, nray), F32),
            jax.ShapeDtypeStruct((slab, hid), F32),
            jax.ShapeDtypeStruct((1, slab), F32),
            jax.ShapeDtypeStruct((slab, width), F32),
        ),
        in_specs=[hbm, vmem, vmem, vmem],
        out_specs=(hbm, vmem, vmem, vmem, vmem),
        scratch_shapes=[pltpu.VMEM((STREAMS, ray, width), F32), dma((STREAMS,)), dma((STREAMS,))],
        name="brick_finish",
    )(residual.reshape(STREAMS, ray, width), dens, g_in, g_out)
    return residual.reshape(nray, width), dens[None], g_in[None], g_den, g_out[None]


def solution(mesh):
    return jax.shard_map(
        per_device,
        mesh=mesh,
        in_specs=(
            P("depth", None, "col", None),
            P("depth", "col"),
            P("depth", "col"),
            P("col", None),
            P("depth", None, None),
            P("depth", None),
            P("depth", None, None),
        ),
        out_specs=(
            P("col", None),
            P("depth", None, "col"),
            P("depth", "col", None),
            P("depth", "col"),
            P("depth", "col", None),
        ),
        check_vma=False,
    )
```

```python
import functools

import jax
import jax.numpy as jnp
from jax import lax
from jax.experimental import pallas as pl
from jax.experimental.pallas import tpu as pltpu
from jax.sharding import PartitionSpec as P

STREAMS = 4
RING = 4
BRICKS = 16
COLS = 8
ORDER = ((0, 0), (0, 1), (0, 2), (1, 0), (0, 3), (1, 1), (1, 2), (2, 0), (1, 3), (2, 1), (2, 2), (2, 3))
F32 = jnp.float32
BF16 = jnp.bfloat16
NT = (((1,), (1,)), ((), ()))
TN = (((0,), (0,)), ((), ()))
NN = (((1,), (0,)), ((), ()))


def mm(a, b, dims):
    return lax.dot_general(a, b, dims, preferred_element_type=F32)


def halves(x):
    high = x.astype(BF16)
    return high, (x - high.astype(F32)).astype(BF16)


def running(x, reverse):
    rows = x.shape[0]
    row = lax.broadcasted_iota(jnp.int32, x.shape, 0)
    total = x
    hop = 1
    while hop < rows:
        moved = pltpu.roll(total, rows - hop if reverse else hop, 0)
        total = total + jnp.where(row < rows - hop if reverse else row >= hop, moved, 0.0)
        hop *= 2
    edge = row < rows - 1 if reverse else row >= 1
    return jnp.where(edge, pltpu.roll(total, rows - 1 if reverse else 1, 0), 0.0)


def body(f_hbm, cnt_hbm, step_hbm, tgt_hbm, win_hbm, wden_hbm, wout_hbm,
         res_hbm, dens_hbm, gin_hbm, gout_hbm,
         cnt_ref, step_ref, win_ref, wden_ref, wout_ref, dens_ref, gin_ref, gout_ref, f_ref, hid_ref, lwt_ref, hbar_ref, p_ref, ps_ref, acc_ref, recv1_ref, recv2_ref, r_ref, prod_ref, tgt_ref,
         t_all, e_all, own_all, ecol_ref, keep_ref, v_ref, wt_ref, dt_ref, dpre_ref,
         gi_ref, go_ref, gi_recv, go_pair, go_sum, go_recv,
         in_sem, f_sem, tgt_sem, out_sem, s_sem, r_sem, ts_sem, tr_sem, os_sem, or_sem, gs_sem, gr_sem):
    smp, ray = f_ref.shape[1], f_ref.shape[2]
    hid, width = win_ref.shape[1], wout_ref.shape[1]
    part_rays = ray // 2
    quarter = part_rays // RING
    slab = gout_ref.shape[0]
    me = lax.axis_index("depth")
    col = lax.axis_index("col")
    y, z = me % RING, me // RING
    first, second = (y, z), (z, y)
    mesh_id = pl.DeviceIdType.MESH

    barrier = pltpu.get_barrier_semaphore()

    def greet_depth(j, _):
        pl.semaphore_signal(barrier, inc=1, device_id={"depth": (me + j) % BRICKS}, device_id_type=mesh_id)
        return 0

    def greet_col(j, _):
        pl.semaphore_signal(barrier, inc=1, device_id={"col": (col + j) % COLS}, device_id_type=mesh_id)
        return 0

    lax.fori_loop(1, BRICKS, greet_depth, 0)
    lax.fori_loop(1, COLS, greet_col, 0)

    weights = [
        pltpu.make_async_copy(src, dst, in_sem.at[i])
        for i, (src, dst) in enumerate((
            (win_hbm, win_ref), (wden_hbm, wden_ref), (cnt_hbm, cnt_ref), (step_hbm, step_ref),
            (wout_hbm, wout_ref)))
    ]

    def fetch(s):
        return pltpu.make_async_copy(f_hbm.at[:, pl.ds(s * ray, ray)], f_ref.at[s], f_sem.at[s])

    def fetch_target(s, part):
        return pltpu.make_async_copy(
            tgt_hbm.at[s, part, first[part], second[part]], tgt_ref.at[s, part], tgt_sem.at[0])

    fetch(0).start()
    for copy in weights:
        copy.start()
    for s in range(1, STREAMS):
        fetch(s).start()
    for s in range(STREAMS):
        for part in range(2):
            fetch_target(s, part).start()

    def arrived(ref, sem):
        pltpu.make_async_copy(ref, ref, sem).wait()

    def to_depth(src, dst, send, recv, who):
        return pltpu.make_async_remote_copy(
            src_ref=src, dst_ref=dst, send_sem=send, recv_sem=recv,
            device_id={"depth": who}, device_id_type=mesh_id)

    def spread_start(row, send, recv):
        def one(j, _):
            to_depth(row, row, send, recv, (me + j) % BRICKS).start()
            return 0
        lax.fori_loop(1, BRICKS, one, 0)

    def along(axis, j):
        at = (first[axis] + j) % RING
        return at, (z * RING + at if axis == 0 else at * RING + y)

    def hop(stage, s, part, j):
        near, far = first[part], second[part]
        at, who = along(part if stage in (0, 3) else 1 - part, j)
        if stage == 0:
            src, dst = p_ref.at[s, part, at], recv1_ref.at[s, part, j - 1]
        elif stage == 1:
            src, dst = acc_ref.at[s, part, at], recv2_ref.at[s, part, j - 1]
        elif stage == 2:
            src = dst = r_ref.at[s, part, near, far]
        else:
            src = dst = r_ref.at[s, part, near]
        return to_depth(src, dst, s_sem.at[stage], r_sem.at[stage, s, part], who)

    def send(stage, s, part):
        for j in (2, 1, 3):
            hop(stage, s, part, j).start()

    def got_all(stage, s, part):
        ref = recv1_ref if stage in (0, 3) else recv2_ref
        arrived(ref.at[s, part], r_sem.at[stage, s, part])

    sample = lax.broadcasted_iota(jnp.int32, (smp, hid), 0)
    pair = ray * 2

    def forward(s):
        fetch(s).wait()
        if s == 0:
            for copy in weights[:4]:
                copy.wait()
        wden = jnp.broadcast_to(wden_ref[...].astype(F32), (smp, hid))
        sig = jnp.zeros((smp, ray), F32)
        for i in range(smp):
            pre = mm(f_ref[s, i], win_ref[...], NN)
            h = jnp.maximum(pre, 0.0).astype(BF16)
            hid_ref[s, i] = h
            sig = sig + mm(jnp.where(sample == i, wden, 0.0).astype(BF16), h, NT)
        here = pl.ds(s * ray, ray)
        row = lax.broadcasted_iota(jnp.int32, (smp, ray), 0)
        gate = jnp.where(row < cnt_ref[:, here], jnp.broadcast_to(step_ref[:, here], (smp, ray)), 0.0)
        soft = jnp.maximum(sig, 0.0) + jnp.log1p(jnp.exp(-jnp.abs(sig)))
        tau = soft * gate
        inner = running(tau, False)
        t_all[s // 2, me, :, s % 2 * ray:(s % 2 + 1) * ray] = (inner + tau)[smp - 1:smp]
        keep = jnp.exp(-tau)
        light = jnp.exp(-inner)
        lw = light * (1.0 - keep)
        keep_ref[s, 0] = lw
        keep_ref[s, 1] = light * keep
        keep_ref[s, 2] = sig
        keep_ref[s, 3] = gate
        lwt_ref[...] = lw.T

    def weigh(s):
        def tile(t, _):
            at = pl.ds(pl.multiple_of(t * 64, 64), 64)
            w = lwt_ref[at]
            total = jnp.zeros((64, hid), F32)
            for i in range(smp):
                total = total + w[:, i:i + 1] * hid_ref[s, i, at].astype(F32)
            hbar_ref[s, at] = total
            return 0
        lax.fori_loop(0, ray // 64, tile, 0)
        if s == 0:
            weights[4].wait()
        high, low = halves(hbar_ref[s])
        value = mm(high, wout_ref[...], NN) + mm(low, wout_ref[...], NN)
        p_ref[s] = value.reshape(2, RING, quarter, width)

    def reduce_near(s):
        if s % 2 == 0:
            arrived(t_all.at[s // 2, pl.ds(0, BRICKS - 1)], tr_sem.at[s // 2])
            before = jnp.zeros((1, pair), F32)
            for b in range(BRICKS):
                light = jnp.exp(-before)
                e_all[s, b] = light[:, :ray]
                e_all[s + 1, b] = light[:, ray:]
                before = before + t_all[s // 2, b]
        row = lax.broadcasted_iota(jnp.int32, (smp, ray), 0)
        table = jnp.broadcast_to(e_all[s, me], (smp, ray))
        for part in range(2):
            for j in range(1, RING):
                mine = e_all[s, along(part, RING - j)[1]]
                table = jnp.where(row == part * RING + j, jnp.broadcast_to(mine, (smp, ray)), table)
        ecol_ref[s] = table.T.reshape(2, RING, quarter, smp)
        for part in range(2):
            near = first[part]
            e = ecol_ref[s, part, near]
            got_all(0, s, part)
            total = None
            for j in range(RING):
                got = p_ref[s, part, near] if j == 0 else recv1_ref[s, part, j - 1]
                got = e[:, part * RING + j:part * RING + j + 1] * got
                ps_ref[s, part, j] = got
                total = got if j == 0 else total + got
            acc_ref[s, part] = total.reshape(RING, quarter // RING, width)
            send(1, s, part)

    def reduce_far(s):
        if s == 0:
            arrived(tgt_ref, tgt_sem.at[0])
        for part in range(2):
            got_all(1, s, part)
            total = acc_ref[s, part, second[part]] - tgt_ref[s, part]
            for j in range(1, RING):
                total = total + recv2_ref[s, part, j - 1]
            r_ref[s, part, first[part], second[part]] = total
            send(2, s, part)

    def gather_far(s):
        for part in range(2):
            got_all(2, s, part)
            send(3, s, part)
        for part in range(2):
            r = r_ref[s, part, first[part]].reshape(quarter, width)
            for j in range(RING):
                prod_ref[pl.ds((part * RING + j) * quarter, quarter)] = ps_ref[s, part, j] * r
        high, low = halves(prod_ref[...])
        ones = jnp.ones((smp, width), BF16)
        own_all[s, me] = (mm(ones, high, NT) + mm(ones, low, NT))[:1]
        spread_start(own_all.at[s, me], os_sem.at[0], or_sem.at[s])

    def put_residual(s):
        return pltpu.make_async_copy(r_ref.at[s], res_hbm.at[s], out_sem.at[0])

    def gather_near(s):
        for part in range(2):
            got_all(3, s, part)
        put_residual(s).start()

    def emissions(s):
        r_high, r_low = halves(r_ref[s].reshape(ray, width))
        v_ref[...] = mm(r_high, wout_ref[...], NT) + mm(r_low, wout_ref[...], NT)
        scaled = hbar_ref[s] * ecol_ref[s].reshape(ray, smp)[:, :1]
        b_high, b_low = halves(scaled)
        out = mm(b_high, r_high, TN) + mm(b_low, r_high, TN) + mm(b_high, r_low, TN)
        for c in range(COLS):
            mine = out[c * slab:(c + 1) * slab]
            go_ref[c % 2, c // 2] = mine if s == 0 else go_ref[c % 2, c // 2] + mine
        if s == STREAMS - 1:
            pair_copy.start()

        def tile(t, _):
            at = pl.ds(pl.multiple_of(t * 64, 64), 64)
            v = v_ref[at]
            lane = lax.broadcasted_iota(jnp.int32, (64, smp), 1)
            found = jnp.zeros((64, smp), F32)
            for i in range(smp):
                e = jnp.sum(v * hid_ref[s, i, at].astype(F32), 1, keepdims=True)
                found = jnp.where(lane == i, e, found)
            wt_ref[at] = found
            return 0
        lax.fori_loop(0, ray // 64, tile, 0)
        return wt_ref[...].T

    def later_bricks(s):
        arrived(own_all.at[s, pl.ds(0, BRICKS - 1)], or_sem.at[s])
        lane = lax.broadcasted_iota(jnp.int32, (1, part_rays), 1)
        slot = lane // quarter
        out = []
        for part in range(2):
            whole = jnp.zeros((1, part_rays), F32)
            for near in range(RING):
                total = jnp.zeros((1, part_rays), F32)
                for far in range(RING):
                    source = (near + RING * far, near * RING + far)[part]
                    from_near = (near - slot + RING) % RING
                    brick = (far * RING + from_near, from_near * RING + far)[part]
                    term = own_all[s, source][:, part * part_rays:(part + 1) * part_rays]
                    total = total + jnp.where(brick > me, term, 0.0)
                total = total + pltpu.roll(total, quarter, 1)
                total = total + pltpu.roll(total, 2 * quarter, 1)
                whole = jnp.where(slot == near, total, whole)
            out.append(whole)
        return jnp.concatenate(out, 1)

    def gradients(s, em):
        e = jnp.broadcast_to(e_all[s, me], (smp, ray))
        wgt = keep_ref[s, 0] * e
        later = running(wgt * em, True) + later_bricks(s)
        dens = (keep_ref[s, 1] * e * em - later) * keep_ref[s, 3]
        dens_ref[:, pl.ds(s * ray, ray)] = dens
        dsig = dens / (1.0 + jnp.exp(-keep_ref[s, 2]))
        wt_ref[...] = wgt.T
        dt_ref[...] = dsig.T
        wden_row = wden_ref[...].astype(F32)

        def tile(t, _):
            at = pl.ds(pl.multiple_of(t * 32, 32), 32)
            v = v_ref[at]
            w = wt_ref[at]
            d = dt_ref[at]
            for i in range(smp):
                dh = w[:, i:i + 1] * v + d[:, i:i + 1] * wden_row
                h = hid_ref[s, i, at].astype(F32)
                dpre_ref[i, at] = jnp.where(h > 0.0, dh, 0.0).astype(BF16)
            return 0
        lax.fori_loop(0, ray // 32, tile, 0)
        if s == STREAMS - 1:
            share_out()
        g_in = mm(f_ref[s].reshape(smp * ray, -1), dpre_ref[...].reshape(smp * ray, hid), TN)
        d_high, d_low = halves(dsig)
        stacked = jnp.concatenate([d_high.astype(F32), d_low.astype(F32)], 0)
        row = lax.broadcasted_iota(jnp.int32, stacked.shape, 0)
        g_den = jnp.zeros((2 * smp, hid), F32)
        for i in range(smp):
            g_den = g_den + mm(jnp.where(row % smp == i, stacked, 0.0).astype(BF16), hid_ref[s, i], NN)
        g_den = g_den[:smp] + g_den[smp:]
        for c in range(COLS):
            mine = g_in[c * slab:(c + 1) * slab]
            if s == 0:
                gi_ref[c, :slab] = mine
                gi_ref[c, slab:] = g_den
            else:
                gi_ref[c, :slab] = gi_ref[c, :slab] + mine
                gi_ref[c, slab:] = gi_ref[c, slab:] + g_den

    x, core = col // 2, col % 2

    def to_col(src, dst, send, recv, who):
        return pltpu.make_async_remote_copy(
            src_ref=src, dst_ref=dst, send_sem=send, recv_sem=recv,
            device_id={"col": who}, device_id_type=mesh_id)

    pair_copy = to_col(go_ref.at[1 - core], go_pair, gs_sem.at[0], gr_sem.at[0], x * 2 + 1 - core)

    def share_out():
        pair_copy.wait_recv()
        go_sum[...] = go_ref[core] + go_pair[...]
        for j in (2, 1, 3):
            to = (x + j) % RING
            to_col(go_sum.at[to], go_recv.at[j - 1], gs_sem.at[1], gr_sem.at[1], to * 2 + core).start()

    def share_in(j, _):
        to = (col + j) % COLS
        to_col(gi_ref.at[to], gi_recv.at[j - 1], gs_sem.at[2], gr_sem.at[2], to).start()
        return 0

    for s in range(STREAMS):
        forward(s)
        if s == 0:
            pl.semaphore_wait(barrier, BRICKS - 1 + COLS - 1)
        if s % 2 == 1:
            spread_start(t_all.at[s // 2, me], ts_sem.at[0], tr_sem.at[s // 2])
        weigh(s)
        for part in range(2):
            send(0, s, part)
    for step, s in ORDER:
        (reduce_near, reduce_far, gather_far)[step](s)
    for s in range(STREAMS):
        gather_near(s)
        em = emissions(s)
        gradients(s, em)
    lax.fori_loop(1, COLS, share_in, 0)
    dens_copy = pltpu.make_async_copy(dens_ref, dens_hbm, out_sem.at[1])
    dens_copy.start()
    arrived(go_recv, gr_sem.at[1])
    total = go_sum[x]
    for j in range(RING - 1):
        total = total + go_recv[j]
    gout_ref[...] = total
    gout_copy = pltpu.make_async_copy(gout_ref, gout_hbm, out_sem.at[2])
    gout_copy.start()
    arrived(recv1_ref, s_sem.at[0])
    arrived(recv2_ref, s_sem.at[1])
    arrived(recv2_ref, s_sem.at[2])
    arrived(recv1_ref, s_sem.at[3])
    arrived(t_all.at[:, pl.ds(0, BRICKS - 1)], ts_sem.at[0])
    arrived(own_all.at[:, pl.ds(0, BRICKS - 1)], os_sem.at[0])
    pair_copy.wait_send()
    arrived(go_recv, gs_sem.at[1])
    arrived(r_ref, out_sem.at[0])
    dens_copy.wait()
    arrived(gi_recv, gr_sem.at[2])
    total = gi_ref[col]
    for j in range(COLS - 1):
        total = total + gi_recv[j]
    gin_ref[...] = total
    gin_copy = pltpu.make_async_copy(gin_ref, gin_hbm, out_sem.at[3])
    gin_copy.start()
    arrived(gi_recv, gs_sem.at[2])
    gout_copy.wait()
    gin_copy.wait()


def finish(res_in, dens_in, gin_in, gout_in, res_hbm, dens_hbm, gin_hbm, gden_hbm, gout_hbm,
           held, dens_ref, gin_ref, gout_ref, gden_ref, in_sem, out_sem):
    parts = res_in.shape[0]
    slab = gin_hbm.shape[0]
    take = [pltpu.make_async_copy(src, dst, in_sem.at[i]) for i, (src, dst) in enumerate(
        [(gin_in, gin_ref), (dens_in, dens_ref), (gout_in, gout_ref)]
        + [(res_in.at[i], held.at[i]) for i in range(parts)])]
    put = [pltpu.make_async_copy(src, dst, out_sem.at[i]) for i, (src, dst) in enumerate(
        [(gin_ref.at[pl.ds(0, slab)], gin_hbm), (dens_ref, dens_hbm), (gout_ref, gout_hbm)]
        + [(held.at[i], res_hbm.at[i]) for i in range(parts)] + [(gden_ref, gden_hbm)])]
    for copy in take:
        copy.start()
    for got, gone in zip(take, put):
        got.wait()
        gone.start()
    den = jnp.sum(gin_ref[slab:], 0, keepdims=True)
    col = lax.axis_index("col")
    mine = den[:, :slab]
    for c in range(1, COLS):
        mine = jnp.where(col == c, den[:, c * slab:(c + 1) * slab], mine)
    gden_ref[...] = mine
    put[-1].start()
    for copy in put:
        copy.wait()


def per_device(features, counts, steps, target, w_in, w_density, w_out):
    _, smp, nray, din = features.shape
    hid, width = w_out.shape[1:]
    ray = nray // STREAMS
    quarter = ray // 2 // RING
    piece = quarter // RING
    slab = din // COLS
    hbm = pl.BlockSpec(memory_space=pl.ANY)
    dma = pltpu.SemaphoreType.DMA
    split = (STREAMS, 2, RING, RING, piece, width)
    scratch = [
        pltpu.VMEM((1, nray), jnp.int32),
        pltpu.VMEM((1, nray), F32),
        pltpu.VMEM((din, hid), BF16),
        pltpu.VMEM((1, hid), BF16),
        pltpu.VMEM((hid, width), BF16),
        pltpu.VMEM((smp, nray), F32),
        pltpu.VMEM((slab + smp, hid), F32),
        pltpu.VMEM((slab, width), F32),
        pltpu.VMEM((STREAMS, smp, ray, din), BF16),
        pltpu.VMEM((STREAMS, smp, ray, hid), BF16),
        pltpu.VMEM((ray, smp), F32),
        pltpu.VMEM((STREAMS, ray, hid), F32),
        pltpu.VMEM((STREAMS, 2, RING, quarter, width), F32),
        pltpu.VMEM((STREAMS, 2, RING, quarter, width), F32),
        pltpu.VMEM((STREAMS, 2, RING, piece, width), F32),
        pltpu.VMEM((STREAMS, 2, RING - 1, quarter, width), F32),
        pltpu.VMEM((STREAMS, 2, RING - 1, piece, width), F32),
        pltpu.VMEM(split, F32),
        pltpu.VMEM((ray, width), F32),
        pltpu.VMEM((STREAMS, 2, piece, width), F32),
        pltpu.VMEM((STREAMS // 2, BRICKS, 1, 2 * ray), F32),
        pltpu.VMEM((STREAMS, BRICKS, 1, ray), F32),
        pltpu.VMEM((STREAMS, BRICKS, 1, ray), F32),
        pltpu.VMEM((STREAMS, 2, RING, quarter, smp), F32),
        pltpu.VMEM((STREAMS, 4, smp, ray), F32),
        pltpu.VMEM((ray, hid), F32),
        pltpu.VMEM((ray, smp), F32),
        pltpu.VMEM((ray, smp), F32),
        pltpu.VMEM((smp, ray, hid), BF16),
        pltpu.VMEM((COLS, slab + smp, hid), F32),
        pltpu.VMEM((2, RING, slab, width), F32),
        pltpu.VMEM((COLS - 1, slab + smp, hid), F32),
        pltpu.VMEM((RING, slab, width), F32),
        pltpu.VMEM((RING, slab, width), F32),
        pltpu.VMEM((RING - 1, slab, width), F32),
        dma((5,)), dma((STREAMS,)), dma((1,)), dma((4,)),
        dma((4,)), dma((4, STREAMS, 2)),
        dma((1,)), dma((STREAMS // 2,)), dma((1,)), dma((STREAMS,)),
        dma((3,)), dma((3,)),
    ]
    residual, dens, g_in, g_out = pl.pallas_call(
        body,
        out_shape=(
            jax.ShapeDtypeStruct(split, F32),
            jax.ShapeDtypeStruct((smp, nray), F32),
            jax.ShapeDtypeStruct((slab + smp, hid), F32),
            jax.ShapeDtypeStruct((slab, width), F32),
        ),
        in_specs=[hbm] * 7,
        out_specs=(hbm,) * 4,
        scratch_shapes=scratch,
        compiler_params=pltpu.CompilerParams(
            collective_id=0, has_side_effects=True, vmem_limit_bytes=60 * 1024 * 1024),
        name="brick_step",
    )(features[0], counts, steps, target.reshape(split), w_in[0], w_density, w_out[0])
    residual, dens, g_in, g_den, g_out = pl.pallas_call(
        finish,
        out_shape=(
            jax.ShapeDtypeStruct((STREAMS, ray, width), F32),
            jax.ShapeDtypeStruct((smp, nray), F32),
            jax.ShapeDtypeStruct((slab, hid), F32),
            jax.ShapeDtypeStruct((1, slab), F32),
            jax.ShapeDtypeStruct((slab, width), F32),
        ),
        in_specs=[hbm] * 4,
        out_specs=(hbm,) * 5,
        scratch_shapes=[
            pltpu.VMEM((STREAMS, ray, width), F32),
            pltpu.VMEM((smp, nray), F32),
            pltpu.VMEM((slab + smp, hid), F32),
            pltpu.VMEM((slab, width), F32),
            pltpu.VMEM((1, slab), F32),
            dma((3 + STREAMS,)), dma((4 + STREAMS,)),
        ],
        name="brick_finish",
    )(residual.reshape(STREAMS, ray, width), dens, g_in, g_out)
    return residual.reshape(nray, width), dens[None], g_in[None], g_den, g_out[None]


def solution(mesh):
    return jax.shard_map(
        per_device,
        mesh=mesh,
        in_specs=(
            P("depth", None, "col", None),
            P("depth", "col"),
            P("depth", "col"),
            P("col", None),
            P("depth", None, None),
            P("depth", None),
            P("depth", None, None),
        ),
        out_specs=(
            P("col", None),
            P("depth", None, "col"),
            P("depth", "col", None),
            P("depth", "col"),
            P("depth", "col", None),
        ),
        check_vma=False,
    )
```

```python
import functools

import jax
import jax.numpy as jnp
from jax import lax
from jax.experimental import pallas as pl
from jax.experimental.pallas import tpu as pltpu
from jax.sharding import PartitionSpec as P

STREAMS = 4
RING = 4
BRICKS = 16
COLS = 8
PARTS = 4
LANES = 128
ORDER = ((0, 0), (0, 1), (1, 0), (0, 2), (1, 1), (0, 3), (1, 2), (2, 0), (1, 3), (2, 1), (2, 2), (3, 0),
         (2, 3), (3, 1), (4, 0), (3, 2), (4, 1), (3, 3), (4, 2), (5, 0), (4, 3), (6, 0), (5, 1), (7, 0),
         (5, 2), (6, 1), (7, 1), (5, 3), (6, 2), (7, 2), (6, 3), (7, 3))
F32 = jnp.float32
BF16 = jnp.bfloat16
NT = (((1,), (1,)), ((), ()))
TN = (((0,), (0,)), ((), ()))
NN = (((1,), (0,)), ((), ()))


def mm(a, b, dims):
    return lax.dot_general(a, b, dims, preferred_element_type=F32)


def halves(x):
    high = x.astype(BF16)
    return high, (x - high.astype(F32)).astype(BF16)


def place(part, block):
    at = 0
    for turn in range(4):
        at = at * 2 + (block // 2 ** ((part + turn) % 4)) % 2
    return at


def block_at(part, at):
    block = 0
    for turn in range(4):
        block = block + (at // 2 ** (3 - turn)) % 2 * 2 ** ((part + turn) % 4)
    return block


def running(x, reverse):
    rows = x.shape[0]
    row = lax.broadcasted_iota(jnp.int32, x.shape, 0)
    total = x
    hop = 1
    while hop < rows:
        moved = pltpu.roll(total, rows - hop if reverse else hop, 0)
        total = total + jnp.where(row < rows - hop if reverse else row >= hop, moved, 0.0)
        hop *= 2
    edge = row < rows - 1 if reverse else row >= 1
    return jnp.where(edge, pltpu.roll(total, rows - 1 if reverse else 1, 0), 0.0)


def body(f_hbm, cnt_hbm, step_hbm, tgt_hbm, win_hbm, wden_hbm, wout_hbm,
         res_hbm, dens_hbm, gin_hbm, gout_hbm,
         cnt_ref, step_ref, win_ref, wden_ref, wout_ref, dens_ref, gin_ref, gout_ref, f_ref, hid_ref, lwt_ref, hbar_ref, p_ref, acc_ref, recv_ref, r_ref, res_ref, emt_ref, tgt_ref,
         t_all, e_all, own_all, ecol_ref, keep_ref, v_ref, wt_ref, dt_ref, dpre_ref,
         gi_ref, go_ref, gi_recv, go_pair, go_sum, go_recv,
         in_sem, f_sem, tgt_sem, out_sem, s_sem, r_sem, ts_sem, tr_sem, os_sem, or_sem, gs_sem, gr_sem):
    smp, ray = f_ref.shape[1], f_ref.shape[2]
    hid, width = win_ref.shape[1], wout_ref.shape[1]
    rows = ray // BRICKS
    slab = gout_ref.shape[0]
    me = lax.axis_index("depth")
    col = lax.axis_index("col")
    y, z = me % RING, me // RING
    bits = ((y // 2 + y % 2) % 2, y // 2, (z // 2 + z % 2) % 2, z // 2)
    home = bits[0] + 2 * bits[1] + 4 * bits[2] + 8 * bits[3]

    def moved(at, low, high):
        if low and high:
            return (at + 2) % RING
        return RING - 1 - at if high else at + 1 - 2 * (at % 2) if low else at

    def other(*dims):
        return (moved(z, 2 in dims, 3 in dims) * RING
                + moved(y, 0 in dims, 1 in dims))

    mesh_id = pl.DeviceIdType.MESH

    barrier = pltpu.get_barrier_semaphore()

    def greet_depth(j, _):
        pl.semaphore_signal(barrier, inc=1, device_id={"depth": (me + j) % BRICKS}, device_id_type=mesh_id)
        return 0

    def greet_col(j, _):
        pl.semaphore_signal(barrier, inc=1, device_id={"col": (col + j) % COLS}, device_id_type=mesh_id)
        return 0

    lax.fori_loop(1, BRICKS, greet_depth, 0)
    lax.fori_loop(1, COLS, greet_col, 0)

    weights = [
        pltpu.make_async_copy(src, dst, in_sem.at[i])
        for i, (src, dst) in enumerate((
            (win_hbm, win_ref), (wden_hbm, wden_ref), (cnt_hbm, cnt_ref), (step_hbm, step_ref),
            (wout_hbm, wout_ref)))
    ]

    def fetch(s):
        return pltpu.make_async_copy(f_hbm.at[:, pl.ds(s * ray, ray)], f_ref.at[s], f_sem.at[s])

    def fetch_target(s):
        return pltpu.make_async_copy(tgt_hbm.at[s, home], tgt_ref.at[s], tgt_sem.at[0])

    fetch(0).start()
    for copy in weights:
        copy.start()
    for s in range(1, STREAMS):
        fetch(s).start()
    for s in range(STREAMS):
        fetch_target(s).start()

    def arrived(ref, sem):
        pltpu.make_async_copy(ref, ref, sem).wait()

    def to_depth(src, dst, send, recv, who):
        return pltpu.make_async_remote_copy(
            src_ref=src, dst_ref=dst, send_sem=send, recv_sem=recv,
            device_id={"depth": who}, device_id_type=mesh_id)

    def spread_start(row, send, recv):
        def one(j, _):
            to_depth(row, row, send, recv, (me + j) % BRICKS).start()
            return 0
        lax.fori_loop(1, BRICKS, one, 0)

    spans = (pl.ds(0, 8), pl.ds(8, 4), pl.ds(12, 3), pl.ds(12, 3), pl.ds(8, 4), pl.ds(0, 8))

    def spots(p):
        half = 8 * bits[p]
        fourth = half + 4 * bits[(p + 1) % 4]
        return half, fourth, fourth + 2 * bits[(p + 2) % 4] + bits[(p + 3) % 4]

    def hops(stage, s, p):
        half, fourth, mine = spots(p)
        d = [(p + t) % 4 for t in range(4)]

        def hop(src, dst, *dims):
            return to_depth(src, dst, s_sem.at[stage], r_sem.at[stage, s], other(*dims))

        if stage == 0:
            return [hop(p_ref.at[s, p, pl.ds(8 - half, 8)], recv_ref.at[s, p, spans[0]], d[0])]
        if stage == 1:
            return [hop(acc_ref.at[s, p, pl.ds(4 - (fourth - half), 4)], recv_ref.at[s, p, spans[1]], d[1])]
        if stage == 4:
            ref = r_ref.at[s, p, pl.ds(fourth, 4)]
            return [hop(ref, ref, d[1])]
        if stage == 5:
            ref = r_ref.at[s, p, pl.ds(half, 8)]
            return [hop(ref, ref, d[0])]
        out = []
        for k in (3, 1, 2):
            dims = [d[2]] * (k // 2) + [d[3]] * (k % 2)
            if stage == 2:
                there = [1 - bits[e] if e in dims else bits[e] for e in d[2:]]
                out.append(hop(acc_ref.at[s, p, fourth - half + 2 * there[0] + there[1]],
                               recv_ref.at[s, p, 11 + k], *dims))
            else:
                ref = r_ref.at[s, p, mine]
                out.append(hop(ref, ref, *dims))
        return out

    def send(stage, s, p):
        for copy in hops(stage, s, p):
            copy.start()

    def got_all(stage, s):
        arrived(recv_ref.at[s, :, spans[stage]], r_sem.at[stage, s])

    sample = lax.broadcasted_iota(jnp.int32, (smp, hid), 0)
    pair = ray * 2

    def forward(s):
        fetch(s).wait()
        if s == 0:
            for copy in weights[:4]:
                copy.wait()
        wden = jnp.broadcast_to(wden_ref[...].astype(F32), (smp, hid))
        sig = jnp.zeros((smp, ray), F32)
        for i in range(smp):
            pre = mm(f_ref[s, i], win_ref[...], NN)
            h = jnp.maximum(pre, 0.0).astype(BF16)
            hid_ref[s, i] = h
            sig = sig + mm(jnp.where(sample == i, wden, 0.0).astype(BF16), h, NT)
        here = pl.ds(s * ray, ray)
        row = lax.broadcasted_iota(jnp.int32, (smp, ray), 0)
        gate = jnp.where(row < cnt_ref[:, here], jnp.broadcast_to(step_ref[:, here], (smp, ray)), 0.0)
        soft = jnp.maximum(sig, 0.0) + jnp.log1p(jnp.exp(-jnp.abs(sig)))
        tau = soft * gate
        inner = running(tau, False)
        t_all[s // 2, me, :, s % 2 * ray:(s % 2 + 1) * ray] = (inner + tau)[smp - 1:smp]
        keep = jnp.exp(-tau)
        light = jnp.exp(-inner)
        lw = light * (1.0 - keep)
        keep_ref[s, 0] = lw
        keep_ref[s, 1] = light * keep
        keep_ref[s, 2] = sig
        keep_ref[s, 3] = gate
        lwt_ref[...] = lw.T

    def weigh(s):
        def tile(t, _):
            at = pl.ds(pl.multiple_of(t * 64, 64), 64)
            w = lwt_ref[at]
            total = jnp.zeros((64, hid), F32)
            for i in range(smp):
                total = total + w[:, i:i + 1] * hid_ref[s, i, at].astype(F32)
            hbar_ref[s, at] = total
            return 0
        lax.fori_loop(0, ray // 64, tile, 0)
        if s == 0:
            weights[4].wait()
        high, low = halves(hbar_ref[s])
        value = mm(high, wout_ref[...], NN) + mm(low, wout_ref[...], NN)
        for n in range(BRICKS):
            for p in range(PARTS):
                p_ref[s, p, place(p, n)] = value[n * rows:(n + 1) * rows, p * LANES:(p + 1) * LANES]

    def reduce_half(s):
        if s % 2 == 0:
            arrived(t_all.at[s // 2, pl.ds(0, BRICKS - 1)], tr_sem.at[s // 2])
            before = jnp.zeros((1, pair), F32)
            for b in range(BRICKS):
                light = jnp.exp(-before)
                e_all[s, b] = light[:, :ray]
                e_all[s + 1, b] = light[:, ray:]
                before = before + t_all[s // 2, b]
        row = lax.broadcasted_iota(jnp.int32, (smp, ray), 0)
        table = jnp.broadcast_to(e_all[s, me], (smp, ray))
        for d in range(4):
            table = jnp.where(row == d + 1, jnp.broadcast_to(e_all[s, other(d)], (smp, ray)), table)
        ecol_ref[s] = table.T.reshape(BRICKS, rows, smp)
        got_all(0, s)
        for p in range(PARTS):
            half = spots(p)[0]
            for i in range(8):
                e = ecol_ref[s, block_at(p, half + i)]
                acc_ref[s, p, i] = (e[:, :1] * p_ref[s, p, half + i]
                                    + e[:, p + 1:p + 2] * recv_ref[s, p, i])
            send(1, s, p)

    def reduce_fourth(s):
        got_all(1, s)
        for p in range(PARTS):
            half, fourth, _ = spots(p)
            here = pl.ds(fourth - half, 4)
            acc_ref[s, p, here] = acc_ref[s, p, here] + recv_ref[s, p, spans[1]]
            send(2, s, p)

    def reduce_block(s):
        if s == 0:
            arrived(tgt_ref, tgt_sem.at[0])
        got_all(2, s)
        for p in range(PARTS):
            half, _, mine = spots(p)
            total = acc_ref[s, p, mine - half] - tgt_ref[s, :, p * LANES:(p + 1) * LANES]
            for k in range(12, 15):
                total = total + recv_ref[s, p, k]
            r_ref[s, p, mine] = total
            send(3, s, p)

    def gather_fourth(s):
        got_all(3, s)
        for p in range(PARTS):
            send(4, s, p)

    def gather_half(s):
        got_all(4, s)
        for p in range(PARTS):
            send(5, s, p)

    def put_residual(s):
        return pltpu.make_async_copy(res_ref.at[s], res_hbm.at[s], out_sem.at[0])

    def own_terms(s):
        got_all(5, s)
        for n in range(BRICKS):
            total = None
            for p in range(PARTS):
                at = place(p, n)
                r = r_ref[s, p, at]
                res_ref[s, n * rows:(n + 1) * rows, p * LANES:(p + 1) * LANES] = r
                term = r * p_ref[s, p, at]
                total = term if p == 0 else total + term
            emt_ref[n * rows:(n + 1) * rows] = total
        put_residual(s).start()
        high, low = halves(emt_ref[...])
        ones = jnp.ones((smp, LANES), BF16)
        own = (mm(ones, high, NT) + mm(ones, low, NT))[:1] * e_all[s, me]
        own_all[s, me] = own
        spread_start(own_all.at[s, me], os_sem.at[0], or_sem.at[s])

    def emissions(s):
        r_high, r_low = halves(res_ref[s])
        v_ref[s] = mm(r_high, wout_ref[...], NT) + mm(r_low, wout_ref[...], NT)
        scaled = hbar_ref[s] * ecol_ref[s].reshape(ray, smp)[:, :1]
        b_high, b_low = halves(scaled)
        out = mm(b_high, r_high, TN) + mm(b_low, r_high, TN) + mm(b_high, r_low, TN)
        for c in range(COLS):
            mine = out[c * slab:(c + 1) * slab]
            go_ref[c % 2, c // 2] = mine if s == 0 else go_ref[c % 2, c // 2] + mine
        if s == STREAMS - 1:
            pair_copy.start()

        def tile(t, _):
            at = pl.ds(pl.multiple_of(t * 64, 64), 64)
            v = v_ref[s, at]
            lane = lax.broadcasted_iota(jnp.int32, (64, smp), 1)
            found = jnp.zeros((64, smp), F32)
            for i in range(smp):
                e = jnp.sum(v * hid_ref[s, i, at].astype(F32), 1, keepdims=True)
                found = jnp.where(lane == i, e, found)
            wt_ref[at] = found
            return 0
        lax.fori_loop(0, ray // 64, tile, 0)
        keep_ref[s, 4] = wt_ref[...].T

    def gradients(s):
        arrived(own_all.at[s, pl.ds(0, BRICKS - 1)], or_sem.at[s])
        after = jnp.zeros((1, ray), F32)
        for b in range(1, BRICKS):
            after = after + jnp.where(b > me, own_all[s, b], 0.0)
        em = keep_ref[s, 4]
        e = jnp.broadcast_to(e_all[s, me], (smp, ray))
        wgt = keep_ref[s, 0] * e
        later = running(wgt * em, True) + after
        dens = (keep_ref[s, 1] * e * em - later) * keep_ref[s, 3]
        dens_ref[:, pl.ds(s * ray, ray)] = dens
        dsig = dens / (1.0 + jnp.exp(-keep_ref[s, 2]))
        wt_ref[...] = wgt.T
        dt_ref[...] = dsig.T
        wden_row = wden_ref[...].astype(F32)

        def tile(t, _):
            at = pl.ds(pl.multiple_of(t * 32, 32), 32)
            v = v_ref[s, at]
            w = wt_ref[at]
            d = dt_ref[at]
            for i in range(smp):
                dh = w[:, i:i + 1] * v + d[:, i:i + 1] * wden_row
                h = hid_ref[s, i, at].astype(F32)
                dpre_ref[i, at] = jnp.where(h > 0.0, dh, 0.0).astype(BF16)
            return 0
        lax.fori_loop(0, ray // 32, tile, 0)
        if s == STREAMS - 1:
            share_out()
        g_in = mm(f_ref[s].reshape(smp * ray, -1), dpre_ref[...].reshape(smp * ray, hid), TN)
        d_high, d_low = halves(dsig)
        stacked = jnp.concatenate([d_high.astype(F32), d_low.astype(F32)], 0)
        row = lax.broadcasted_iota(jnp.int32, stacked.shape, 0)
        g_den = jnp.zeros((2 * smp, hid), F32)
        for i in range(smp):
            g_den = g_den + mm(jnp.where(row % smp == i, stacked, 0.0).astype(BF16), hid_ref[s, i], NN)
        g_den = g_den[:smp] + g_den[smp:]
        for c in range(COLS):
            mine = g_in[c * slab:(c + 1) * slab]
            if s == 0:
                gi_ref[c, :slab] = mine
                gi_ref[c, slab:] = g_den
            else:
                gi_ref[c, :slab] = gi_ref[c, :slab] + mine
                gi_ref[c, slab:] = gi_ref[c, slab:] + g_den

    x, core = col // 2, col % 2

    def to_col(src, dst, send, recv, who):
        return pltpu.make_async_remote_copy(
            src_ref=src, dst_ref=dst, send_sem=send, recv_sem=recv,
            device_id={"col": who}, device_id_type=mesh_id)

    pair_copy = to_col(go_ref.at[1 - core], go_pair, gs_sem.at[0], gr_sem.at[0], x * 2 + 1 - core)

    def share_out():
        pair_copy.wait_recv()
        go_sum[...] = go_ref[core] + go_pair[...]
        for j in (2, 1, 3):
            to = (x + j) % RING
            to_col(go_sum.at[to], go_recv.at[j - 1], gs_sem.at[1], gr_sem.at[1], to * 2 + core).start()

    def share_in(j, _):
        to = (col + j) % COLS
        to_col(gi_ref.at[to], gi_recv.at[j - 1], gs_sem.at[2], gr_sem.at[2], to).start()
        return 0

    for s in range(STREAMS):
        forward(s)
        if s == 0:
            pl.semaphore_wait(barrier, BRICKS - 1 + COLS - 1)
        if s % 2 == 1:
            spread_start(t_all.at[s // 2, me], ts_sem.at[0], tr_sem.at[s // 2])
        weigh(s)
        for p in range(PARTS):
            send(0, s, p)
    for step, s in ORDER:
        (reduce_half, reduce_fourth, reduce_block, gather_fourth, gather_half,
         own_terms, emissions, gradients)[step](s)
    lax.fori_loop(1, COLS, share_in, 0)
    dens_copy = pltpu.make_async_copy(dens_ref, dens_hbm, out_sem.at[1])
    dens_copy.start()
    arrived(go_recv, gr_sem.at[1])
    total = go_sum[x]
    for j in range(RING - 1):
        total = total + go_recv[j]
    gout_ref[...] = total
    gout_copy = pltpu.make_async_copy(gout_ref, gout_hbm, out_sem.at[2])
    gout_copy.start()
    for stage in range(6):
        arrived(recv_ref.at[:, :, spans[stage]], s_sem.at[stage])
    arrived(t_all.at[:, pl.ds(0, BRICKS - 1)], ts_sem.at[0])
    arrived(own_all.at[:, pl.ds(0, BRICKS - 1)], os_sem.at[0])
    pair_copy.wait_send()
    arrived(go_recv, gs_sem.at[1])
    arrived(res_ref, out_sem.at[0])
    dens_copy.wait()
    arrived(gi_recv, gr_sem.at[2])
    total = gi_ref[col]
    for j in range(COLS - 1):
        total = total + gi_recv[j]
    gin_ref[...] = total
    gin_copy = pltpu.make_async_copy(gin_ref, gin_hbm, out_sem.at[3])
    gin_copy.start()
    arrived(gi_recv, gs_sem.at[2])
    gout_copy.wait()
    gin_copy.wait()


def finish(res_in, dens_in, gin_in, gout_in, res_hbm, dens_hbm, gin_hbm, gden_hbm, gout_hbm,
           held, dens_ref, gin_ref, gout_ref, gden_ref, in_sem, out_sem):
    parts = res_in.shape[0]
    slab = gin_hbm.shape[0]
    take = [pltpu.make_async_copy(src, dst, in_sem.at[i]) for i, (src, dst) in enumerate(
        [(gin_in, gin_ref), (dens_in, dens_ref), (gout_in, gout_ref)]
        + [(res_in.at[i], held.at[i]) for i in range(parts)])]
    put = [pltpu.make_async_copy(src, dst, out_sem.at[i]) for i, (src, dst) in enumerate(
        [(gin_ref.at[pl.ds(0, slab)], gin_hbm), (dens_ref, dens_hbm), (gout_ref, gout_hbm)]
        + [(held.at[i], res_hbm.at[i]) for i in range(parts)] + [(gden_ref, gden_hbm)])]
    for copy in take:
        copy.start()
    for got, gone in zip(take, put):
        got.wait()
        gone.start()
    den = jnp.sum(gin_ref[slab:], 0, keepdims=True)
    col = lax.axis_index("col")
    mine = den[:, :slab]
    for c in range(1, COLS):
        mine = jnp.where(col == c, den[:, c * slab:(c + 1) * slab], mine)
    gden_ref[...] = mine
    put[-1].start()
    for copy in put:
        copy.wait()


def per_device(features, counts, steps, target, w_in, w_density, w_out):
    _, smp, nray, din = features.shape
    hid, width = w_out.shape[1:]
    ray = nray // STREAMS
    rows = ray // BRICKS
    slab = din // COLS
    hbm = pl.BlockSpec(memory_space=pl.ANY)
    dma = pltpu.SemaphoreType.DMA
    stage = (STREAMS, PARTS)
    scratch = [
        pltpu.VMEM((1, nray), jnp.int32),
        pltpu.VMEM((1, nray), F32),
        pltpu.VMEM((din, hid), BF16),
        pltpu.VMEM((1, hid), BF16),
        pltpu.VMEM((hid, width), BF16),
        pltpu.VMEM((smp, nray), F32),
        pltpu.VMEM((slab + smp, hid), F32),
        pltpu.VMEM((slab, width), F32),
        pltpu.VMEM((STREAMS, smp, ray, din), BF16),
        pltpu.VMEM((STREAMS, smp, ray, hid), BF16),
        pltpu.VMEM((ray, smp), F32),
        pltpu.VMEM((STREAMS, ray, hid), F32),
        pltpu.VMEM((*stage, BRICKS, rows, LANES), F32),
        pltpu.VMEM((*stage, BRICKS // 2, rows, LANES), F32),
        pltpu.VMEM((*stage, BRICKS - 1, rows, LANES), F32),
        pltpu.VMEM((*stage, BRICKS, rows, LANES), F32),
        pltpu.VMEM((STREAMS, ray, width), F32),
        pltpu.VMEM((ray, LANES), F32),
        pltpu.VMEM((STREAMS, rows, width), F32),
        pltpu.VMEM((STREAMS // 2, BRICKS, 1, 2 * ray), F32),
        pltpu.VMEM((STREAMS, BRICKS, 1, ray), F32),
        pltpu.VMEM((STREAMS, BRICKS, 1, ray), F32),
        pltpu.VMEM((STREAMS, BRICKS, rows, smp), F32),
        pltpu.VMEM((STREAMS, 5, smp, ray), F32),
        pltpu.VMEM((STREAMS, ray, hid), F32),
        pltpu.VMEM((ray, smp), F32),
        pltpu.VMEM((ray, smp), F32),
        pltpu.VMEM((smp, ray, hid), BF16),
        pltpu.VMEM((COLS, slab + smp, hid), F32),
        pltpu.VMEM((2, RING, slab, width), F32),
        pltpu.VMEM((COLS - 1, slab + smp, hid), F32),
        pltpu.VMEM((RING, slab, width), F32),
        pltpu.VMEM((RING, slab, width), F32),
        pltpu.VMEM((RING - 1, slab, width), F32),
        dma((5,)), dma((STREAMS,)), dma((1,)), dma((4,)),
        dma((6,)), dma((6, STREAMS)),
        dma((1,)), dma((STREAMS // 2,)), dma((1,)), dma((STREAMS,)),
        dma((3,)), dma((3,)),
    ]
    residual, dens, g_in, g_out = pl.pallas_call(
        body,
        out_shape=(
            jax.ShapeDtypeStruct((STREAMS, ray, width), F32),
            jax.ShapeDtypeStruct((smp, nray), F32),
            jax.ShapeDtypeStruct((slab + smp, hid), F32),
            jax.ShapeDtypeStruct((slab, width), F32),
        ),
        in_specs=[hbm] * 7,
        out_specs=(hbm,) * 4,
        scratch_shapes=scratch,
        compiler_params=pltpu.CompilerParams(
            collective_id=0, has_side_effects=True, vmem_limit_bytes=60 * 1024 * 1024),
        name="brick_step",
    )(features[0], counts, steps, target.reshape(STREAMS, BRICKS, rows, width), w_in[0], w_density, w_out[0])
    residual, dens, g_in, g_den, g_out = pl.pallas_call(
        finish,
        out_shape=(
            jax.ShapeDtypeStruct((STREAMS, ray, width), F32),
            jax.ShapeDtypeStruct((smp, nray), F32),
            jax.ShapeDtypeStruct((slab, hid), F32),
            jax.ShapeDtypeStruct((1, slab), F32),
            jax.ShapeDtypeStruct((slab, width), F32),
        ),
        in_specs=[hbm] * 4,
        out_specs=(hbm,) * 5,
        scratch_shapes=[
            pltpu.VMEM((STREAMS, ray, width), F32),
            pltpu.VMEM((smp, nray), F32),
            pltpu.VMEM((slab + smp, hid), F32),
            pltpu.VMEM((slab, width), F32),
            pltpu.VMEM((1, slab), F32),
            dma((3 + STREAMS,)), dma((4 + STREAMS,)),
        ],
        name="brick_finish",
    )(residual, dens, g_in, g_out)
    return residual.reshape(nray, width), dens[None], g_in[None], g_den, g_out[None]


def solution(mesh):
    return jax.shard_map(
        per_device,
        mesh=mesh,
        in_specs=(
            P("depth", None, "col", None),
            P("depth", "col"),
            P("depth", "col"),
            P("col", None),
            P("depth", None, None),
            P("depth", None),
            P("depth", None, None),
        ),
        out_specs=(
            P("col", None),
            P("depth", None, "col"),
            P("depth", "col", None),
            P("depth", "col"),
            P("depth", "col", None),
        ),
        check_vma=False,
    )
```

```python
import functools

import jax
import jax.numpy as jnp
from jax import lax
from jax.experimental import pallas as pl
from jax.experimental.pallas import tpu as pltpu
from jax.sharding import PartitionSpec as P

STREAMS = 4
RING = 4
BRICKS = 16
COLS = 8
LANES = 128
ORDER = ((0, 0), (0, 1), (1, 0), (0, 2), (1, 1), (0, 3), (2, 0), (1, 2), (2, 1), (1, 3), (2, 2),
         (3, 0), (4, 0), (2, 3), (3, 1), (4, 1), (3, 2), (4, 2), (3, 3), (4, 3))
F32 = jnp.float32
BF16 = jnp.bfloat16
NT = (((1,), (1,)), ((), ()))
TN = (((0,), (0,)), ((), ()))
NN = (((1,), (0,)), ((), ()))


def mm(a, b, dims):
    return lax.dot_general(a, b, dims, preferred_element_type=F32)


def halves(x):
    high = x.astype(BF16)
    return high, (x - high.astype(F32)).astype(BF16)


def running(x, reverse):
    rows = x.shape[0]
    row = lax.broadcasted_iota(jnp.int32, x.shape, 0)
    total = x
    hop = 1
    while hop < rows:
        moved = pltpu.roll(total, rows - hop if reverse else hop, 0)
        total = total + jnp.where(row < rows - hop if reverse else row >= hop, moved, 0.0)
        hop *= 2
    edge = row < rows - 1 if reverse else row >= 1
    return jnp.where(edge, pltpu.roll(total, rows - 1 if reverse else 1, 0), 0.0)


def body(f_hbm, cnt_hbm, step_hbm, tgt_hbm, win_hbm, wden_hbm, wout_hbm,
         res_hbm, dens_hbm, gin_hbm, gout_hbm,
         cnt_ref, step_ref, win_ref, wden_ref, wout_ref, dens_ref, gin_ref, gout_ref, wint_ref, wcol_ref, f_ref, hid_ref, hbar_ref, p_ref, ps_ref, acc_ref, recv1_ref, recv2_ref, r_ref, prod_ref, tgt_ref,
         t_all, e_all, own_all, ecol_ref, keep_ref, v_ref, dpre_ref, gt_ref, gd_ref,
         gi_ref, go_ref, gi_recv, go_pair, go_sum, go_recv,
         in_sem, f_sem, tgt_sem, out_sem, s_sem, r_sem, ts_sem, tr_sem, os_sem, or_sem, gs_sem, gr_sem):
    smp, ray = f_ref.shape[1], f_ref.shape[2]
    hid, width = wout_ref.shape
    part_rays = ray // 2
    quarter = part_rays // RING
    slab = gout_ref.shape[0]
    me = lax.axis_index("depth")
    col = lax.axis_index("col")
    y, z = me % RING, me // RING
    first, second = (y, z), (z, y)
    mesh_id = pl.DeviceIdType.MESH

    barrier = pltpu.get_barrier_semaphore()

    def greet_depth(j, _):
        pl.semaphore_signal(barrier, inc=1, device_id={"depth": (me + j) % BRICKS}, device_id_type=mesh_id)
        return 0

    def greet_col(j, _):
        pl.semaphore_signal(barrier, inc=1, device_id={"col": (col + j) % COLS}, device_id_type=mesh_id)
        return 0

    lax.fori_loop(1, BRICKS, greet_depth, 0)
    lax.fori_loop(1, COLS, greet_col, 0)

    weights = [
        pltpu.make_async_copy(src, dst, in_sem.at[i])
        for i, (src, dst) in enumerate((
            (win_hbm, win_ref), (wden_hbm, wden_ref), (cnt_hbm, cnt_ref), (step_hbm, step_ref),
            (wout_hbm, wout_ref)))
    ]

    def fetch(s):
        return pltpu.make_async_copy(f_hbm.at[:, pl.ds(s * ray, ray)], f_ref.at[s], f_sem.at[s])

    def fetch_target(s, part):
        return pltpu.make_async_copy(
            tgt_hbm.at[s, part, first[part], second[part]], tgt_ref.at[s, part], tgt_sem.at[0])

    fetch(0).start()
    for copy in weights:
        copy.start()
    for s in range(1, STREAMS):
        fetch(s).start()
    for s in range(STREAMS):
        for part in range(2):
            fetch_target(s, part).start()

    def arrived(ref, sem):
        pltpu.make_async_copy(ref, ref, sem).wait()

    def to_depth(src, dst, send, recv, who):
        return pltpu.make_async_remote_copy(
            src_ref=src, dst_ref=dst, send_sem=send, recv_sem=recv,
            device_id={"depth": who}, device_id_type=mesh_id)

    def spread_start(row, send, recv):
        def one(j, _):
            to_depth(row, row, send, recv, (me + j) % BRICKS).start()
            return 0
        lax.fori_loop(1, BRICKS, one, 0)

    def along(axis, j):
        at = (first[axis] + j) % RING
        return at, (z * RING + at if axis == 0 else at * RING + y)

    def hop(stage, s, part, j):
        near, far = first[part], second[part]
        at, who = along(part if stage in (0, 3) else 1 - part, j)
        if stage == 0:
            src, dst = p_ref.at[s, part, at], recv1_ref.at[s, part, j - 1]
        elif stage == 1:
            src, dst = acc_ref.at[s, part, at], recv2_ref.at[s, part, j - 1]
        elif stage == 2:
            src = dst = r_ref.at[s, part, near, far]
        else:
            src = dst = r_ref.at[s, part, near]
        return to_depth(src, dst, s_sem.at[stage], r_sem.at[stage, s, part], who)

    def send(stage, s, part):
        for j in (2, 1, 3):
            hop(stage, s, part, j).start()

    def got_all(stage, s, part):
        ref = recv1_ref if stage in (0, 3) else recv2_ref
        arrived(ref.at[s, part], r_sem.at[stage, s, part])

    sample = lax.broadcasted_iota(jnp.int32, (smp, hid), 0)
    pair = ray * 2

    def forward(s):
        fetch(s).wait()
        if s == 0:
            for copy in weights[:4]:
                copy.wait()
            wint_ref[...] = win_ref[...].astype(F32).T.astype(BF16)
            wcol_ref[...] = jnp.broadcast_to(wden_ref[...].astype(F32), (LANES, hid)).T
        wden = jnp.broadcast_to(wden_ref[...].astype(F32), (smp, hid))
        sig = jnp.zeros((smp, ray), F32)
        for i in range(smp):
            pre = mm(wint_ref[...], f_ref[s, i], NT)
            h = jnp.maximum(pre, 0.0).astype(BF16)
            hid_ref[s, i] = h
            sig = sig + mm(jnp.where(sample == i, wden, 0.0).astype(BF16), h, NN)
        here = pl.ds(s * ray, ray)
        row = lax.broadcasted_iota(jnp.int32, (smp, ray), 0)
        gate = jnp.where(row < cnt_ref[:, here], jnp.broadcast_to(step_ref[:, here], (smp, ray)), 0.0)
        soft = jnp.maximum(sig, 0.0) + jnp.log1p(jnp.exp(-jnp.abs(sig)))
        tau = soft * gate
        inner = running(tau, False)
        t_all[s // 2, me, :, s % 2 * ray:(s % 2 + 1) * ray] = (inner + tau)[smp - 1:smp]
        keep = jnp.exp(-tau)
        light = jnp.exp(-inner)
        lw = light * (1.0 - keep)
        keep_ref[s, 0] = lw
        keep_ref[s, 1] = light * keep
        keep_ref[s, 2] = sig
        keep_ref[s, 3] = gate

    def weigh(s):
        lw = keep_ref[s, 0]
        for t in range(0, hid, 32):
            total = None
            for i in range(smp):
                term = lw[i:i + 1] * hid_ref[s, i, t:t + 32].astype(F32)
                total = term if i == 0 else total + term
            hbar_ref[s, t:t + 32] = total
        if s == 0:
            weights[4].wait()
        high, low = halves(hbar_ref[s])
        value = mm(high, wout_ref[...], TN) + mm(low, wout_ref[...], TN)
        p_ref[s] = value.reshape(2, RING, quarter, width)

    def reduce_near(s):
        if s % 2 == 0:
            arrived(t_all.at[s // 2, pl.ds(0, BRICKS - 1)], tr_sem.at[s // 2])
            before = jnp.zeros((1, pair), F32)
            for b in range(BRICKS):
                light = jnp.exp(-before)
                e_all[s, b] = light[:, :ray]
                e_all[s + 1, b] = light[:, ray:]
                before = before + t_all[s // 2, b]
        row = lax.broadcasted_iota(jnp.int32, (smp, ray), 0)
        table = jnp.broadcast_to(e_all[s, me], (smp, ray))
        for part in range(2):
            for j in range(1, RING):
                mine = e_all[s, along(part, RING - j)[1]]
                table = jnp.where(row == part * RING + j, jnp.broadcast_to(mine, (smp, ray)), table)
        ecol_ref[s] = table.T.reshape(2, RING, quarter, smp)
        for part in range(2):
            near = first[part]
            e = ecol_ref[s, part, near]
            got_all(0, s, part)
            total = None
            for j in range(RING):
                got = p_ref[s, part, near] if j == 0 else recv1_ref[s, part, j - 1]
                got = e[:, part * RING + j:part * RING + j + 1] * got
                ps_ref[s, part, j] = got
                total = got if j == 0 else total + got
            acc_ref[s, part] = total.reshape(RING, quarter // RING, width)
            send(1, s, part)

    def reduce_far(s):
        if s == 0:
            arrived(tgt_ref, tgt_sem.at[0])
        for part in range(2):
            got_all(1, s, part)
            total = acc_ref[s, part, second[part]] - tgt_ref[s, part]
            for j in range(1, RING):
                total = total + recv2_ref[s, part, j - 1]
            r_ref[s, part, first[part], second[part]] = total
            send(2, s, part)

    def gather_far(s):
        for part in range(2):
            got_all(2, s, part)
            send(3, s, part)
        for part in range(2):
            r = r_ref[s, part, first[part]].reshape(quarter, width)
            for j in range(RING):
                prod_ref[pl.ds((part * RING + j) * quarter, quarter)] = ps_ref[s, part, j] * r
        high, low = halves(prod_ref[...])
        ones = jnp.ones((smp, width), BF16)
        own_all[s, me] = (mm(ones, high, NT) + mm(ones, low, NT))[:1]
        spread_start(own_all.at[s, me], os_sem.at[0], or_sem.at[s])

    def put_residual(s):
        return pltpu.make_async_copy(r_ref.at[s], res_hbm.at[s], out_sem.at[0])

    def gather_near(s):
        for part in range(2):
            got_all(3, s, part)
        put_residual(s).start()

    def emissions(s):
        gather_near(s)
        r_high, r_low = halves(r_ref[s].reshape(ray, width))
        v_ref[s] = mm(wout_ref[...], r_high, NT) + mm(wout_ref[...], r_low, NT)
        b_high, b_low = halves(hbar_ref[s] * e_all[s, me])
        out = mm(b_high, r_high, NN) + mm(b_low, r_high, NN) + mm(b_high, r_low, NN)
        for c in range(COLS):
            mine = out[c * slab:(c + 1) * slab]
            go_ref[c % 2, c // 2] = mine if s == 0 else go_ref[c % 2, c // 2] + mine
        if s == STREAMS - 1:
            pair_copy.start()

        row = lax.broadcasted_iota(jnp.int32, (smp, LANES), 0)
        for at in range(0, ray, LANES):
            here = slice(at, at + LANES)
            v = v_ref[s, :, here]
            em = jnp.zeros((smp, LANES), F32)
            for i in range(smp):
                e = jnp.sum(v * hid_ref[s, i, :, here].astype(F32), 0, keepdims=True)
                em = jnp.where(row == i, e, em)
            keep_ref[s, 4, :, here] = em

    def later_bricks(s):
        arrived(own_all.at[s, pl.ds(0, BRICKS - 1)], or_sem.at[s])
        lane = lax.broadcasted_iota(jnp.int32, (1, part_rays), 1)
        slot = lane // quarter
        out = []
        for part in range(2):
            whole = jnp.zeros((1, part_rays), F32)
            for near in range(RING):
                total = jnp.zeros((1, part_rays), F32)
                for far in range(RING):
                    source = (near + RING * far, near * RING + far)[part]
                    from_near = (near - slot + RING) % RING
                    brick = (far * RING + from_near, from_near * RING + far)[part]
                    term = own_all[s, source][:, part * part_rays:(part + 1) * part_rays]
                    total = total + jnp.where(brick > me, term, 0.0)
                total = total + pltpu.roll(total, quarter, 1)
                total = total + pltpu.roll(total, 2 * quarter, 1)
                whole = jnp.where(slot == near, total, whole)
            out.append(whole)
        return jnp.concatenate(out, 1)

    def gradients(s):
        e = jnp.broadcast_to(e_all[s, me], (smp, ray))
        em = keep_ref[s, 4]
        wgt = keep_ref[s, 0] * e
        later = running(wgt * em, True) + later_bricks(s)
        dens = (keep_ref[s, 1] * e * em - later) * keep_ref[s, 3]
        dens_ref[:, pl.ds(s * ray, ray)] = dens
        dsig = dens / (1.0 + jnp.exp(-keep_ref[s, 2]))
        for at in range(0, ray, LANES):
            here = slice(at, at + LANES)
            for t in range(0, hid, 64):
                down = slice(t, t + 64)
                v = v_ref[s, down, here]
                wden = wcol_ref[down]
                for i in range(smp):
                    dh = wgt[i:i + 1, here] * v + dsig[i:i + 1, here] * wden
                    dpre_ref[down, i * ray + at:i * ray + at + LANES] = jnp.where(
                        hid_ref[s, i, down, here] > 0, dh.astype(BF16), jnp.zeros((), BF16))
        if s == STREAMS - 1:
            share_out()
        g_in = mm(dpre_ref[...], f_ref[s].reshape(smp * ray, -1), NN)
        gt_ref[...] = g_in if s == 0 else gt_ref[...] + g_in
        d_high, d_low = halves(dsig)
        stacked = jnp.concatenate([d_high.astype(F32), d_low.astype(F32)], 0)
        row = lax.broadcasted_iota(jnp.int32, stacked.shape, 0)
        g_den = jnp.zeros((hid, 2 * smp), F32)
        for i in range(smp):
            g_den = g_den + mm(hid_ref[s, i], jnp.where(row % smp == i, stacked, 0.0).astype(BF16), NT)
        gd_ref[...] = g_den if s == 0 else gd_ref[...] + g_den
        if s == STREAMS - 1:
            turned = gt_ref[...].T
            den = gd_ref[...].T
            den = den[:smp] + den[smp:]
            for c in range(COLS):
                gi_ref[c, :slab] = turned[c * slab:(c + 1) * slab]
                gi_ref[c, slab:] = den

    x, core = col // 2, col % 2

    def to_col(src, dst, send, recv, who):
        return pltpu.make_async_remote_copy(
            src_ref=src, dst_ref=dst, send_sem=send, recv_sem=recv,
            device_id={"col": who}, device_id_type=mesh_id)

    pair_copy = to_col(go_ref.at[1 - core], go_pair, gs_sem.at[0], gr_sem.at[0], x * 2 + 1 - core)

    def share_out():
        pair_copy.wait_recv()
        go_sum[...] = go_ref[core] + go_pair[...]
        for j in (2, 1, 3):
            to = (x + j) % RING
            to_col(go_sum.at[to], go_recv.at[j - 1], gs_sem.at[1], gr_sem.at[1], to * 2 + core).start()

    def share_in(j, _):
        to = (col + j) % COLS
        to_col(gi_ref.at[to], gi_recv.at[j - 1], gs_sem.at[2], gr_sem.at[2], to).start()
        return 0

    for s in range(STREAMS):
        forward(s)
        if s == 0:
            pl.semaphore_wait(barrier, BRICKS - 1 + COLS - 1)
        if s % 2 == 1:
            spread_start(t_all.at[s // 2, me], ts_sem.at[0], tr_sem.at[s // 2])
        weigh(s)
        for part in range(2):
            send(0, s, part)
    for step, s in ORDER:
        (reduce_near, reduce_far, gather_far, emissions, gradients)[step](s)
    lax.fori_loop(1, COLS, share_in, 0)
    dens_copy = pltpu.make_async_copy(dens_ref, dens_hbm, out_sem.at[1])
    dens_copy.start()
    arrived(go_recv, gr_sem.at[1])
    total = go_sum[x]
    for j in range(RING - 1):
        total = total + go_recv[j]
    gout_ref[...] = total
    gout_copy = pltpu.make_async_copy(gout_ref, gout_hbm, out_sem.at[2])
    gout_copy.start()
    arrived(recv1_ref, s_sem.at[0])
    arrived(recv2_ref, s_sem.at[1])
    arrived(recv2_ref, s_sem.at[2])
    arrived(recv1_ref, s_sem.at[3])
    arrived(t_all.at[:, pl.ds(0, BRICKS - 1)], ts_sem.at[0])
    arrived(own_all.at[:, pl.ds(0, BRICKS - 1)], os_sem.at[0])
    pair_copy.wait_send()
    arrived(go_recv, gs_sem.at[1])
    arrived(r_ref, out_sem.at[0])
    dens_copy.wait()
    arrived(gi_recv, gr_sem.at[2])
    total = gi_ref[col]
    for j in range(COLS - 1):
        total = total + gi_recv[j]
    gin_ref[...] = total
    gin_copy = pltpu.make_async_copy(gin_ref, gin_hbm, out_sem.at[3])
    gin_copy.start()
    arrived(gi_recv, gs_sem.at[2])
    gout_copy.wait()
    gin_copy.wait()


def finish(res_in, dens_in, gin_in, gout_in, res_hbm, dens_hbm, gin_hbm, gden_hbm, gout_hbm,
           held, dens_ref, gin_ref, gout_ref, gden_ref, in_sem, out_sem):
    parts = res_in.shape[0]
    slab = gin_hbm.shape[0]
    take = [pltpu.make_async_copy(src, dst, in_sem.at[i]) for i, (src, dst) in enumerate(
        [(gin_in, gin_ref), (dens_in, dens_ref), (gout_in, gout_ref)]
        + [(res_in.at[i], held.at[i]) for i in range(parts)])]
    put = [pltpu.make_async_copy(src, dst, out_sem.at[i]) for i, (src, dst) in enumerate(
        [(gin_ref.at[pl.ds(0, slab)], gin_hbm), (dens_ref, dens_hbm), (gout_ref, gout_hbm)]
        + [(held.at[i], res_hbm.at[i]) for i in range(parts)] + [(gden_ref, gden_hbm)])]
    for copy in take:
        copy.start()
    for got, gone in zip(take, put):
        got.wait()
        gone.start()
    den = jnp.sum(gin_ref[slab:], 0, keepdims=True)
    col = lax.axis_index("col")
    mine = den[:, :slab]
    for c in range(1, COLS):
        mine = jnp.where(col == c, den[:, c * slab:(c + 1) * slab], mine)
    gden_ref[...] = mine
    put[-1].start()
    for copy in put:
        copy.wait()


def per_device(features, counts, steps, target, w_in, w_density, w_out):
    _, smp, nray, din = features.shape
    hid, width = w_out.shape[1:]
    ray = nray // STREAMS
    quarter = ray // 2 // RING
    piece = quarter // RING
    slab = din // COLS
    hbm = pl.BlockSpec(memory_space=pl.ANY)
    dma = pltpu.SemaphoreType.DMA
    split = (STREAMS, 2, RING, RING, piece, width)
    scratch = [
        pltpu.VMEM((1, nray), jnp.int32),
        pltpu.VMEM((1, nray), F32),
        pltpu.VMEM((din, hid), BF16),
        pltpu.VMEM((1, hid), BF16),
        pltpu.VMEM((hid, width), BF16),
        pltpu.VMEM((smp, nray), F32),
        pltpu.VMEM((slab + smp, hid), F32),
        pltpu.VMEM((slab, width), F32),
        pltpu.VMEM((hid, din), BF16),
        pltpu.VMEM((hid, LANES), F32),
        pltpu.VMEM((STREAMS, smp, ray, din), BF16),
        pltpu.VMEM((STREAMS, smp, hid, ray), BF16),
        pltpu.VMEM((STREAMS, hid, ray), F32),
        pltpu.VMEM((STREAMS, 2, RING, quarter, width), F32),
        pltpu.VMEM((STREAMS, 2, RING, quarter, width), F32),
        pltpu.VMEM((STREAMS, 2, RING, piece, width), F32),
        pltpu.VMEM((STREAMS, 2, RING - 1, quarter, width), F32),
        pltpu.VMEM((STREAMS, 2, RING - 1, piece, width), F32),
        pltpu.VMEM(split, F32),
        pltpu.VMEM((ray, width), F32),
        pltpu.VMEM((STREAMS, 2, piece, width), F32),
        pltpu.VMEM((STREAMS // 2, BRICKS, 1, 2 * ray), F32),
        pltpu.VMEM((STREAMS, BRICKS, 1, ray), F32),
        pltpu.VMEM((STREAMS, BRICKS, 1, ray), F32),
        pltpu.VMEM((STREAMS, 2, RING, quarter, smp), F32),
        pltpu.VMEM((STREAMS, 5, smp, ray), F32),
        pltpu.VMEM((STREAMS, hid, ray), F32),
        pltpu.VMEM((hid, smp * ray), BF16),
        pltpu.VMEM((hid, din), F32),
        pltpu.VMEM((hid, 2 * smp), F32),
        pltpu.VMEM((COLS, slab + smp, hid), F32),
        pltpu.VMEM((2, RING, slab, width), F32),
        pltpu.VMEM((COLS - 1, slab + smp, hid), F32),
        pltpu.VMEM((RING, slab, width), F32),
        pltpu.VMEM((RING, slab, width), F32),
        pltpu.VMEM((RING - 1, slab, width), F32),
        dma((5,)), dma((STREAMS,)), dma((1,)), dma((4,)),
        dma((4,)), dma((4, STREAMS, 2)),
        dma((1,)), dma((STREAMS // 2,)), dma((1,)), dma((STREAMS,)),
        dma((3,)), dma((3,)),
    ]
    residual, dens, g_in, g_out = pl.pallas_call(
        body,
        out_shape=(
            jax.ShapeDtypeStruct(split, F32),
            jax.ShapeDtypeStruct((smp, nray), F32),
            jax.ShapeDtypeStruct((slab + smp, hid), F32),
            jax.ShapeDtypeStruct((slab, width), F32),
        ),
        in_specs=[hbm] * 7,
        out_specs=(hbm,) * 4,
        scratch_shapes=scratch,
        compiler_params=pltpu.CompilerParams(
            collective_id=0, has_side_effects=True, vmem_limit_bytes=60 * 1024 * 1024),
        name="brick_step",
    )(features[0], counts, steps, target.reshape(split), w_in[0], w_density, w_out[0])
    residual, dens, g_in, g_den, g_out = pl.pallas_call(
        finish,
        out_shape=(
            jax.ShapeDtypeStruct((STREAMS, ray, width), F32),
            jax.ShapeDtypeStruct((smp, nray), F32),
            jax.ShapeDtypeStruct((slab, hid), F32),
            jax.ShapeDtypeStruct((1, slab), F32),
            jax.ShapeDtypeStruct((slab, width), F32),
        ),
        in_specs=[hbm] * 4,
        out_specs=(hbm,) * 5,
        scratch_shapes=[
            pltpu.VMEM((STREAMS, ray, width), F32),
            pltpu.VMEM((smp, nray), F32),
            pltpu.VMEM((slab + smp, hid), F32),
            pltpu.VMEM((slab, width), F32),
            pltpu.VMEM((1, slab), F32),
            dma((3 + STREAMS,)), dma((4 + STREAMS,)),
        ],
        name="brick_finish",
    )(residual.reshape(STREAMS, ray, width), dens, g_in, g_out)
    return residual.reshape(nray, width), dens[None], g_in[None], g_den, g_out[None]


def solution(mesh):
    return jax.shard_map(
        per_device,
        mesh=mesh,
        in_specs=(
            P("depth", None, "col", None),
            P("depth", "col"),
            P("depth", "col"),
            P("col", None),
            P("depth", None, None),
            P("depth", None),
            P("depth", None, None),
        ),
        out_specs=(
            P("col", None),
            P("depth", None, "col"),
            P("depth", "col", None),
            P("depth", "col"),
            P("depth", "col", None),
        ),
        check_vma=False,
    )
```

```python
import functools

import jax
import jax.numpy as jnp
from jax import lax
from jax.experimental import pallas as pl
from jax.experimental.pallas import tpu as pltpu
from jax.sharding import PartitionSpec as P

STREAMS = 4
RING = 4
BRICKS = 16
COLS = 8
LANES = 128
ORDER = ((0, 0), (0, 1), (0, 2), (0, 3), (1, 0), (1, 1), (1, 2), (1, 3), (2, 0), (2, 1), (2, 2), (2, 3),
         (3, 0), (4, 0), (3, 1), (4, 1), (3, 2), (4, 2), (3, 3), (4, 3))
F32 = jnp.float32
BF16 = jnp.bfloat16
NT = (((1,), (1,)), ((), ()))
TN = (((0,), (0,)), ((), ()))
NN = (((1,), (0,)), ((), ()))


def mm(a, b, dims):
    return lax.dot_general(a, b, dims, preferred_element_type=F32)


def halves(x):
    high = x.astype(BF16)
    return high, (x - high.astype(F32)).astype(BF16)


def running(x, reverse):
    rows = x.shape[0]
    row = lax.broadcasted_iota(jnp.int32, x.shape, 0)
    total = x
    hop = 1
    while hop < rows:
        moved = pltpu.roll(total, rows - hop if reverse else hop, 0)
        total = total + jnp.where(row < rows - hop if reverse else row >= hop, moved, 0.0)
        hop *= 2
    edge = row < rows - 1 if reverse else row >= 1
    return jnp.where(edge, pltpu.roll(total, rows - 1 if reverse else 1, 0), 0.0)


def body(f_hbm, cnt_hbm, step_hbm, tgt_hbm, win_hbm, wden_hbm, wout_hbm,
         res_hbm, dens_hbm, gin_hbm, gout_hbm,
         cnt_ref, step_ref, win_ref, wden_ref, wout_ref, dens_ref, gin_ref, gout_ref, wint_ref, wcol_ref, f_ref, hid_ref, hbar_ref, p_ref, ps_ref, acc_ref, recv1_ref, recv2_ref, r_ref, prod_ref, tgt_ref,
         t_all, e_all, own_all, ecol_ref, keep_ref, v_ref, dpre_ref, gt_ref, gd_ref,
         gi_ref, go_ref, gi_recv, go_pair, go_sum, go_recv,
         in_sem, f_sem, tgt_sem, out_sem, s_sem, r_sem, ts_sem, tr_sem, os_sem, or_sem, gs_sem, gr_sem):
    smp, ray = f_ref.shape[1], f_ref.shape[2]
    hid, width = wout_ref.shape
    part_rays = ray // 2
    half_rays = part_rays // 2
    half_width = width // 2
    parts = [(rp, cp) for rp in range(2) for cp in range(2)]
    slab = gout_ref.shape[0]
    me = lax.axis_index("depth")
    col = lax.axis_index("col")
    y, z = me % RING, me // RING
    bits = ((y // 2 + y % 2) % 2, y // 2, (z // 2 + z % 2) % 2, z // 2)

    def moved(at, low, high):
        if low and high:
            return (at + 2) % RING
        return RING - 1 - at if high else at + 1 - 2 * (at % 2) if low else at

    def other(*dims):
        return (moved(z, 2 in dims, 3 in dims) * RING
                + moved(y, 0 in dims, 1 in dims))

    def spot(rp, cp, flipped=()):
        d = 2 * rp + cp
        block = 0
        for e in range(4):
            if e != d:
                block = block * 2 + (1 - bits[e] if e in flipped else bits[e])
        return d, bits[d], block

    mesh_id = pl.DeviceIdType.MESH

    barrier = pltpu.get_barrier_semaphore()

    def greet_depth(j, _):
        pl.semaphore_signal(barrier, inc=1, device_id={"depth": (me + j) % BRICKS}, device_id_type=mesh_id)
        return 0

    def greet_col(j, _):
        pl.semaphore_signal(barrier, inc=1, device_id={"col": (col + j) % COLS}, device_id_type=mesh_id)
        return 0

    lax.fori_loop(1, BRICKS, greet_depth, 0)
    lax.fori_loop(1, COLS, greet_col, 0)

    weights = [
        pltpu.make_async_copy(src, dst, in_sem.at[i])
        for i, (src, dst) in enumerate((
            (win_hbm, win_ref), (wden_hbm, wden_ref), (cnt_hbm, cnt_ref), (step_hbm, step_ref),
            (wout_hbm, wout_ref)))
    ]

    def fetch(s):
        return pltpu.make_async_copy(f_hbm.at[:, pl.ds(s * ray, ray)], f_ref.at[s], f_sem.at[s])

    def fetch_target(s, rp, cp):
        _, half, block = spot(rp, cp)
        return pltpu.make_async_copy(
            tgt_hbm.at[s, rp, half, block, :, pl.ds(cp * half_width, half_width)],
            tgt_ref.at[s, rp, cp], tgt_sem.at[0])

    fetch(0).start()
    for copy in weights:
        copy.start()
    for s in range(1, STREAMS):
        fetch(s).start()
    for s in range(STREAMS):
        for rp, cp in parts:
            fetch_target(s, rp, cp).start()

    def arrived(ref, sem):
        pltpu.make_async_copy(ref, ref, sem).wait()

    def to_depth(src, dst, send, recv, who):
        return pltpu.make_async_remote_copy(
            src_ref=src, dst_ref=dst, send_sem=send, recv_sem=recv,
            device_id={"depth": who}, device_id_type=mesh_id)

    def spread_start(row, send, recv):
        def one(j, _):
            to_depth(row, row, send, recv, (me + j) % BRICKS).start()
            return 0
        lax.fori_loop(1, BRICKS, one, 0)

    def hops(stage, s, rp, cp):
        d, half, block = spot(rp, cp)

        def hop(src, dst, *dims):
            return to_depth(src, dst, s_sem.at[stage], r_sem.at[stage, s], other(*dims))

        if stage == 0:
            return [hop(p_ref.at[s, cp, rp, 1 - half], recv1_ref.at[s, rp, cp], d)]
        if stage == 3:
            ref = r_ref.at[s, cp, rp, half]
            return [hop(ref, ref, d)]
        out = []
        rest = [e for e in range(4) if e != d]
        for k in (7, 6, 5, 3, 4, 2, 1):
            dims = [e for i, e in enumerate(rest) if k // 2 ** i % 2]
            if stage == 1:
                out.append(hop(acc_ref.at[s, rp, cp, spot(rp, cp, dims)[2]],
                               recv2_ref.at[s, rp, cp, k - 1], *dims))
            else:
                ref = r_ref.at[s, cp, rp, half, block]
                out.append(hop(ref, ref, *dims))
        return out

    def send(stage, s, rp, cp):
        for copy in hops(stage, s, rp, cp):
            copy.start()

    def got_all(stage, s):
        ref = recv1_ref if stage in (0, 3) else recv2_ref
        arrived(ref.at[s], r_sem.at[stage, s])

    sample = lax.broadcasted_iota(jnp.int32, (smp, hid), 0)
    pair = ray * 2

    def forward(s):
        fetch(s).wait()
        if s == 0:
            for copy in weights[:4]:
                copy.wait()
            wint_ref[...] = win_ref[...].astype(F32).T.astype(BF16)
            wcol_ref[...] = jnp.broadcast_to(wden_ref[...].astype(F32), (LANES, hid)).T
        wden = jnp.broadcast_to(wden_ref[...].astype(F32), (smp, hid))
        sig = jnp.zeros((smp, ray), F32)
        for i in range(smp):
            pre = mm(wint_ref[...], f_ref[s, i], NT)
            h = jnp.maximum(pre, 0.0).astype(BF16)
            hid_ref[s, i] = h
            sig = sig + mm(jnp.where(sample == i, wden, 0.0).astype(BF16), h, NN)
        here = pl.ds(s * ray, ray)
        row = lax.broadcasted_iota(jnp.int32, (smp, ray), 0)
        gate = jnp.where(row < cnt_ref[:, here], jnp.broadcast_to(step_ref[:, here], (smp, ray)), 0.0)
        soft = jnp.maximum(sig, 0.0) + jnp.log1p(jnp.exp(-jnp.abs(sig)))
        tau = soft * gate
        inner = running(tau, False)
        t_all[s // 2, me, :, s % 2 * ray:(s % 2 + 1) * ray] = (inner + tau)[smp - 1:smp]
        keep = jnp.exp(-tau)
        light = jnp.exp(-inner)
        lw = light * (1.0 - keep)
        keep_ref[s, 0] = lw
        keep_ref[s, 1] = light * keep
        keep_ref[s, 2] = sig
        keep_ref[s, 3] = gate

    def weigh(s):
        lw = keep_ref[s, 0]
        for t in range(0, hid, 32):
            total = None
            for i in range(smp):
                term = lw[i:i + 1] * hid_ref[s, i, t:t + 32].astype(F32)
                total = term if i == 0 else total + term
            hbar_ref[s, t:t + 32] = total
        if s == 0:
            weights[4].wait()
        high, low = halves(hbar_ref[s])
        value = mm(high, wout_ref[...], TN) + mm(low, wout_ref[...], TN)
        for cp in range(2):
            p_ref[s, cp] = value[:, cp * half_width:(cp + 1) * half_width].reshape(p_ref.shape[2:])

    def reduce_near(s):
        if s % 2 == 0:
            arrived(t_all.at[s // 2, pl.ds(0, BRICKS - 1)], tr_sem.at[s // 2])
            before = jnp.zeros((1, pair), F32)
            for b in range(BRICKS):
                light = jnp.exp(-before)
                e_all[s, b] = light[:, :ray]
                e_all[s + 1, b] = light[:, ray:]
                before = before + t_all[s // 2, b]
        row = lax.broadcasted_iota(jnp.int32, (smp, ray), 0)
        table = jnp.broadcast_to(e_all[s, me], (smp, ray))
        for d in range(4):
            table = jnp.where(row == d + 1, jnp.broadcast_to(e_all[s, other(d)], (smp, ray)), table)
        ecol_ref[s] = table.T.reshape(2, 2, half_rays, smp)
        got_all(0, s)
        for rp, cp in parts:
            d, half, _ = spot(rp, cp)
            e = ecol_ref[s, rp, half]
            own = e[:, :1] * p_ref[s, cp, rp, half].reshape(half_rays, half_width)
            got = e[:, d + 1:d + 2] * recv1_ref[s, rp, cp].reshape(half_rays, half_width)
            ps_ref[s, rp, cp, 0] = own
            ps_ref[s, rp, cp, 1] = got
            acc_ref[s, rp, cp] = (own + got).reshape(acc_ref.shape[3:])
            send(1, s, rp, cp)

    def reduce_far(s):
        if s == 0:
            arrived(tgt_ref, tgt_sem.at[0])
        got_all(1, s)
        for rp, cp in parts:
            _, half, block = spot(rp, cp)
            total = acc_ref[s, rp, cp, block] - tgt_ref[s, rp, cp]
            for k in range(7):
                total = total + recv2_ref[s, rp, cp, k]
            r_ref[s, cp, rp, half, block] = total
            send(2, s, rp, cp)

    def gather_far(s):
        got_all(2, s)
        for rp, cp in parts:
            send(3, s, rp, cp)
        for i, (rp, cp) in enumerate(parts):
            r = r_ref[s, cp, rp, spot(rp, cp)[1]].reshape(half_rays, half_width)
            for j in range(2):
                prod_ref[pl.ds((2 * i + j) * half_rays, half_rays)] = ps_ref[s, rp, cp, j] * r
        high, low = halves(prod_ref[...])
        ones = jnp.ones((smp, half_width), BF16)
        own_all[s, me] = (mm(ones, high, NT) + mm(ones, low, NT))[:1]
        spread_start(own_all.at[s, me], os_sem.at[0], or_sem.at[s])

    def put_residual(s, cp):
        return pltpu.make_async_copy(
            r_ref.at[s, cp], res_hbm.at[s, :, :, :, :, pl.ds(cp * half_width, half_width)], out_sem.at[0])

    def gather_near(s):
        got_all(3, s)
        for cp in range(2):
            put_residual(s, cp).start()

    def emissions(s):
        gather_near(s)
        b_high, b_low = halves(hbar_ref[s] * e_all[s, me])
        v = None
        out = []
        for cp in range(2):
            r_high, r_low = halves(r_ref[s, cp].reshape(ray, half_width))
            w = wout_ref[:, cp * half_width:(cp + 1) * half_width]
            term = mm(w, r_high, NT) + mm(w, r_low, NT)
            v = term if cp == 0 else v + term
            out.append(mm(b_high, r_high, NN) + mm(b_low, r_high, NN) + mm(b_high, r_low, NN))
        v_ref[s] = v
        out = jnp.concatenate(out, 1)
        for c in range(COLS):
            mine = out[c * slab:(c + 1) * slab]
            go_ref[c % 2, c // 2] = mine if s == 0 else go_ref[c % 2, c // 2] + mine
        if s == STREAMS - 1:
            pair_copy.start()

        row = lax.broadcasted_iota(jnp.int32, (smp, LANES), 0)
        for at in range(0, ray, LANES):
            here = slice(at, at + LANES)
            v = v_ref[s, :, here]
            em = jnp.zeros((smp, LANES), F32)
            for i in range(smp):
                e = jnp.sum(v * hid_ref[s, i, :, here].astype(F32), 0, keepdims=True)
                em = jnp.where(row == i, e, em)
            keep_ref[s, 4, :, here] = em

    def later_bricks(s):
        arrived(own_all.at[s, pl.ds(0, BRICKS - 1)], or_sem.at[s])
        side = lax.broadcasted_iota(jnp.int32, (1, part_rays), 1) // half_rays
        out = []
        for rp in range(2):
            whole = jnp.zeros((1, part_rays), F32)
            for cp in range(2):
                d = 2 * rp + cp
                totals = [jnp.zeros((1, part_rays), F32) for _ in range(2)]
                for source in range(BRICKS):
                    at = (source % RING, source // RING)
                    code = (at[0] ^ at[0] // 2) + RING * (at[1] ^ at[1] // 2)
                    mate = (moved(at[1], d == 2, d == 3) * RING
                            + moved(at[0], d == 0, d == 1))
                    term = own_all[s, source][:, d * part_rays:(d + 1) * part_rays]
                    brick = jnp.where(side == 0, source, mate)
                    half = code >> d & 1
                    totals[half] = totals[half] + jnp.where(brick > me, term, 0.0)
                totals = [t + pltpu.roll(t, half_rays, 1) for t in totals]
                whole = whole + jnp.where(side == 0, totals[0], totals[1])
            out.append(whole)
        return jnp.concatenate(out, 1)

    def gradients(s):
        e = jnp.broadcast_to(e_all[s, me], (smp, ray))
        em = keep_ref[s, 4]
        wgt = keep_ref[s, 0] * e
        later = running(wgt * em, True) + later_bricks(s)
        dens = (keep_ref[s, 1] * e * em - later) * keep_ref[s, 3]
        dens_ref[:, pl.ds(s * ray, ray)] = dens
        dsig = dens / (1.0 + jnp.exp(-keep_ref[s, 2]))
        for at in range(0, ray, LANES):
            here = slice(at, at + LANES)
            for t in range(0, hid, 64):
                down = slice(t, t + 64)
                v = v_ref[s, down, here]
                wden = wcol_ref[down]
                for i in range(smp):
                    dh = wgt[i:i + 1, here] * v + dsig[i:i + 1, here] * wden
                    dpre_ref[down, i * ray + at:i * ray + at + LANES] = jnp.where(
                        hid_ref[s, i, down, here] > 0, dh.astype(BF16), jnp.zeros((), BF16))
        g_in = mm(dpre_ref[...], f_ref[s].reshape(smp * ray, -1), NN)
        gt_ref[...] = g_in if s == 0 else gt_ref[...] + g_in
        d_high, d_low = halves(dsig)
        stacked = jnp.concatenate([d_high.astype(F32), d_low.astype(F32)], 0)
        row = lax.broadcasted_iota(jnp.int32, stacked.shape, 0)
        g_den = jnp.zeros((hid, 2 * smp), F32)
        for i in range(smp):
            g_den = g_den + mm(hid_ref[s, i], jnp.where(row % smp == i, stacked, 0.0).astype(BF16), NT)
        gd_ref[...] = g_den if s == 0 else gd_ref[...] + g_den
        if s == STREAMS - 1:
            turned = gt_ref[...].T
            den = gd_ref[...].T
            den = den[:smp] + den[smp:]
            for c in range(COLS):
                gi_ref[c, :slab] = turned[c * slab:(c + 1) * slab]
                gi_ref[c, slab:] = den

    x, core = col // 2, col % 2

    def to_col(src, dst, send, recv, who):
        return pltpu.make_async_remote_copy(
            src_ref=src, dst_ref=dst, send_sem=send, recv_sem=recv,
            device_id={"col": who}, device_id_type=mesh_id)

    pair_copy = to_col(go_ref.at[1 - core], go_pair, gs_sem.at[0], gr_sem.at[0], x * 2 + 1 - core)

    def share_out():
        pair_copy.wait_recv()
        go_sum[...] = go_ref[core] + go_pair[...]
        for j in (2, 1, 3):
            to = (x + j) % RING
            to_col(go_sum.at[to], go_recv.at[j - 1], gs_sem.at[1], gr_sem.at[1], to * 2 + core).start()

    def share_in(j, _):
        to = (col + j) % COLS
        to_col(gi_ref.at[to], gi_recv.at[j - 1], gs_sem.at[2], gr_sem.at[2], to).start()
        return 0

    for s in range(STREAMS):
        forward(s)
        if s == 0:
            pl.semaphore_wait(barrier, BRICKS - 1 + COLS - 1)
        if s % 2 == 1:
            spread_start(t_all.at[s // 2, me], ts_sem.at[0], tr_sem.at[s // 2])
        weigh(s)
        for rp, cp in parts:
            send(0, s, rp, cp)
    for step, s in ORDER:
        (reduce_near, reduce_far, gather_far, emissions, gradients)[step](s)
    lax.fori_loop(1, COLS, share_in, 0)
    share_out()
    dens_copy = pltpu.make_async_copy(dens_ref, dens_hbm, out_sem.at[1])
    dens_copy.start()
    arrived(go_recv, gr_sem.at[1])
    total = go_sum[x]
    for j in range(RING - 1):
        total = total + go_recv[j]
    gout_ref[...] = total
    gout_copy = pltpu.make_async_copy(gout_ref, gout_hbm, out_sem.at[2])
    gout_copy.start()
    arrived(recv1_ref, s_sem.at[0])
    arrived(recv2_ref, s_sem.at[1])
    arrived(recv2_ref, s_sem.at[2])
    arrived(recv1_ref, s_sem.at[3])
    arrived(t_all.at[:, pl.ds(0, BRICKS - 1)], ts_sem.at[0])
    arrived(own_all.at[:, pl.ds(0, BRICKS - 1)], os_sem.at[0])
    pair_copy.wait_send()
    arrived(go_recv, gs_sem.at[1])
    arrived(r_ref, out_sem.at[0])
    dens_copy.wait()
    arrived(gi_recv, gr_sem.at[2])
    total = gi_ref[col]
    for j in range(COLS - 1):
        total = total + gi_recv[j]
    gin_ref[...] = total
    gin_copy = pltpu.make_async_copy(gin_ref, gin_hbm, out_sem.at[3])
    gin_copy.start()
    arrived(gi_recv, gs_sem.at[2])
    gout_copy.wait()
    gin_copy.wait()


def finish(res_in, dens_in, gin_in, gout_in, res_hbm, dens_hbm, gin_hbm, gden_hbm, gout_hbm,
           held, dens_ref, gin_ref, gout_ref, gden_ref, in_sem, out_sem):
    parts = res_in.shape[0]
    slab = gin_hbm.shape[0]
    take = [pltpu.make_async_copy(src, dst, in_sem.at[i]) for i, (src, dst) in enumerate(
        [(gin_in, gin_ref), (dens_in, dens_ref), (gout_in, gout_ref)]
        + [(res_in.at[i], held.at[i]) for i in range(parts)])]
    put = [pltpu.make_async_copy(src, dst, out_sem.at[i]) for i, (src, dst) in enumerate(
        [(gin_ref.at[pl.ds(0, slab)], gin_hbm), (dens_ref, dens_hbm), (gout_ref, gout_hbm)]
        + [(held.at[i], res_hbm.at[i]) for i in range(parts)] + [(gden_ref, gden_hbm)])]
    for copy in take:
        copy.start()
    for got, gone in zip(take, put):
        got.wait()
        gone.start()
    den = jnp.sum(gin_ref[slab:], 0, keepdims=True)
    col = lax.axis_index("col")
    mine = den[:, :slab]
    for c in range(1, COLS):
        mine = jnp.where(col == c, den[:, c * slab:(c + 1) * slab], mine)
    gden_ref[...] = mine
    put[-1].start()
    for copy in put:
        copy.wait()


def per_device(features, counts, steps, target, w_in, w_density, w_out):
    _, smp, nray, din = features.shape
    hid, width = w_out.shape[1:]
    ray = nray // STREAMS
    half_rays = ray // 4
    half_width = width // 2
    block = half_rays // 8
    slab = din // COLS
    hbm = pl.BlockSpec(memory_space=pl.ANY)
    dma = pltpu.SemaphoreType.DMA
    split = (STREAMS, 2, 2, 8, block, width)
    quads = (STREAMS, 2, 2)
    scratch = [
        pltpu.VMEM((1, nray), jnp.int32),
        pltpu.VMEM((1, nray), F32),
        pltpu.VMEM((din, hid), BF16),
        pltpu.VMEM((1, hid), BF16),
        pltpu.VMEM((hid, width), BF16),
        pltpu.VMEM((smp, nray), F32),
        pltpu.VMEM((slab + smp, hid), F32),
        pltpu.VMEM((slab, width), F32),
        pltpu.VMEM((hid, din), BF16),
        pltpu.VMEM((hid, LANES), F32),
        pltpu.VMEM((STREAMS, smp, ray, din), BF16),
        pltpu.VMEM((STREAMS, smp, hid, ray), BF16),
        pltpu.VMEM((STREAMS, hid, ray), F32),
        pltpu.VMEM((*quads, 2, 8, block, half_width), F32),
        pltpu.VMEM((*quads, 2, half_rays, half_width), F32),
        pltpu.VMEM((*quads, 8, block, half_width), F32),
        pltpu.VMEM((*quads, 8, block, half_width), F32),
        pltpu.VMEM((*quads, 7, block, half_width), F32),
        pltpu.VMEM((*quads, 2, 8, block, half_width), F32),
        pltpu.VMEM((2 * ray, half_width), F32),
        pltpu.VMEM((*quads, block, half_width), F32),
        pltpu.VMEM((STREAMS // 2, BRICKS, 1, 2 * ray), F32),
        pltpu.VMEM((STREAMS, BRICKS, 1, ray), F32),
        pltpu.VMEM((STREAMS, BRICKS, 1, 2 * ray), F32),
        pltpu.VMEM((STREAMS, 2, 2, half_rays, smp), F32),
        pltpu.VMEM((STREAMS, 5, smp, ray), F32),
        pltpu.VMEM((STREAMS, hid, ray), F32),
        pltpu.VMEM((hid, smp * ray), BF16),
        pltpu.VMEM((hid, din), F32),
        pltpu.VMEM((hid, 2 * smp), F32),
        pltpu.VMEM((COLS, slab + smp, hid), F32),
        pltpu.VMEM((2, RING, slab, width), F32),
        pltpu.VMEM((COLS - 1, slab + smp, hid), F32),
        pltpu.VMEM((RING, slab, width), F32),
        pltpu.VMEM((RING, slab, width), F32),
        pltpu.VMEM((RING - 1, slab, width), F32),
        dma((5,)), dma((STREAMS,)), dma((1,)), dma((4,)),
        dma((4,)), dma((4, STREAMS)),
        dma((1,)), dma((STREAMS // 2,)), dma((1,)), dma((STREAMS,)),
        dma((3,)), dma((3,)),
    ]
    residual, dens, g_in, g_out = pl.pallas_call(
        body,
        out_shape=(
            jax.ShapeDtypeStruct(split, F32),
            jax.ShapeDtypeStruct((smp, nray), F32),
            jax.ShapeDtypeStruct((slab + smp, hid), F32),
            jax.ShapeDtypeStruct((slab, width), F32),
        ),
        in_specs=[hbm] * 7,
        out_specs=(hbm,) * 4,
        scratch_shapes=scratch,
        compiler_params=pltpu.CompilerParams(
            collective_id=0, has_side_effects=True, vmem_limit_bytes=60 * 1024 * 1024),
        name="brick_step",
    )(features[0], counts, steps, target.reshape(split), w_in[0], w_density, w_out[0])
    residual, dens, g_in, g_den, g_out = pl.pallas_call(
        finish,
        out_shape=(
            jax.ShapeDtypeStruct((STREAMS, ray, width), F32),
            jax.ShapeDtypeStruct((smp, nray), F32),
            jax.ShapeDtypeStruct((slab, hid), F32),
            jax.ShapeDtypeStruct((1, slab), F32),
            jax.ShapeDtypeStruct((slab, width), F32),
        ),
        in_specs=[hbm] * 4,
        out_specs=(hbm,) * 5,
        scratch_shapes=[
            pltpu.VMEM((STREAMS, ray, width), F32),
            pltpu.VMEM((smp, nray), F32),
            pltpu.VMEM((slab + smp, hid), F32),
            pltpu.VMEM((slab, width), F32),
            pltpu.VMEM((1, slab), F32),
            dma((3 + STREAMS,)), dma((4 + STREAMS,)),
        ],
        name="brick_finish",
    )(residual.reshape(STREAMS, ray, width), dens, g_in, g_out)
    return residual.reshape(nray, width), dens[None], g_in[None], g_den, g_out[None]


def solution(mesh):
    return jax.shard_map(
        per_device,
        mesh=mesh,
        in_specs=(
            P("depth", None, "col", None),
            P("depth", "col"),
            P("depth", "col"),
            P("col", None),
            P("depth", None, None),
            P("depth", None),
            P("depth", None, None),
        ),
        out_specs=(
            P("col", None),
            P("depth", None, "col"),
            P("depth", "col", None),
            P("depth", "col"),
            P("depth", "col", None),
        ),
        check_vma=False,
    )
```

```python
import functools

import jax
import jax.numpy as jnp
from jax import lax
from jax.experimental import pallas as pl
from jax.experimental.pallas import tpu as pltpu
from jax.sharding import PartitionSpec as P

STREAMS = 4
RING = 4
BRICKS = 16
COLS = 8
LANES = 128
ORDER = ((0, 0), (0, 1), (0, 2), (0, 3), (1, 0), (1, 1), (1, 2), (1, 3), (2, 0), (2, 1), (2, 2), (2, 3),
         (3, 0), (4, 0), (3, 1), (4, 1), (3, 2), (4, 2), (3, 3), (4, 3))
F32 = jnp.float32
BF16 = jnp.bfloat16
NT = (((1,), (1,)), ((), ()))
TN = (((0,), (0,)), ((), ()))
NN = (((1,), (0,)), ((), ()))


def mm(a, b, dims):
    return lax.dot_general(a, b, dims, preferred_element_type=F32)


def halves(x):
    high = x.astype(BF16)
    return high, (x - high.astype(F32)).astype(BF16)


def running(x, reverse):
    rows = x.shape[0]
    row = lax.broadcasted_iota(jnp.int32, x.shape, 0)
    total = x
    hop = 1
    while hop < rows:
        moved = pltpu.roll(total, rows - hop if reverse else hop, 0)
        total = total + jnp.where(row < rows - hop if reverse else row >= hop, moved, 0.0)
        hop *= 2
    edge = row < rows - 1 if reverse else row >= 1
    return jnp.where(edge, pltpu.roll(total, rows - 1 if reverse else 1, 0), 0.0)


def body(f_hbm, cnt_hbm, step_hbm, tgt_hbm, win_hbm, wden_hbm, wout_hbm,
         res_hbm, dens_hbm, gin_hbm, gout_hbm,
         cnt_ref, step_ref, win_ref, wden_ref, wout_ref, dens_ref, gin_ref, gout_ref, wint_ref, wcol_ref, f_ref, hid_ref, hbar_ref, p_ref, ps_ref, acc_ref, recv1_ref, recv2_ref, r_ref, prod_ref, tgt_ref,
         t_all, e_all, own_all, ecol_ref, keep_ref, v_ref, dpre_ref, gt_ref, gd_ref,
         gi_ref, go_ref, gi_recv, gr_ref, gr_recv, go_pair, go_sum, go_recv,
         in_sem, f_sem, tgt_sem, out_sem, s_sem, r_sem, ts_sem, tr_sem, os_sem, or_sem, gs_sem, gr_sem):
    smp, ray = f_ref.shape[1], f_ref.shape[2]
    hid, width = wout_ref.shape
    part_rays = ray // 2
    half_rays = part_rays // 2
    half_width = width // 2
    parts = [(rp, cp) for rp in range(2) for cp in range(2)]
    slab = gout_ref.shape[0]
    me = lax.axis_index("depth")
    col = lax.axis_index("col")
    y, z = me % RING, me // RING
    bits = ((y // 2 + y % 2) % 2, y // 2, (z // 2 + z % 2) % 2, z // 2)

    def moved(at, low, high):
        if low and high:
            return (at + 2) % RING
        return RING - 1 - at if high else at + 1 - 2 * (at % 2) if low else at

    def other(*dims):
        return (moved(z, 2 in dims, 3 in dims) * RING
                + moved(y, 0 in dims, 1 in dims))

    def spot(rp, cp, flipped=()):
        d = 2 * rp + cp
        block = 0
        for e in range(4):
            if e != d:
                block = block * 2 + (1 - bits[e] if e in flipped else bits[e])
        return d, bits[d], block

    mesh_id = pl.DeviceIdType.MESH

    weights = [
        pltpu.make_async_copy(src, dst, in_sem.at[i])
        for i, (src, dst) in enumerate((
            (win_hbm, win_ref), (wden_hbm, wden_ref), (cnt_hbm, cnt_ref), (step_hbm, step_ref),
            (wout_hbm, wout_ref)))
    ]

    def fetch(s):
        return pltpu.make_async_copy(f_hbm.at[:, pl.ds(s * ray, ray)], f_ref.at[s], f_sem.at[s])

    def fetch_target(s, rp, cp):
        _, half, block = spot(rp, cp)
        return pltpu.make_async_copy(
            tgt_hbm.at[s, rp, half, block, :, pl.ds(cp * half_width, half_width)],
            tgt_ref.at[s, rp, cp], tgt_sem.at[0])

    weights[0].start()
    fetch(0).start()
    for copy in weights[1:]:
        copy.start()

    barrier = pltpu.get_barrier_semaphore()

    def greet_depth(j, _):
        pl.semaphore_signal(barrier, inc=1, device_id={"depth": (me + j) % BRICKS}, device_id_type=mesh_id)
        return 0

    def greet_col(j, _):
        pl.semaphore_signal(barrier, inc=1, device_id={"col": (col + j) % COLS}, device_id_type=mesh_id)
        return 0

    lax.fori_loop(1, BRICKS, greet_depth, 0)
    lax.fori_loop(1, COLS, greet_col, 0)

    for s in range(1, STREAMS):
        fetch(s).start()
    for s in range(STREAMS):
        for rp, cp in parts:
            fetch_target(s, rp, cp).start()

    def arrived(ref, sem):
        pltpu.make_async_copy(ref, ref, sem).wait()

    def to_depth(src, dst, send, recv, who):
        return pltpu.make_async_remote_copy(
            src_ref=src, dst_ref=dst, send_sem=send, recv_sem=recv,
            device_id={"depth": who}, device_id_type=mesh_id)

    def spread_start(row, send, recv):
        def one(j, _):
            to_depth(row, row, send, recv, (me + j) % BRICKS).start()
            return 0
        lax.fori_loop(1, BRICKS, one, 0)

    def hops(stage, s, rp, cp):
        d, half, block = spot(rp, cp)

        def hop(src, dst, *dims):
            return to_depth(src, dst, s_sem.at[stage], r_sem.at[stage, s], other(*dims))

        if stage == 0:
            return [hop(p_ref.at[s, cp, rp, 1 - half], recv1_ref.at[s, rp, cp], d)]
        if stage == 3:
            ref = r_ref.at[s, cp, rp, half]
            return [hop(ref, ref, d)]
        out = []
        rest = [e for e in range(4) if e != d]
        for k in (7, 6, 5, 3, 4, 2, 1):
            dims = [e for i, e in enumerate(rest) if k // 2 ** i % 2]
            if stage == 1:
                out.append(hop(acc_ref.at[s, rp, cp, spot(rp, cp, dims)[2]],
                               recv2_ref.at[s, rp, cp, k - 1], *dims))
            else:
                ref = r_ref.at[s, cp, rp, half, block]
                out.append(hop(ref, ref, *dims))
        return out

    def send(stage, s, rp, cp):
        for copy in hops(stage, s, rp, cp):
            copy.start()

    def got_all(stage, s):
        ref = recv1_ref if stage in (0, 3) else recv2_ref
        arrived(ref.at[s], r_sem.at[stage, s])

    pair = ray * 2

    def forward(s):
        if s == 0:
            weights[0].wait()
            wint_ref[...] = win_ref[...].astype(F32).T.astype(BF16)
            for copy in weights[1:4]:
                copy.wait()
            wcol_ref[...] = jnp.broadcast_to(wden_ref[...].astype(F32), (LANES, hid)).T
        fetch(s).wait()
        place = lax.broadcasted_iota(jnp.int32, (smp, ray), 0)
        sig = jnp.zeros((smp, ray), F32)
        for i in range(smp):
            pre = mm(wint_ref[...], f_ref[s, i], NT)
            h = jnp.maximum(pre, 0.0).astype(BF16)
            hid_ref[s, i] = h
            dense = jnp.sum(h.astype(F32) * jnp.concatenate([wcol_ref[...]] * (ray // LANES), 1), 0, keepdims=True)
            sig = jnp.where(place == i, dense, sig)
        here = pl.ds(s * ray, ray)
        row = lax.broadcasted_iota(jnp.int32, (smp, ray), 0)
        gate = jnp.where(row < cnt_ref[:, here], jnp.broadcast_to(step_ref[:, here], (smp, ray)), 0.0)
        soft = jnp.maximum(sig, 0.0) + jnp.log1p(jnp.exp(-jnp.abs(sig)))
        tau = soft * gate
        inner = running(tau, False)
        t_all[s // 2, me, :, s % 2 * ray:(s % 2 + 1) * ray] = (inner + tau)[smp - 1:smp]
        keep = jnp.exp(-tau)
        light = jnp.exp(-inner)
        lw = light * (1.0 - keep)
        keep_ref[s, 0] = lw
        keep_ref[s, 1] = light * keep
        keep_ref[s, 2] = sig
        keep_ref[s, 3] = gate

    def weigh(s):
        lw = keep_ref[s, 0]
        for t in range(0, hid, 32):
            total = None
            for i in range(smp):
                term = lw[i:i + 1] * hid_ref[s, i, t:t + 32].astype(F32)
                total = term if i == 0 else total + term
            hbar_ref[s, t:t + 32] = total
        if s == 0:
            weights[4].wait()
        high, low = halves(hbar_ref[s])
        value = mm(high, wout_ref[...], TN) + mm(low, wout_ref[...], TN)
        for cp in range(2):
            p_ref[s, cp] = value[:, cp * half_width:(cp + 1) * half_width].reshape(p_ref.shape[2:])

    def reduce_near(s):
        if s % 2 == 0:
            arrived(t_all.at[s // 2, pl.ds(0, BRICKS - 1)], tr_sem.at[s // 2])
            before = jnp.zeros((1, pair), F32)
            for b in range(BRICKS):
                light = jnp.exp(-before)
                e_all[s, b] = light[:, :ray]
                e_all[s + 1, b] = light[:, ray:]
                before = before + t_all[s // 2, b]
        row = lax.broadcasted_iota(jnp.int32, (smp, ray), 0)
        table = jnp.broadcast_to(e_all[s, me], (smp, ray))
        for d in range(4):
            table = jnp.where(row == d + 1, jnp.broadcast_to(e_all[s, other(d)], (smp, ray)), table)
        ecol_ref[s] = table.T.reshape(2, 2, half_rays, smp)
        got_all(0, s)
        for rp, cp in parts:
            d, half, _ = spot(rp, cp)
            e = ecol_ref[s, rp, half]
            own = e[:, :1] * p_ref[s, cp, rp, half].reshape(half_rays, half_width)
            got = e[:, d + 1:d + 2] * recv1_ref[s, rp, cp].reshape(half_rays, half_width)
            ps_ref[s, rp, cp, 0] = own
            ps_ref[s, rp, cp, 1] = got
            acc_ref[s, rp, cp] = (own + got).reshape(acc_ref.shape[3:])
            send(1, s, rp, cp)

    def reduce_far(s):
        if s == 0:
            arrived(tgt_ref, tgt_sem.at[0])
        got_all(1, s)
        for rp, cp in parts:
            _, half, block = spot(rp, cp)
            total = acc_ref[s, rp, cp, block] - tgt_ref[s, rp, cp]
            for k in range(7):
                total = total + recv2_ref[s, rp, cp, k]
            r_ref[s, cp, rp, half, block] = total
            send(2, s, rp, cp)

    def gather_far(s):
        got_all(2, s)
        for rp, cp in parts:
            send(3, s, rp, cp)
        for i, (rp, cp) in enumerate(parts):
            r = r_ref[s, cp, rp, spot(rp, cp)[1]].reshape(half_rays, half_width)
            for j in range(2):
                prod_ref[pl.ds((2 * i + j) * half_rays, half_rays)] = ps_ref[s, rp, cp, j] * r
        high, low = halves(prod_ref[...])
        ones = jnp.ones((smp, half_width), BF16)
        own_all[s, me] = (mm(ones, high, NT) + mm(ones, low, NT))[:1]
        spread_start(own_all.at[s, me], os_sem.at[0], or_sem.at[s])

    def put_residual(s, cp):
        return pltpu.make_async_copy(
            r_ref.at[s, cp], res_hbm.at[s, :, :, :, :, pl.ds(cp * half_width, half_width)], out_sem.at[0])

    def gather_near(s):
        got_all(3, s)
        for cp in range(2):
            put_residual(s, cp).start()

    def emissions(s):
        gather_near(s)
        b_high, b_low = halves(hbar_ref[s] * e_all[s, me])
        v = None
        out = []
        for cp in range(2):
            r_high, r_low = halves(r_ref[s, cp].reshape(ray, half_width))
            w = wout_ref[:, cp * half_width:(cp + 1) * half_width]
            term = mm(w, r_high, NT) + mm(w, r_low, NT)
            v = term if cp == 0 else v + term
            out.append(mm(b_high, r_high, NN) + mm(b_low, r_high, NN))
        v_ref[s] = v
        out = jnp.concatenate(out, 1)
        for c in range(COLS):
            mine = out[c * slab:(c + 1) * slab]
            go_ref[c % 2, c // 2] = mine if s == 0 else go_ref[c % 2, c // 2] + mine
        if s == STREAMS - 1:
            pair_copy.start()

        row = lax.broadcasted_iota(jnp.int32, (smp, LANES), 0)
        for at in range(0, ray, LANES):
            here = slice(at, at + LANES)
            v = v_ref[s, :, here]
            em = jnp.zeros((smp, LANES), F32)
            for i in range(smp):
                e = jnp.sum(v * hid_ref[s, i, :, here].astype(F32), 0, keepdims=True)
                em = jnp.where(row == i, e, em)
            keep_ref[s, 4, :, here] = em

    def later_bricks(s):
        arrived(own_all.at[s, pl.ds(0, BRICKS - 1)], or_sem.at[s])
        side = lax.broadcasted_iota(jnp.int32, (1, part_rays), 1) // half_rays
        out = []
        for rp in range(2):
            whole = jnp.zeros((1, part_rays), F32)
            for cp in range(2):
                d = 2 * rp + cp
                totals = [jnp.zeros((1, part_rays), F32) for _ in range(2)]
                for source in range(BRICKS):
                    at = (source % RING, source // RING)
                    code = (at[0] ^ at[0] // 2) + RING * (at[1] ^ at[1] // 2)
                    mate = (moved(at[1], d == 2, d == 3) * RING
                            + moved(at[0], d == 0, d == 1))
                    term = own_all[s, source][:, d * part_rays:(d + 1) * part_rays]
                    brick = jnp.where(side == 0, source, mate)
                    half = code >> d & 1
                    totals[half] = totals[half] + jnp.where(brick > me, term, 0.0)
                totals = [t + pltpu.roll(t, half_rays, 1) for t in totals]
                whole = whole + jnp.where(side == 0, totals[0], totals[1])
            out.append(whole)
        return jnp.concatenate(out, 1)

    def gradients(s):
        e = jnp.broadcast_to(e_all[s, me], (smp, ray))
        em = keep_ref[s, 4]
        wgt = keep_ref[s, 0] * e
        later = running(wgt * em, True) + later_bricks(s)
        dens = (keep_ref[s, 1] * e * em - later) * keep_ref[s, 3]
        dens_ref[:, pl.ds(s * ray, ray)] = dens
        dsig = dens / (1.0 + jnp.exp(-keep_ref[s, 2]))
        for at in range(0, ray, LANES):
            here = slice(at, at + LANES)
            for t in range(0, hid, 64):
                down = slice(t, t + 64)
                v = v_ref[s, down, here]
                wden = wcol_ref[down]
                for i in range(smp):
                    dh = wgt[i:i + 1, here] * v + dsig[i:i + 1, here] * wden
                    dpre_ref[down, i * ray + at:i * ray + at + LANES] = jnp.where(
                        hid_ref[s, i, down, here] > 0, dh.astype(BF16), jnp.zeros((), BF16))
        g_in = mm(dpre_ref[...], f_ref[s].reshape(smp * ray, -1), NN)
        gt_ref[...] = g_in if s == 0 else gt_ref[...] + g_in
        d_high, d_low = halves(dsig)
        stacked = jnp.concatenate([d_high.astype(F32), d_low.astype(F32)], 0)
        row = lax.broadcasted_iota(jnp.int32, stacked.shape, 0)
        g_den = jnp.zeros((hid, 2 * smp), F32)
        for i in range(smp):
            g_den = g_den + mm(hid_ref[s, i], jnp.where(row % smp == i, stacked, 0.0).astype(BF16), NT)
        gd_ref[...] = g_den if s == 0 else gd_ref[...] + g_den
        if s == STREAMS - 1:
            turned = gt_ref[...].T
            den = gd_ref[...].T
            gr_ref[...] = jnp.sum(den, 0, keepdims=True)
            gi_ref[...] = turned.reshape(gi_ref.shape)

    x, core = col // 2, col % 2

    def to_col(src, dst, send, recv, who):
        return pltpu.make_async_remote_copy(
            src_ref=src, dst_ref=dst, send_sem=send, recv_sem=recv,
            device_id={"col": who}, device_id_type=mesh_id)

    pair_copy = to_col(go_ref.at[1 - core], go_pair, gs_sem.at[0], gr_sem.at[0], x * 2 + 1 - core)

    def share_out():
        pair_copy.wait_recv()
        go_sum[...] = go_ref[core] + go_pair[...]
        for j in (2, 1, 3):
            to = (x + j) % RING
            to_col(go_sum.at[to], go_recv.at[j - 1], gs_sem.at[1], gr_sem.at[1], to * 2 + core).start()

    def share_in(j, _):
        to = (col + j) % COLS
        to_col(gi_ref.at[to], gi_recv.at[j - 1], gs_sem.at[2], gr_sem.at[2], to).start()
        to_col(gr_ref, gr_recv.at[j - 1], gs_sem.at[3], gr_sem.at[3], to).start()
        return 0

    for s in range(STREAMS):
        forward(s)
        if s == 0:
            pl.semaphore_wait(barrier, BRICKS - 1 + COLS - 1)
        if s % 2 == 1:
            spread_start(t_all.at[s // 2, me], ts_sem.at[0], tr_sem.at[s // 2])
        weigh(s)
        for rp, cp in parts:
            send(0, s, rp, cp)
    for step, s in ORDER:
        (reduce_near, reduce_far, gather_far, emissions, gradients)[step](s)
    lax.fori_loop(1, COLS, share_in, 0)
    share_out()
    dens_copy = pltpu.make_async_copy(dens_ref, dens_hbm, out_sem.at[1])
    dens_copy.start()
    arrived(go_recv, gr_sem.at[1])
    total = go_sum[x]
    for j in range(RING - 1):
        total = total + go_recv[j]
    gout_ref[...] = total
    gout_copy = pltpu.make_async_copy(gout_ref, gout_hbm, out_sem.at[2])
    gout_copy.start()
    arrived(recv1_ref, s_sem.at[0])
    arrived(recv2_ref, s_sem.at[1])
    arrived(recv2_ref, s_sem.at[2])
    arrived(recv1_ref, s_sem.at[3])
    arrived(t_all.at[:, pl.ds(0, BRICKS - 1)], ts_sem.at[0])
    arrived(own_all.at[:, pl.ds(0, BRICKS - 1)], os_sem.at[0])
    pair_copy.wait_send()
    arrived(go_recv, gs_sem.at[1])
    arrived(r_ref, out_sem.at[0])
    dens_copy.wait()
    arrived(gi_recv, gr_sem.at[2])
    total = gi_ref[col]
    for j in range(COLS - 1):
        total = total + gi_recv[j]
    gin_ref[:slab] = total
    arrived(gr_recv, gr_sem.at[3])
    total = gr_ref[...]
    for j in range(COLS - 1):
        total = total + gr_recv[j]
    gin_ref[slab:] = jnp.broadcast_to(total, (smp, hid))
    gin_copy = pltpu.make_async_copy(gin_ref, gin_hbm, out_sem.at[3])
    gin_copy.start()
    arrived(gi_recv, gs_sem.at[2])
    arrived(gr_recv, gs_sem.at[3])
    gout_copy.wait()
    gin_copy.wait()


def finish(res_in, dens_in, gin_in, gout_in, res_hbm, dens_hbm, gin_hbm, gden_hbm, gout_hbm,
           held, dens_ref, gin_ref, gout_ref, gden_ref, in_sem, out_sem):
    parts = res_in.shape[0]
    slab = gin_hbm.shape[0]
    take = [pltpu.make_async_copy(src, dst, in_sem.at[i]) for i, (src, dst) in enumerate(
        [(gin_in, gin_ref), (dens_in, dens_ref), (gout_in, gout_ref)]
        + [(res_in.at[i], held.at[i]) for i in range(parts)])]
    put = [pltpu.make_async_copy(src, dst, out_sem.at[i]) for i, (src, dst) in enumerate(
        [(gin_ref.at[pl.ds(0, slab)], gin_hbm), (dens_ref, dens_hbm), (gout_ref, gout_hbm)]
        + [(held.at[i], res_hbm.at[i]) for i in range(parts)] + [(gden_ref, gden_hbm)])]
    for copy in take:
        copy.start()
    for got, gone in zip(take, put):
        got.wait()
        gone.start()
    den = gin_ref[slab:slab + 1]
    col = lax.axis_index("col")
    mine = den[:, :slab]
    for c in range(1, COLS):
        mine = jnp.where(col == c, den[:, c * slab:(c + 1) * slab], mine)
    gden_ref[...] = mine
    put[-1].start()
    for copy in put:
        copy.wait()


def per_device(features, counts, steps, target, w_in, w_density, w_out):
    _, smp, nray, din = features.shape
    hid, width = w_out.shape[1:]
    ray = nray // STREAMS
    half_rays = ray // 4
    half_width = width // 2
    block = half_rays // 8
    slab = din // COLS
    hbm = pl.BlockSpec(memory_space=pl.ANY)
    dma = pltpu.SemaphoreType.DMA
    split = (STREAMS, 2, 2, 8, block, width)
    quads = (STREAMS, 2, 2)
    scratch = [
        pltpu.VMEM((1, nray), jnp.int32),
        pltpu.VMEM((1, nray), F32),
        pltpu.VMEM((din, hid), BF16),
        pltpu.VMEM((1, hid), BF16),
        pltpu.VMEM((hid, width), BF16),
        pltpu.VMEM((smp, nray), F32),
        pltpu.VMEM((slab + smp, hid), F32),
        pltpu.VMEM((slab, width), F32),
        pltpu.VMEM((hid, din), BF16),
        pltpu.VMEM((hid, LANES), F32),
        pltpu.VMEM((STREAMS, smp, ray, din), BF16),
        pltpu.VMEM((STREAMS, smp, hid, ray), BF16),
        pltpu.VMEM((STREAMS, hid, ray), F32),
        pltpu.VMEM((*quads, 2, 8, block, half_width), F32),
        pltpu.VMEM((*quads, 2, half_rays, half_width), F32),
        pltpu.VMEM((*quads, 8, block, half_width), F32),
        pltpu.VMEM((*quads, 8, block, half_width), F32),
        pltpu.VMEM((*quads, 7, block, half_width), F32),
        pltpu.VMEM((*quads, 2, 8, block, half_width), F32),
        pltpu.VMEM((2 * ray, half_width), F32),
        pltpu.VMEM((*quads, block, half_width), F32),
        pltpu.VMEM((STREAMS // 2, BRICKS, 1, 2 * ray), F32),
        pltpu.VMEM((STREAMS, BRICKS, 1, ray), F32),
        pltpu.VMEM((STREAMS, BRICKS, 1, 2 * ray), F32),
        pltpu.VMEM((STREAMS, 2, 2, half_rays, smp), F32),
        pltpu.VMEM((STREAMS, 5, smp, ray), F32),
        pltpu.VMEM((STREAMS, hid, ray), F32),
        pltpu.VMEM((hid, smp * ray), BF16),
        pltpu.VMEM((hid, din), F32),
        pltpu.VMEM((hid, 2 * smp), F32),
        pltpu.VMEM((COLS, slab, hid), F32),
        pltpu.VMEM((2, RING, slab, width), F32),
        pltpu.VMEM((COLS - 1, slab, hid), F32),
        pltpu.VMEM((1, hid), F32),
        pltpu.VMEM((COLS - 1, 1, hid), F32),
        pltpu.VMEM((RING, slab, width), F32),
        pltpu.VMEM((RING, slab, width), F32),
        pltpu.VMEM((RING - 1, slab, width), F32),
        dma((5,)), dma((STREAMS,)), dma((1,)), dma((4,)),
        dma((4,)), dma((4, STREAMS)),
        dma((1,)), dma((STREAMS // 2,)), dma((1,)), dma((STREAMS,)),
        dma((4,)), dma((4,)),
    ]
    residual, dens, g_in, g_out = pl.pallas_call(
        body,
        out_shape=(
            jax.ShapeDtypeStruct(split, F32),
            jax.ShapeDtypeStruct((smp, nray), F32),
            jax.ShapeDtypeStruct((slab + smp, hid), F32),
            jax.ShapeDtypeStruct((slab, width), F32),
        ),
        in_specs=[hbm] * 7,
        out_specs=(hbm,) * 4,
        scratch_shapes=scratch,
        compiler_params=pltpu.CompilerParams(
            collective_id=0, has_side_effects=True, vmem_limit_bytes=60 * 1024 * 1024),
        name="brick_step",
    )(features[0], counts, steps, target.reshape(split), w_in[0], w_density, w_out[0])
    residual, dens, g_in, g_den, g_out = pl.pallas_call(
        finish,
        out_shape=(
            jax.ShapeDtypeStruct((8, nray // 8, width), F32),
            jax.ShapeDtypeStruct((smp, nray), F32),
            jax.ShapeDtypeStruct((slab, hid), F32),
            jax.ShapeDtypeStruct((1, slab), F32),
            jax.ShapeDtypeStruct((slab, width), F32),
        ),
        in_specs=[hbm] * 4,
        out_specs=(hbm,) * 5,
        scratch_shapes=[
            pltpu.VMEM((8, nray // 8, width), F32),
            pltpu.VMEM((smp, nray), F32),
            pltpu.VMEM((slab + smp, hid), F32),
            pltpu.VMEM((slab, width), F32),
            pltpu.VMEM((1, slab), F32),
            dma((11,)), dma((12,)),
        ],
        name="brick_finish",
    )(residual.reshape(8, nray // 8, width), dens, g_in, g_out)
    return residual.reshape(nray, width), dens[None], g_in[None], g_den, g_out[None]


def solution(mesh):
    return jax.shard_map(
        per_device,
        mesh=mesh,
        in_specs=(
            P("depth", None, "col", None),
            P("depth", "col"),
            P("depth", "col"),
            P("col", None),
            P("depth", None, None),
            P("depth", None),
            P("depth", None, None),
        ),
        out_specs=(
            P("col", None),
            P("depth", None, "col"),
            P("depth", "col", None),
            P("depth", "col"),
            P("depth", "col", None),
        ),
        check_vma=False,
    )
```

```python
import functools

import jax
import jax.numpy as jnp
from jax import lax
from jax.experimental import pallas as pl
from jax.experimental.pallas import tpu as pltpu
from jax.sharding import PartitionSpec as P

STREAMS = 4
RING = 4
BRICKS = 16
COLS = 8
LANES = 128
ORDER = ((0, 0), (0, 1), (0, 2), (0, 3), (1, 0), (1, 1), (1, 2), (1, 3), (2, 0), (2, 1), (2, 2), (2, 3),
         (3, 0), (4, 0), (3, 1), (4, 1), (3, 2), (4, 2), (3, 3), (4, 3))
F32 = jnp.float32
BF16 = jnp.bfloat16
NT = (((1,), (1,)), ((), ()))
TN = (((0,), (0,)), ((), ()))
NN = (((1,), (0,)), ((), ()))


def mm(a, b, dims):
    return lax.dot_general(a, b, dims, preferred_element_type=F32)


def halves(x):
    high = x.astype(BF16)
    return high, (x - high.astype(F32)).astype(BF16)


def running(x, reverse):
    rows = x.shape[0]
    row = lax.broadcasted_iota(jnp.int32, x.shape, 0)
    total = x
    hop = 1
    while hop < rows:
        moved = pltpu.roll(total, rows - hop if reverse else hop, 0)
        total = total + jnp.where(row < rows - hop if reverse else row >= hop, moved, 0.0)
        hop *= 2
    edge = row < rows - 1 if reverse else row >= 1
    return jnp.where(edge, pltpu.roll(total, rows - 1 if reverse else 1, 0), 0.0)


def body(f_hbm, cnt_hbm, step_hbm, tgt_hbm, win_hbm, wden_hbm, wout_hbm,
         res_hbm, dens_hbm, gin_hbm, gout_hbm,
         cnt_ref, step_ref, win_ref, wden_ref, wout_ref, dens_ref, gin_ref, gout_ref, wint_ref, wcol_ref, f_ref, hid_ref, hbar_ref, p_ref, ps_ref, acc_ref, recv1_ref, recv2_ref, r_ref, prod_ref, tgt_ref,
         t_all, e_all, own_all, ecol_ref, keep_ref, v_ref, dpre_ref, gt_ref, gd_ref,
         gi_ref, go_ref, gi_recv, gr_ref, gr_recv, go_pair, go_sum, go_recv,
         in_sem, f_sem, tgt_sem, out_sem, s_sem, r_sem, ts_sem, tr_sem, os_sem, or_sem, gs_sem, gr_sem):
    smp, ray = f_ref.shape[1], f_ref.shape[2]
    hid, width = wout_ref.shape
    part_rays = ray // 2
    half_rays = part_rays // 2
    half_width = width // 2
    parts = [(rp, cp) for rp in range(2) for cp in range(2)]
    slab = gout_ref.shape[0]
    me = lax.axis_index("depth")
    col = lax.axis_index("col")
    y, z = me % RING, me // RING
    bits = ((y // 2 + y % 2) % 2, y // 2, (z // 2 + z % 2) % 2, z // 2)

    def moved(at, low, high):
        if low and high:
            return (at + 2) % RING
        return RING - 1 - at if high else at + 1 - 2 * (at % 2) if low else at

    def other(*dims):
        return (moved(z, 2 in dims, 3 in dims) * RING
                + moved(y, 0 in dims, 1 in dims))

    def spot(rp, cp, flipped=()):
        d = 2 * rp + cp
        block = 0
        for e in range(4):
            if e != d:
                block = block * 2 + (1 - bits[e] if e in flipped else bits[e])
        return d, bits[d], block

    mesh_id = pl.DeviceIdType.MESH

    weights = [
        pltpu.make_async_copy(src, dst, in_sem.at[i])
        for i, (src, dst) in enumerate((
            (win_hbm, win_ref), (wden_hbm, wden_ref), (cnt_hbm, cnt_ref), (step_hbm, step_ref),
            (wout_hbm, wout_ref)))
    ]

    def fetch(s):
        return pltpu.make_async_copy(f_hbm.at[:, pl.ds(s * ray, ray)], f_ref.at[s], f_sem.at[s])

    def fetch_target(s, rp, cp):
        _, half, block = spot(rp, cp)
        return pltpu.make_async_copy(
            tgt_hbm.at[s, rp, half, block, :, pl.ds(cp * half_width, half_width)],
            tgt_ref.at[s, rp, cp], tgt_sem.at[0])

    weights[0].start()
    fetch(0).start()
    for copy in weights[1:]:
        copy.start()

    barrier = pltpu.get_barrier_semaphore()

    def greet_depth(j, _):
        pl.semaphore_signal(barrier, inc=1, device_id={"depth": (me + j) % BRICKS}, device_id_type=mesh_id)
        return 0

    def greet_col(j, _):
        pl.semaphore_signal(barrier, inc=1, device_id={"col": (col + j) % COLS}, device_id_type=mesh_id)
        return 0

    lax.fori_loop(1, BRICKS, greet_depth, 0)
    lax.fori_loop(1, COLS, greet_col, 0)

    for s in range(1, STREAMS):
        fetch(s).start()
    for s in range(STREAMS):
        for rp, cp in parts:
            fetch_target(s, rp, cp).start()

    def arrived(ref, sem):
        pltpu.make_async_copy(ref, ref, sem).wait()

    def to_depth(src, dst, send, recv, who):
        return pltpu.make_async_remote_copy(
            src_ref=src, dst_ref=dst, send_sem=send, recv_sem=recv,
            device_id={"depth": who}, device_id_type=mesh_id)

    def spread_start(row, send, recv):
        def one(j, _):
            to_depth(row, row, send, recv, (me + j) % BRICKS).start()
            return 0
        lax.fori_loop(1, BRICKS, one, 0)

    def hops(stage, s, rp, cp):
        d, half, block = spot(rp, cp)

        def hop(src, dst, *dims):
            return to_depth(src, dst, s_sem.at[stage], r_sem.at[stage, s], other(*dims))

        if stage == 0:
            return [hop(p_ref.at[s, cp, rp, 1 - half], recv1_ref.at[s, rp, cp], d)]
        if stage == 3:
            ref = r_ref.at[s, cp, rp, half]
            return [hop(ref, ref, d)]
        out = []
        rest = [e for e in range(4) if e != d]
        for k in (7, 6, 5, 3, 4, 2, 1):
            dims = [e for i, e in enumerate(rest) if k // 2 ** i % 2]
            if stage == 1:
                out.append(hop(acc_ref.at[s, rp, cp, spot(rp, cp, dims)[2]],
                               recv2_ref.at[s, rp, cp, k - 1], *dims))
            else:
                ref = r_ref.at[s, cp, rp, half, block]
                out.append(hop(ref, ref, *dims))
        return out

    def send(stage, s, rp, cp):
        for copy in hops(stage, s, rp, cp):
            copy.start()

    def got_all(stage, s):
        ref = recv1_ref if stage in (0, 3) else recv2_ref
        arrived(ref.at[s], r_sem.at[stage, s])


    def forward(s):
        if s == 0:
            weights[0].wait()
            wint_ref[...] = win_ref[...].astype(F32).T.astype(BF16)
            for copy in weights[1:4]:
                copy.wait()
            wcol_ref[...] = jnp.broadcast_to(wden_ref[...].astype(F32), (LANES, hid)).T
        fetch(s).wait()
        place = lax.broadcasted_iota(jnp.int32, (smp, ray), 0)
        sig = jnp.zeros((smp, ray), F32)
        for i in range(smp):
            pre = mm(wint_ref[...], f_ref[s, i], NT)
            h = jnp.maximum(pre, 0.0).astype(BF16)
            hid_ref[s, i] = h
            dense = jnp.sum(h.astype(F32) * jnp.concatenate([wcol_ref[...]] * (ray // LANES), 1), 0, keepdims=True)
            sig = jnp.where(place == i, dense, sig)
        here = pl.ds(s * ray, ray)
        row = lax.broadcasted_iota(jnp.int32, (smp, ray), 0)
        gate = jnp.where(row < cnt_ref[:, here], jnp.broadcast_to(step_ref[:, here], (smp, ray)), 0.0)
        soft = jnp.maximum(sig, 0.0) + jnp.log1p(jnp.exp(-jnp.abs(sig)))
        tau = soft * gate
        inner = running(tau, False)
        t_all[s, me] = (inner + tau)[smp - 1:smp]
        if s == 0:
            pl.semaphore_wait(barrier, BRICKS - 1 + COLS - 1)
        spread_start(t_all.at[s, me], ts_sem.at[0], tr_sem.at[s])
        keep = jnp.exp(-tau)
        light = jnp.exp(-inner)
        lw = light * (1.0 - keep)
        keep_ref[s, 0] = lw
        keep_ref[s, 1] = light * keep
        keep_ref[s, 2] = sig
        keep_ref[s, 3] = gate

    def weigh(s):
        lw = keep_ref[s, 0]
        for t in range(0, hid, 32):
            total = None
            for i in range(smp):
                term = lw[i:i + 1] * hid_ref[s, i, t:t + 32].astype(F32)
                total = term if i == 0 else total + term
            hbar_ref[s, t:t + 32] = total
        if s == 0:
            weights[4].wait()
        high, low = halves(hbar_ref[s])
        value = mm(high, wout_ref[...], TN) + mm(low, wout_ref[...], TN)
        for cp in range(2):
            p_ref[s, cp] = value[:, cp * half_width:(cp + 1) * half_width].reshape(p_ref.shape[2:])

    def reduce_near(s):
        arrived(t_all.at[s, pl.ds(0, BRICKS - 1)], tr_sem.at[s])
        before = jnp.zeros((1, ray), F32)
        for b in range(BRICKS):
            e_all[s, b] = jnp.exp(-before)
            before = before + t_all[s, b]
        row = lax.broadcasted_iota(jnp.int32, (smp, ray), 0)
        table = jnp.broadcast_to(e_all[s, me], (smp, ray))
        for d in range(4):
            table = jnp.where(row == d + 1, jnp.broadcast_to(e_all[s, other(d)], (smp, ray)), table)
        ecol_ref[s] = table.T.reshape(2, 2, half_rays, smp)
        got_all(0, s)
        for rp, cp in parts:
            d, half, _ = spot(rp, cp)
            e = ecol_ref[s, rp, half]
            own = e[:, :1] * p_ref[s, cp, rp, half].reshape(half_rays, half_width)
            got = e[:, d + 1:d + 2] * recv1_ref[s, rp, cp].reshape(half_rays, half_width)
            ps_ref[s, rp, cp, 0] = own
            ps_ref[s, rp, cp, 1] = got
            acc_ref[s, rp, cp] = (own + got).reshape(acc_ref.shape[3:])
            send(1, s, rp, cp)

    def reduce_far(s):
        if s == 0:
            arrived(tgt_ref, tgt_sem.at[0])
        got_all(1, s)
        for rp, cp in parts:
            _, half, block = spot(rp, cp)
            total = acc_ref[s, rp, cp, block] - tgt_ref[s, rp, cp]
            for k in range(7):
                total = total + recv2_ref[s, rp, cp, k]
            r_ref[s, cp, rp, half, block] = total
            send(2, s, rp, cp)

    def gather_far(s):
        got_all(2, s)
        for rp, cp in parts:
            send(3, s, rp, cp)
        for i, (rp, cp) in enumerate(parts):
            r = r_ref[s, cp, rp, spot(rp, cp)[1]].reshape(half_rays, half_width)
            for j in range(2):
                prod_ref[pl.ds((2 * i + j) * half_rays, half_rays)] = ps_ref[s, rp, cp, j] * r
        high, low = halves(prod_ref[...])
        ones = jnp.ones((smp, half_width), BF16)
        own_all[s, me] = (mm(ones, high, NT) + mm(ones, low, NT))[:1]
        spread_start(own_all.at[s, me], os_sem.at[0], or_sem.at[s])

    def put_residual(s, cp):
        return pltpu.make_async_copy(
            r_ref.at[s, cp], res_hbm.at[s, :, :, :, :, pl.ds(cp * half_width, half_width)], out_sem.at[0])

    def gather_near(s):
        got_all(3, s)
        for cp in range(2):
            put_residual(s, cp).start()

    def emissions(s):
        gather_near(s)
        b_high, b_low = halves(hbar_ref[s] * e_all[s, me])
        v = None
        out = []
        for cp in range(2):
            r_high, r_low = halves(r_ref[s, cp].reshape(ray, half_width))
            w = wout_ref[:, cp * half_width:(cp + 1) * half_width]
            term = mm(w, r_high, NT) + mm(w, r_low, NT)
            v = term if cp == 0 else v + term
            out.append(mm(b_high, r_high, NN) + mm(b_low, r_high, NN))
        v_ref[s] = v
        out = jnp.concatenate(out, 1)
        for c in range(COLS):
            mine = out[c * slab:(c + 1) * slab]
            go_ref[c % 2, c // 2] = mine if s == 0 else go_ref[c % 2, c // 2] + mine
        if s == STREAMS - 1:
            pair_copy.start()

        row = lax.broadcasted_iota(jnp.int32, (smp, LANES), 0)
        for at in range(0, ray, LANES):
            here = slice(at, at + LANES)
            v = v_ref[s, :, here]
            em = jnp.zeros((smp, LANES), F32)
            for i in range(smp):
                e = jnp.sum(v * hid_ref[s, i, :, here].astype(F32), 0, keepdims=True)
                em = jnp.where(row == i, e, em)
            keep_ref[s, 4, :, here] = em

    def later_bricks(s):
        arrived(own_all.at[s, pl.ds(0, BRICKS - 1)], or_sem.at[s])
        side = lax.broadcasted_iota(jnp.int32, (1, part_rays), 1) // half_rays
        out = []
        for rp in range(2):
            whole = jnp.zeros((1, part_rays), F32)
            for cp in range(2):
                d = 2 * rp + cp
                totals = [jnp.zeros((1, part_rays), F32) for _ in range(2)]
                for source in range(BRICKS):
                    at = (source % RING, source // RING)
                    code = (at[0] ^ at[0] // 2) + RING * (at[1] ^ at[1] // 2)
                    mate = (moved(at[1], d == 2, d == 3) * RING
                            + moved(at[0], d == 0, d == 1))
                    term = own_all[s, source][:, d * part_rays:(d + 1) * part_rays]
                    brick = jnp.where(side == 0, source, mate)
                    half = code >> d & 1
                    totals[half] = totals[half] + jnp.where(brick > me, term, 0.0)
                totals = [t + pltpu.roll(t, half_rays, 1) for t in totals]
                whole = whole + jnp.where(side == 0, totals[0], totals[1])
            out.append(whole)
        return jnp.concatenate(out, 1)

    def gradients(s):
        e = jnp.broadcast_to(e_all[s, me], (smp, ray))
        em = keep_ref[s, 4]
        wgt = keep_ref[s, 0] * e
        later = running(wgt * em, True) + later_bricks(s)
        dens = (keep_ref[s, 1] * e * em - later) * keep_ref[s, 3]
        dens_ref[:, pl.ds(s * ray, ray)] = dens
        dsig = dens / (1.0 + jnp.exp(-keep_ref[s, 2]))
        for at in range(0, ray, LANES):
            here = slice(at, at + LANES)
            for t in range(0, hid, 64):
                down = slice(t, t + 64)
                v = v_ref[s, down, here]
                wden = wcol_ref[down]
                for i in range(smp):
                    dh = wgt[i:i + 1, here] * v + dsig[i:i + 1, here] * wden
                    dpre_ref[down, i * ray + at:i * ray + at + LANES] = jnp.where(
                        hid_ref[s, i, down, here] > 0, dh.astype(BF16), jnp.zeros((), BF16))
        g_in = mm(dpre_ref[...], f_ref[s].reshape(smp * ray, -1), NN)
        gt_ref[...] = g_in if s == 0 else gt_ref[...] + g_in
        d_high, d_low = halves(dsig)
        stacked = jnp.concatenate([d_high.astype(F32), d_low.astype(F32)], 0)
        row = lax.broadcasted_iota(jnp.int32, stacked.shape, 0)
        g_den = jnp.zeros((hid, 2 * smp), F32)
        for i in range(smp):
            g_den = g_den + mm(hid_ref[s, i], jnp.where(row % smp == i, stacked, 0.0).astype(BF16), NT)
        gd_ref[...] = g_den if s == 0 else gd_ref[...] + g_den
        if s == STREAMS - 1:
            turned = gt_ref[...].T
            den = gd_ref[...].T
            gr_ref[...] = jnp.sum(den, 0, keepdims=True)
            gi_ref[...] = turned.reshape(gi_ref.shape)

    x, core = col // 2, col % 2

    def to_col(src, dst, send, recv, who):
        return pltpu.make_async_remote_copy(
            src_ref=src, dst_ref=dst, send_sem=send, recv_sem=recv,
            device_id={"col": who}, device_id_type=mesh_id)

    pair_copy = to_col(go_ref.at[1 - core], go_pair, gs_sem.at[0], gr_sem.at[0], x * 2 + 1 - core)

    def share_out():
        pair_copy.wait_recv()
        go_sum[...] = go_ref[core] + go_pair[...]
        for j in (2, 1, 3):
            to = (x + j) % RING
            to_col(go_sum.at[to], go_recv.at[j - 1], gs_sem.at[1], gr_sem.at[1], to * 2 + core).start()

    def share_in(j, _):
        to = (col + j) % COLS
        to_col(gi_ref.at[to], gi_recv.at[j - 1], gs_sem.at[2], gr_sem.at[2], to).start()
        to_col(gr_ref, gr_recv.at[j - 1], gs_sem.at[3], gr_sem.at[3], to).start()
        return 0

    for s in range(STREAMS):
        forward(s)
        weigh(s)
        for rp, cp in parts:
            send(0, s, rp, cp)
    for step, s in ORDER:
        (reduce_near, reduce_far, gather_far, emissions, gradients)[step](s)
    lax.fori_loop(1, COLS, share_in, 0)
    share_out()
    dens_copy = pltpu.make_async_copy(dens_ref, dens_hbm, out_sem.at[1])
    dens_copy.start()
    arrived(go_recv, gr_sem.at[1])
    total = go_sum[x]
    for j in range(RING - 1):
        total = total + go_recv[j]
    gout_ref[...] = total
    gout_copy = pltpu.make_async_copy(gout_ref, gout_hbm, out_sem.at[2])
    gout_copy.start()
    arrived(recv1_ref, s_sem.at[0])
    arrived(recv2_ref, s_sem.at[1])
    arrived(recv2_ref, s_sem.at[2])
    arrived(recv1_ref, s_sem.at[3])
    arrived(t_all.at[:, pl.ds(0, BRICKS - 1)], ts_sem.at[0])
    arrived(own_all.at[:, pl.ds(0, BRICKS - 1)], os_sem.at[0])
    pair_copy.wait_send()
    arrived(go_recv, gs_sem.at[1])
    arrived(r_ref, out_sem.at[0])
    dens_copy.wait()
    arrived(gi_recv, gr_sem.at[2])
    total = gi_ref[col]
    for j in range(COLS - 1):
        total = total + gi_recv[j]
    gin_ref[:slab] = total
    arrived(gr_recv, gr_sem.at[3])
    total = gr_ref[...]
    for j in range(COLS - 1):
        total = total + gr_recv[j]
    gin_ref[slab:] = jnp.broadcast_to(total, (smp, hid))
    gin_copy = pltpu.make_async_copy(gin_ref, gin_hbm, out_sem.at[3])
    gin_copy.start()
    arrived(gi_recv, gs_sem.at[2])
    arrived(gr_recv, gs_sem.at[3])
    gout_copy.wait()
    gin_copy.wait()


def finish(res_in, dens_in, gin_in, gout_in, res_hbm, dens_hbm, gin_hbm, gden_hbm, gout_hbm,
           held, dens_ref, gin_ref, gout_ref, gden_ref, in_sem, out_sem):
    parts = res_in.shape[0]
    slab = gin_hbm.shape[0]
    take = [pltpu.make_async_copy(src, dst, in_sem.at[i]) for i, (src, dst) in enumerate(
        [(gin_in, gin_ref), (dens_in, dens_ref), (gout_in, gout_ref)]
        + [(res_in.at[i], held.at[i]) for i in range(parts)])]
    put = [pltpu.make_async_copy(src, dst, out_sem.at[i]) for i, (src, dst) in enumerate(
        [(gin_ref.at[pl.ds(0, slab)], gin_hbm), (dens_ref, dens_hbm), (gout_ref, gout_hbm)]
        + [(held.at[i], res_hbm.at[i]) for i in range(parts)] + [(gden_ref, gden_hbm)])]
    for copy in take:
        copy.start()
    for got, gone in zip(take, put):
        got.wait()
        gone.start()
    den = gin_ref[slab:slab + 1]
    col = lax.axis_index("col")
    mine = den[:, :slab]
    for c in range(1, COLS):
        mine = jnp.where(col == c, den[:, c * slab:(c + 1) * slab], mine)
    gden_ref[...] = mine
    put[-1].start()
    for copy in put:
        copy.wait()


def per_device(features, counts, steps, target, w_in, w_density, w_out):
    _, smp, nray, din = features.shape
    hid, width = w_out.shape[1:]
    ray = nray // STREAMS
    half_rays = ray // 4
    half_width = width // 2
    block = half_rays // 8
    slab = din // COLS
    hbm = pl.BlockSpec(memory_space=pl.ANY)
    dma = pltpu.SemaphoreType.DMA
    split = (STREAMS, 2, 2, 8, block, width)
    quads = (STREAMS, 2, 2)
    scratch = [
        pltpu.VMEM((1, nray), jnp.int32),
        pltpu.VMEM((1, nray), F32),
        pltpu.VMEM((din, hid), BF16),
        pltpu.VMEM((1, hid), BF16),
        pltpu.VMEM((hid, width), BF16),
        pltpu.VMEM((smp, nray), F32),
        pltpu.VMEM((slab + smp, hid), F32),
        pltpu.VMEM((slab, width), F32),
        pltpu.VMEM((hid, din), BF16),
        pltpu.VMEM((hid, LANES), F32),
        pltpu.VMEM((STREAMS, smp, ray, din), BF16),
        pltpu.VMEM((STREAMS, smp, hid, ray), BF16),
        pltpu.VMEM((STREAMS, hid, ray), F32),
        pltpu.VMEM((*quads, 2, 8, block, half_width), F32),
        pltpu.VMEM((*quads, 2, half_rays, half_width), F32),
        pltpu.VMEM((*quads, 8, block, half_width), F32),
        pltpu.VMEM((*quads, 8, block, half_width), F32),
        pltpu.VMEM((*quads, 7, block, half_width), F32),
        pltpu.VMEM((*quads, 2, 8, block, half_width), F32),
        pltpu.VMEM((2 * ray, half_width), F32),
        pltpu.VMEM((*quads, block, half_width), F32),
        pltpu.VMEM((STREAMS, BRICKS, 1, ray), F32),
        pltpu.VMEM((STREAMS, BRICKS, 1, ray), F32),
        pltpu.VMEM((STREAMS, BRICKS, 1, 2 * ray), F32),
        pltpu.VMEM((STREAMS, 2, 2, half_rays, smp), F32),
        pltpu.VMEM((STREAMS, 5, smp, ray), F32),
        pltpu.VMEM((STREAMS, hid, ray), F32),
        pltpu.VMEM((hid, smp * ray), BF16),
        pltpu.VMEM((hid, din), F32),
        pltpu.VMEM((hid, 2 * smp), F32),
        pltpu.VMEM((COLS, slab, hid), F32),
        pltpu.VMEM((2, RING, slab, width), F32),
        pltpu.VMEM((COLS - 1, slab, hid), F32),
        pltpu.VMEM((1, hid), F32),
        pltpu.VMEM((COLS - 1, 1, hid), F32),
        pltpu.VMEM((RING, slab, width), F32),
        pltpu.VMEM((RING, slab, width), F32),
        pltpu.VMEM((RING - 1, slab, width), F32),
        dma((5,)), dma((STREAMS,)), dma((1,)), dma((4,)),
        dma((4,)), dma((4, STREAMS)),
        dma((1,)), dma((STREAMS,)), dma((1,)), dma((STREAMS,)),
        dma((4,)), dma((4,)),
    ]
    residual, dens, g_in, g_out = pl.pallas_call(
        body,
        out_shape=(
            jax.ShapeDtypeStruct(split, F32),
            jax.ShapeDtypeStruct((smp, nray), F32),
            jax.ShapeDtypeStruct((slab + smp, hid), F32),
            jax.ShapeDtypeStruct((slab, width), F32),
        ),
        in_specs=[hbm] * 7,
        out_specs=(hbm,) * 4,
        scratch_shapes=scratch,
        compiler_params=pltpu.CompilerParams(
            collective_id=0, has_side_effects=True, vmem_limit_bytes=60 * 1024 * 1024),
        name="brick_step",
    )(features[0], counts, steps, target.reshape(split), w_in[0], w_density, w_out[0])
    residual, dens, g_in, g_den, g_out = pl.pallas_call(
        finish,
        out_shape=(
            jax.ShapeDtypeStruct((8, nray // 8, width), F32),
            jax.ShapeDtypeStruct((smp, nray), F32),
            jax.ShapeDtypeStruct((slab, hid), F32),
            jax.ShapeDtypeStruct((1, slab), F32),
            jax.ShapeDtypeStruct((slab, width), F32),
        ),
        in_specs=[hbm] * 4,
        out_specs=(hbm,) * 5,
        scratch_shapes=[
            pltpu.VMEM((8, nray // 8, width), F32),
            pltpu.VMEM((smp, nray), F32),
            pltpu.VMEM((slab + smp, hid), F32),
            pltpu.VMEM((slab, width), F32),
            pltpu.VMEM((1, slab), F32),
            dma((11,)), dma((12,)),
        ],
        name="brick_finish",
    )(residual.reshape(8, nray // 8, width), dens, g_in, g_out)
    return residual.reshape(nray, width), dens[None], g_in[None], g_den, g_out[None]


def solution(mesh):
    return jax.shard_map(
        per_device,
        mesh=mesh,
        in_specs=(
            P("depth", None, "col", None),
            P("depth", "col"),
            P("depth", "col"),
            P("col", None),
            P("depth", None, None),
            P("depth", None),
            P("depth", None, None),
        ),
        out_specs=(
            P("col", None),
            P("depth", None, "col"),
            P("depth", "col", None),
            P("depth", "col"),
            P("depth", "col", None),
        ),
        check_vma=False,
    )
```

```python
import functools

import jax
import jax.numpy as jnp
from jax import lax
from jax.experimental import pallas as pl
from jax.experimental.pallas import tpu as pltpu
from jax.sharding import PartitionSpec as P

STREAMS = 4
RING = 4
BRICKS = 16
COLS = 8
LANES = 128
ORDER = ((0, 0), (0, 1), (0, 2), (0, 3), (1, 0), (1, 1), (1, 2), (1, 3), (2, 0), (2, 1), (2, 2), (2, 3),
         (3, 0), (4, 0), (3, 1), (4, 1), (3, 2), (4, 2), (3, 3), (4, 3))
F32 = jnp.float32
BF16 = jnp.bfloat16
NT = (((1,), (1,)), ((), ()))
TN = (((0,), (0,)), ((), ()))
NN = (((1,), (0,)), ((), ()))


def mm(a, b, dims):
    return lax.dot_general(a, b, dims, preferred_element_type=F32)


def halves(x):
    high = x.astype(BF16)
    return high, (x - high.astype(F32)).astype(BF16)


def running(x, reverse):
    rows = x.shape[0]
    row = lax.broadcasted_iota(jnp.int32, x.shape, 0)
    total = x
    hop = 1
    while hop < rows:
        moved = pltpu.roll(total, rows - hop if reverse else hop, 0)
        total = total + jnp.where(row < rows - hop if reverse else row >= hop, moved, 0.0)
        hop *= 2
    edge = row < rows - 1 if reverse else row >= 1
    return jnp.where(edge, pltpu.roll(total, rows - 1 if reverse else 1, 0), 0.0)


def body(f_hbm, cnt_hbm, step_hbm, tgt_hbm, win_hbm, wden_hbm, wout_hbm,
         res_hbm, dens_hbm, gin_hbm, gout_hbm,
         cnt_ref, step_ref, win_ref, wden_ref, wout_ref, dens_ref, gin_ref, gout_ref, wint_ref, wcol_ref, f_ref, hid_ref, hbar_ref, p_ref, ps_ref, acc_ref, recv1_ref, recv2_ref, r_ref, prod_ref, tgt_ref,
         t_all, e_all, own_all, ecol_ref, keep_ref, v_ref, dpre_ref, gt_ref, gd_ref,
         gi_ref, go_ref, gi_recv, gr_ref, gr_recv, go_pair, go_sum, go_recv,
         in_sem, f_sem, tgt_sem, out_sem, s_sem, r_sem, ts_sem, tr_sem, os_sem, or_sem, gs_sem, gr_sem):
    smp, ray = f_ref.shape[1], f_ref.shape[2]
    hid, width = wout_ref.shape
    part_rays = ray // 2
    half_rays = part_rays // 2
    half_width = width // 2
    parts = [(rp, cp) for rp in range(2) for cp in range(2)]
    slab = gout_ref.shape[0]
    me = lax.axis_index("depth")
    col = lax.axis_index("col")
    y, z = me % RING, me // RING
    bits = ((y // 2 + y % 2) % 2, y // 2, (z // 2 + z % 2) % 2, z // 2)

    def moved(at, low, high):
        if low and high:
            return (at + 2) % RING
        return RING - 1 - at if high else at + 1 - 2 * (at % 2) if low else at

    def other(*dims):
        return (moved(z, 2 in dims, 3 in dims) * RING
                + moved(y, 0 in dims, 1 in dims))

    def spot(rp, cp, flipped=()):
        d = 2 * rp + cp
        block = 0
        for e in range(4):
            if e != d:
                block = block * 2 + (1 - bits[e] if e in flipped else bits[e])
        return d, bits[d], block

    mesh_id = pl.DeviceIdType.MESH

    weights = [
        pltpu.make_async_copy(src, dst, in_sem.at[i])
        for i, (src, dst) in enumerate((
            (win_hbm, win_ref), (wden_hbm, wden_ref), (cnt_hbm, cnt_ref), (step_hbm, step_ref),
            (wout_hbm, wout_ref)))
    ]

    def fetch(s):
        return pltpu.make_async_copy(f_hbm.at[:, pl.ds(s * ray, ray)], f_ref.at[s], f_sem.at[s])

    def fetch_target(s, rp, cp):
        _, half, block = spot(rp, cp)
        return pltpu.make_async_copy(
            tgt_hbm.at[s, rp, half, block, :, pl.ds(cp * half_width, half_width)],
            tgt_ref.at[s, rp, cp], tgt_sem.at[0])

    weights[0].start()
    fetch(0).start()
    for copy in weights[1:]:
        copy.start()

    barrier = pltpu.get_barrier_semaphore()

    def greet_depth(j, _):
        pl.semaphore_signal(barrier, inc=1, device_id={"depth": (me + j) % BRICKS}, device_id_type=mesh_id)
        return 0

    def greet_col(j, _):
        pl.semaphore_signal(barrier, inc=1, device_id={"col": (col + j) % COLS}, device_id_type=mesh_id)
        return 0

    lax.fori_loop(1, BRICKS, greet_depth, 0)
    lax.fori_loop(1, COLS, greet_col, 0)

    for s in range(1, STREAMS):
        fetch(s).start()
    for s in range(STREAMS):
        for rp, cp in parts:
            fetch_target(s, rp, cp).start()

    def arrived(ref, sem):
        pltpu.make_async_copy(ref, ref, sem).wait()

    def to_depth(src, dst, send, recv, who):
        return pltpu.make_async_remote_copy(
            src_ref=src, dst_ref=dst, send_sem=send, recv_sem=recv,
            device_id={"depth": who}, device_id_type=mesh_id)

    def spread_start(row, send, recv):
        def one(j, _):
            to_depth(row, row, send, recv, (me + j) % BRICKS).start()
            return 0
        lax.fori_loop(1, BRICKS, one, 0)

    def hops(stage, s, rp, cp):
        d, half, block = spot(rp, cp)

        def hop(src, dst, *dims):
            return to_depth(src, dst, s_sem.at[stage], r_sem.at[stage, s], other(*dims))

        if stage == 0:
            return [hop(p_ref.at[s, cp, rp, 1 - half], recv1_ref.at[s, rp, cp], d)]
        if stage == 3:
            ref = r_ref.at[s, cp, rp, half]
            return [hop(ref, ref, d)]
        out = []
        rest = [e for e in range(4) if e != d]
        for k in (7, 6, 5, 3, 4, 2, 1):
            dims = [e for i, e in enumerate(rest) if k // 2 ** i % 2]
            if stage == 1:
                out.append(hop(acc_ref.at[s, rp, cp, spot(rp, cp, dims)[2]],
                               recv2_ref.at[s, rp, cp, k - 1], *dims))
            else:
                ref = r_ref.at[s, cp, rp, half, block]
                out.append(hop(ref, ref, *dims))
        return out

    def send(stage, s, rp, cp):
        for copy in hops(stage, s, rp, cp):
            copy.start()

    def send_mixed(stage, s):
        for group in zip(*(hops(stage, s, rp, cp) for rp, cp in parts)):
            for copy in group:
                copy.start()

    def got_all(stage, s):
        ref = recv1_ref if stage in (0, 3) else recv2_ref
        arrived(ref.at[s], r_sem.at[stage, s])


    def forward(s):
        if s == 0:
            weights[0].wait()
            wint_ref[...] = win_ref[...].astype(F32).T.astype(BF16)
            for copy in weights[1:4]:
                copy.wait()
            wcol_ref[...] = jnp.broadcast_to(wden_ref[...].astype(F32), (LANES, hid)).T
        fetch(s).wait()
        place = lax.broadcasted_iota(jnp.int32, (smp, ray), 0)
        sig = jnp.zeros((smp, ray), F32)
        for i in range(smp):
            pre = mm(wint_ref[...], f_ref[s, i], NT)
            h = jnp.maximum(pre, 0.0).astype(BF16)
            hid_ref[s, i] = h
            dense = jnp.sum(h.astype(F32) * jnp.concatenate([wcol_ref[...]] * (ray // LANES), 1), 0, keepdims=True)
            sig = jnp.where(place == i, dense, sig)
        here = pl.ds(s * ray, ray)
        row = lax.broadcasted_iota(jnp.int32, (smp, ray), 0)
        gate = jnp.where(row < cnt_ref[:, here], jnp.broadcast_to(step_ref[:, here], (smp, ray)), 0.0)
        soft = jnp.maximum(sig, 0.0) + jnp.log1p(jnp.exp(-jnp.abs(sig)))
        tau = soft * gate
        inner = running(tau, False)
        t_all[s, me] = (inner + tau)[smp - 1:smp]
        if s == 0:
            pl.semaphore_wait(barrier, BRICKS - 1 + COLS - 1)
        spread_start(t_all.at[s, me], ts_sem.at[0], tr_sem.at[s])
        keep = jnp.exp(-tau)
        light = jnp.exp(-inner)
        lw = light * (1.0 - keep)
        keep_ref[s, 0] = lw
        keep_ref[s, 1] = light * keep
        keep_ref[s, 2] = sig
        keep_ref[s, 3] = gate

    def weigh(s):
        lw = keep_ref[s, 0]
        for t in range(0, hid, 32):
            total = None
            for i in range(smp):
                term = lw[i:i + 1] * hid_ref[s, i, t:t + 32].astype(F32)
                total = term if i == 0 else total + term
            hbar_ref[s, t:t + 32] = total
        if s == 0:
            weights[4].wait()
        high, low = halves(hbar_ref[s])
        value = mm(high, wout_ref[...], TN) + mm(low, wout_ref[...], TN)
        for cp in range(2):
            p_ref[s, cp] = value[:, cp * half_width:(cp + 1) * half_width].reshape(p_ref.shape[2:])

    def reduce_near(s):
        arrived(t_all.at[s, pl.ds(0, BRICKS - 1)], tr_sem.at[s])
        before = jnp.zeros((1, ray), F32)
        for b in range(BRICKS):
            e_all[s, b] = jnp.exp(-before)
            before = before + t_all[s, b]
        row = lax.broadcasted_iota(jnp.int32, (smp, ray), 0)
        table = jnp.broadcast_to(e_all[s, me], (smp, ray))
        for d in range(4):
            table = jnp.where(row == d + 1, jnp.broadcast_to(e_all[s, other(d)], (smp, ray)), table)
        ecol_ref[s] = table.T.reshape(2, 2, half_rays, smp)
        got_all(0, s)
        for rp, cp in parts:
            d, half, _ = spot(rp, cp)
            e = ecol_ref[s, rp, half]
            own = e[:, :1] * p_ref[s, cp, rp, half].reshape(half_rays, half_width)
            got = e[:, d + 1:d + 2] * recv1_ref[s, rp, cp].reshape(half_rays, half_width)
            ps_ref[s, rp, cp, 0] = own
            ps_ref[s, rp, cp, 1] = got
            acc_ref[s, rp, cp] = (own + got).reshape(acc_ref.shape[3:])
        send_mixed(1, s)

    def reduce_far(s):
        if s == 0:
            arrived(tgt_ref, tgt_sem.at[0])
        got_all(1, s)
        for rp, cp in parts:
            _, half, block = spot(rp, cp)
            total = acc_ref[s, rp, cp, block] - tgt_ref[s, rp, cp]
            for k in range(7):
                total = total + recv2_ref[s, rp, cp, k]
            r_ref[s, cp, rp, half, block] = total
        send_mixed(2, s)

    def gather_far(s):
        got_all(2, s)
        for rp, cp in parts:
            send(3, s, rp, cp)
        for i, (rp, cp) in enumerate(parts):
            r = r_ref[s, cp, rp, spot(rp, cp)[1]].reshape(half_rays, half_width)
            for j in range(2):
                prod_ref[pl.ds((2 * i + j) * half_rays, half_rays)] = ps_ref[s, rp, cp, j] * r
        high, low = halves(prod_ref[...])
        ones = jnp.ones((smp, half_width), BF16)
        own_all[s, me] = (mm(ones, high, NT) + mm(ones, low, NT))[:1]
        spread_start(own_all.at[s, me], os_sem.at[0], or_sem.at[s])

    def put_residual(s, cp):
        return pltpu.make_async_copy(
            r_ref.at[s, cp], res_hbm.at[s, :, :, :, :, pl.ds(cp * half_width, half_width)], out_sem.at[0])

    def gather_near(s):
        got_all(3, s)
        for cp in range(2):
            put_residual(s, cp).start()

    def emissions(s):
        gather_near(s)
        b_high, b_low = halves(hbar_ref[s] * e_all[s, me])
        v = None
        out = []
        for cp in range(2):
            r_high, r_low = halves(r_ref[s, cp].reshape(ray, half_width))
            w = wout_ref[:, cp * half_width:(cp + 1) * half_width]
            term = mm(w, r_high, NT) + mm(w, r_low, NT)
            v = term if cp == 0 else v + term
            out.append(mm(b_high, r_high, NN) + mm(b_low, r_high, NN))
        v_ref[s] = v
        out = jnp.concatenate(out, 1)
        for c in range(COLS):
            mine = out[c * slab:(c + 1) * slab]
            go_ref[c % 2, c // 2] = mine if s == 0 else go_ref[c % 2, c // 2] + mine
        if s == STREAMS - 1:
            pair_copy.start()

        row = lax.broadcasted_iota(jnp.int32, (smp, LANES), 0)
        for at in range(0, ray, LANES):
            here = slice(at, at + LANES)
            v = v_ref[s, :, here]
            em = jnp.zeros((smp, LANES), F32)
            for i in range(smp):
                e = jnp.sum(v * hid_ref[s, i, :, here].astype(F32), 0, keepdims=True)
                em = jnp.where(row == i, e, em)
            keep_ref[s, 4, :, here] = em

    def later_bricks(s):
        arrived(own_all.at[s, pl.ds(0, BRICKS - 1)], or_sem.at[s])
        side = lax.broadcasted_iota(jnp.int32, (1, part_rays), 1) // half_rays
        out = []
        for rp in range(2):
            whole = jnp.zeros((1, part_rays), F32)
            for cp in range(2):
                d = 2 * rp + cp
                totals = [jnp.zeros((1, part_rays), F32) for _ in range(2)]
                for source in range(BRICKS):
                    at = (source % RING, source // RING)
                    code = (at[0] ^ at[0] // 2) + RING * (at[1] ^ at[1] // 2)
                    mate = (moved(at[1], d == 2, d == 3) * RING
                            + moved(at[0], d == 0, d == 1))
                    term = own_all[s, source][:, d * part_rays:(d + 1) * part_rays]
                    brick = jnp.where(side == 0, source, mate)
                    half = code >> d & 1
                    totals[half] = totals[half] + jnp.where(brick > me, term, 0.0)
                totals = [t + pltpu.roll(t, half_rays, 1) for t in totals]
                whole = whole + jnp.where(side == 0, totals[0], totals[1])
            out.append(whole)
        return jnp.concatenate(out, 1)

    def gradients(s):
        e = jnp.broadcast_to(e_all[s, me], (smp, ray))
        em = keep_ref[s, 4]
        wgt = keep_ref[s, 0] * e
        later = running(wgt * em, True) + later_bricks(s)
        dens = (keep_ref[s, 1] * e * em - later) * keep_ref[s, 3]
        dens_ref[:, pl.ds(s * ray, ray)] = dens
        dsig = dens / (1.0 + jnp.exp(-keep_ref[s, 2]))
        for at in range(0, ray, LANES):
            here = slice(at, at + LANES)
            for t in range(0, hid, 64):
                down = slice(t, t + 64)
                v = v_ref[s, down, here]
                wden = wcol_ref[down]
                for i in range(smp):
                    dh = wgt[i:i + 1, here] * v + dsig[i:i + 1, here] * wden
                    dpre_ref[down, i * ray + at:i * ray + at + LANES] = jnp.where(
                        hid_ref[s, i, down, here] > 0, dh.astype(BF16), jnp.zeros((), BF16))
        g_in = mm(dpre_ref[...], f_ref[s].reshape(smp * ray, -1), NN)
        gt_ref[...] = g_in if s == 0 else gt_ref[...] + g_in
        d_high, d_low = halves(dsig)
        stacked = jnp.concatenate([d_high.astype(F32), d_low.astype(F32)], 0)
        row = lax.broadcasted_iota(jnp.int32, stacked.shape, 0)
        g_den = jnp.zeros((hid, 2 * smp), F32)
        for i in range(smp):
            g_den = g_den + mm(hid_ref[s, i], jnp.where(row % smp == i, stacked, 0.0).astype(BF16), NT)
        gd_ref[...] = g_den if s == 0 else gd_ref[...] + g_den
        if s == STREAMS - 1:
            turned = gt_ref[...].T
            den = gd_ref[...].T
            gr_ref[...] = jnp.sum(den, 0, keepdims=True)
            gi_ref[...] = turned.reshape(gi_ref.shape)

    x, core = col // 2, col % 2

    def to_col(src, dst, send, recv, who):
        return pltpu.make_async_remote_copy(
            src_ref=src, dst_ref=dst, send_sem=send, recv_sem=recv,
            device_id={"col": who}, device_id_type=mesh_id)

    pair_copy = to_col(go_ref.at[1 - core], go_pair, gs_sem.at[0], gr_sem.at[0], x * 2 + 1 - core)

    def share_out():
        pair_copy.wait_recv()
        go_sum[...] = go_ref[core] + go_pair[...]
        for j in (2, 1, 3):
            to = (x + j) % RING
            to_col(go_sum.at[to], go_recv.at[j - 1], gs_sem.at[1], gr_sem.at[1], to * 2 + core).start()

    def share_in(j, _):
        to = (col + j) % COLS
        to_col(gi_ref.at[to], gi_recv.at[j - 1], gs_sem.at[2], gr_sem.at[2], to).start()
        to_col(gr_ref, gr_recv.at[j - 1], gs_sem.at[3], gr_sem.at[3], to).start()
        return 0

    for s in range(STREAMS):
        forward(s)
        weigh(s)
        for rp, cp in parts:
            send(0, s, rp, cp)
    for step, s in ORDER:
        (reduce_near, reduce_far, gather_far, emissions, gradients)[step](s)
    for j in (4, 3, 5, 2, 6, 1, 7):
        share_in(j, 0)
    share_out()
    dens_copy = pltpu.make_async_copy(dens_ref, dens_hbm, out_sem.at[1])
    dens_copy.start()
    arrived(go_recv, gr_sem.at[1])
    total = go_sum[x]
    for j in range(RING - 1):
        total = total + go_recv[j]
    gout_ref[...] = total
    gout_copy = pltpu.make_async_copy(gout_ref, gout_hbm, out_sem.at[2])
    gout_copy.start()
    arrived(recv1_ref, s_sem.at[0])
    arrived(recv2_ref, s_sem.at[1])
    arrived(recv2_ref, s_sem.at[2])
    arrived(recv1_ref, s_sem.at[3])
    arrived(t_all.at[:, pl.ds(0, BRICKS - 1)], ts_sem.at[0])
    arrived(own_all.at[:, pl.ds(0, BRICKS - 1)], os_sem.at[0])
    pair_copy.wait_send()
    arrived(go_recv, gs_sem.at[1])
    arrived(r_ref, out_sem.at[0])
    dens_copy.wait()
    arrived(gi_recv, gr_sem.at[2])
    total = gi_ref[col]
    for j in range(COLS - 1):
        total = total + gi_recv[j]
    gin_ref[:slab] = total
    arrived(gr_recv, gr_sem.at[3])
    total = gr_ref[...]
    for j in range(COLS - 1):
        total = total + gr_recv[j]
    gin_ref[slab:] = jnp.broadcast_to(total, (smp, hid))
    gin_copy = pltpu.make_async_copy(gin_ref, gin_hbm, out_sem.at[3])
    gin_copy.start()
    arrived(gi_recv, gs_sem.at[2])
    arrived(gr_recv, gs_sem.at[3])
    gout_copy.wait()
    gin_copy.wait()


def finish(res_in, dens_in, gin_in, gout_in, res_hbm, dens_hbm, gin_hbm, gden_hbm, gout_hbm,
           held, dens_ref, gin_ref, gout_ref, gden_ref, in_sem, out_sem):
    parts = res_in.shape[0]
    slab = gin_hbm.shape[0]
    take = [pltpu.make_async_copy(src, dst, in_sem.at[i]) for i, (src, dst) in enumerate(
        [(gin_in, gin_ref), (dens_in, dens_ref), (gout_in, gout_ref)]
        + [(res_in.at[i], held.at[i]) for i in range(parts)])]
    put = [pltpu.make_async_copy(src, dst, out_sem.at[i]) for i, (src, dst) in enumerate(
        [(gin_ref.at[pl.ds(0, slab)], gin_hbm), (dens_ref, dens_hbm), (gout_ref, gout_hbm)]
        + [(held.at[i], res_hbm.at[i]) for i in range(parts)] + [(gden_ref, gden_hbm)])]
    for copy in take:
        copy.start()
    for got, gone in zip(take, put):
        got.wait()
        gone.start()
    den = gin_ref[slab:slab + 1]
    col = lax.axis_index("col")
    mine = den[:, :slab]
    for c in range(1, COLS):
        mine = jnp.where(col == c, den[:, c * slab:(c + 1) * slab], mine)
    gden_ref[...] = mine
    put[-1].start()
    for copy in put:
        copy.wait()


def per_device(features, counts, steps, target, w_in, w_density, w_out):
    _, smp, nray, din = features.shape
    hid, width = w_out.shape[1:]
    ray = nray // STREAMS
    half_rays = ray // 4
    half_width = width // 2
    block = half_rays // 8
    slab = din // COLS
    hbm = pl.BlockSpec(memory_space=pl.ANY)
    dma = pltpu.SemaphoreType.DMA
    split = (STREAMS, 2, 2, 8, block, width)
    quads = (STREAMS, 2, 2)
    scratch = [
        pltpu.VMEM((1, nray), jnp.int32),
        pltpu.VMEM((1, nray), F32),
        pltpu.VMEM((din, hid), BF16),
        pltpu.VMEM((1, hid), BF16),
        pltpu.VMEM((hid, width), BF16),
        pltpu.VMEM((smp, nray), F32),
        pltpu.VMEM((slab + smp, hid), F32),
        pltpu.VMEM((slab, width), F32),
        pltpu.VMEM((hid, din), BF16),
        pltpu.VMEM((hid, LANES), F32),
        pltpu.VMEM((STREAMS, smp, ray, din), BF16),
        pltpu.VMEM((STREAMS, smp, hid, ray), BF16),
        pltpu.VMEM((STREAMS, hid, ray), F32),
        pltpu.VMEM((*quads, 2, 8, block, half_width), F32),
        pltpu.VMEM((*quads, 2, half_rays, half_width), F32),
        pltpu.VMEM((*quads, 8, block, half_width), F32),
        pltpu.VMEM((*quads, 8, block, half_width), F32),
        pltpu.VMEM((*quads, 7, block, half_width), F32),
        pltpu.VMEM((*quads, 2, 8, block, half_width), F32),
        pltpu.VMEM((2 * ray, half_width), F32),
        pltpu.VMEM((*quads, block, half_width), F32),
        pltpu.VMEM((STREAMS, BRICKS, 1, ray), F32),
        pltpu.VMEM((STREAMS, BRICKS, 1, ray), F32),
        pltpu.VMEM((STREAMS, BRICKS, 1, 2 * ray), F32),
        pltpu.VMEM((STREAMS, 2, 2, half_rays, smp), F32),
        pltpu.VMEM((STREAMS, 5, smp, ray), F32),
        pltpu.VMEM((STREAMS, hid, ray), F32),
        pltpu.VMEM((hid, smp * ray), BF16),
        pltpu.VMEM((hid, din), F32),
        pltpu.VMEM((hid, 2 * smp), F32),
        pltpu.VMEM((COLS, slab, hid), F32),
        pltpu.VMEM((2, RING, slab, width), F32),
        pltpu.VMEM((COLS - 1, slab, hid), F32),
        pltpu.VMEM((1, hid), F32),
        pltpu.VMEM((COLS - 1, 1, hid), F32),
        pltpu.VMEM((RING, slab, width), F32),
        pltpu.VMEM((RING, slab, width), F32),
        pltpu.VMEM((RING - 1, slab, width), F32),
        dma((5,)), dma((STREAMS,)), dma((1,)), dma((4,)),
        dma((4,)), dma((4, STREAMS)),
        dma((1,)), dma((STREAMS,)), dma((1,)), dma((STREAMS,)),
        dma((4,)), dma((4,)),
    ]
    residual, dens, g_in, g_out = pl.pallas_call(
        body,
        out_shape=(
            jax.ShapeDtypeStruct(split, F32),
            jax.ShapeDtypeStruct((smp, nray), F32),
            jax.ShapeDtypeStruct((slab + smp, hid), F32),
            jax.ShapeDtypeStruct((slab, width), F32),
        ),
        in_specs=[hbm] * 7,
        out_specs=(hbm,) * 4,
        scratch_shapes=scratch,
        compiler_params=pltpu.CompilerParams(
            collective_id=0, has_side_effects=True, vmem_limit_bytes=60 * 1024 * 1024),
        name="brick_step",
    )(features[0], counts, steps, target.reshape(split), w_in[0], w_density, w_out[0])
    residual, dens, g_in, g_den, g_out = pl.pallas_call(
        finish,
        out_shape=(
            jax.ShapeDtypeStruct((8, nray // 8, width), F32),
            jax.ShapeDtypeStruct((smp, nray), F32),
            jax.ShapeDtypeStruct((slab, hid), F32),
            jax.ShapeDtypeStruct((1, slab), F32),
            jax.ShapeDtypeStruct((slab, width), F32),
        ),
        in_specs=[hbm] * 4,
        out_specs=(hbm,) * 5,
        scratch_shapes=[
            pltpu.VMEM((8, nray // 8, width), F32),
            pltpu.VMEM((smp, nray), F32),
            pltpu.VMEM((slab + smp, hid), F32),
            pltpu.VMEM((slab, width), F32),
            pltpu.VMEM((1, slab), F32),
            dma((11,)), dma((12,)),
        ],
        name="brick_finish",
    )(residual.reshape(8, nray // 8, width), dens, g_in, g_out)
    return residual.reshape(nray, width), dens[None], g_in[None], g_den, g_out[None]


def solution(mesh):
    return jax.shard_map(
        per_device,
        mesh=mesh,
        in_specs=(
            P("depth", None, "col", None),
            P("depth", "col"),
            P("depth", "col"),
            P("col", None),
            P("depth", None, None),
            P("depth", None),
            P("depth", None, None),
        ),
        out_specs=(
            P("col", None),
            P("depth", None, "col"),
            P("depth", "col", None),
            P("depth", "col"),
            P("depth", "col", None),
        ),
        check_vma=False,
    )
```

```python
import functools

import jax
import jax.numpy as jnp
from jax import lax
from jax.experimental import pallas as pl
from jax.experimental.pallas import tpu as pltpu
from jax.sharding import PartitionSpec as P

STREAMS = 4
RING = 4
BRICKS = 16
COLS = 8
LANES = 128
ORDER = ((0, 0), (0, 1), (0, 2), (0, 3), (1, 0), (1, 1), (1, 2), (1, 3), (2, 0), (2, 1), (2, 2), (2, 3),
         (3, 0), (4, 0), (3, 1), (4, 1), (3, 2), (4, 2), (3, 3), (4, 3))
F32 = jnp.float32
BF16 = jnp.bfloat16
NT = (((1,), (1,)), ((), ()))
TN = (((0,), (0,)), ((), ()))
NN = (((1,), (0,)), ((), ()))


def mm(a, b, dims):
    return lax.dot_general(a, b, dims, preferred_element_type=F32)


def halves(x):
    high = x.astype(BF16)
    return high, (x - high.astype(F32)).astype(BF16)


def running(x, reverse):
    rows = x.shape[0]
    row = lax.broadcasted_iota(jnp.int32, x.shape, 0)
    total = x
    hop = 1
    while hop < rows:
        moved = pltpu.roll(total, rows - hop if reverse else hop, 0)
        total = total + jnp.where(row < rows - hop if reverse else row >= hop, moved, 0.0)
        hop *= 2
    edge = row < rows - 1 if reverse else row >= 1
    return jnp.where(edge, pltpu.roll(total, rows - 1 if reverse else 1, 0), 0.0)


def body(f_hbm, cnt_hbm, step_hbm, tgt_hbm, win_hbm, wden_hbm, wout_hbm,
         res_hbm, dens_hbm, gin_hbm, gout_hbm,
         cnt_ref, step_ref, win_ref, wden_ref, wout_ref, dens_ref, gin_ref, gout_ref, wint_ref, wcol_ref, f_ref, hid_ref, hbar_ref, p_ref, ps_ref, acc_ref, recv1_ref, recv2_ref, r_ref, prod_ref, tgt_ref,
         t_all, e_all, own_all, ecol_ref, keep_ref, v_ref, dpre_ref, gt_ref, gd_ref,
         gi_ref, go_ref, gi_recv, gr_ref, gr_recv, go_pair, go_sum, go_recv,
         in_sem, f_sem, tgt_sem, out_sem, s_sem, r_sem, ts_sem, tr_sem, os_sem, or_sem, gs_sem, gr_sem):
    smp, ray = f_ref.shape[1], f_ref.shape[2]
    hid, width = wout_ref.shape
    part_rays = ray // 2
    half_rays = part_rays // 2
    half_width = width // 2
    parts = [(rp, cp) for rp in range(2) for cp in range(2)]
    slab = gout_ref.shape[0]
    me = lax.axis_index("depth")
    col = lax.axis_index("col")
    y, z = me % RING, me // RING
    bits = ((y // 2 + y % 2) % 2, y // 2, (z // 2 + z % 2) % 2, z // 2)

    def moved(at, low, high):
        if low and high:
            return (at + 2) % RING
        return RING - 1 - at if high else at + 1 - 2 * (at % 2) if low else at

    def other(*dims):
        return (moved(z, 2 in dims, 3 in dims) * RING
                + moved(y, 0 in dims, 1 in dims))

    def spot(rp, cp, flipped=()):
        d = 2 * rp + cp
        block = 0
        for e in range(4):
            if e != d:
                block = block * 2 + (1 - bits[e] if e in flipped else bits[e])
        return d, bits[d], block

    mesh_id = pl.DeviceIdType.MESH

    weights = [
        pltpu.make_async_copy(src, dst, in_sem.at[i])
        for i, (src, dst) in enumerate((
            (win_hbm, win_ref), (wden_hbm, wden_ref), (cnt_hbm, cnt_ref), (step_hbm, step_ref),
            (wout_hbm, wout_ref)))
    ]

    def fetch(s):
        return pltpu.make_async_copy(f_hbm.at[:, pl.ds(s * ray, ray)], f_ref.at[s], f_sem.at[s])

    def fetch_target(s, rp, cp):
        _, half, block = spot(rp, cp)
        return pltpu.make_async_copy(
            tgt_hbm.at[s, rp, half, block, :, pl.ds(cp * half_width, half_width)],
            tgt_ref.at[s, rp, cp], tgt_sem.at[0])

    weights[0].start()
    fetch(0).start()
    for copy in weights[1:]:
        copy.start()

    barrier = pltpu.get_barrier_semaphore()

    def greet_depth(j, _):
        pl.semaphore_signal(barrier, inc=1, device_id={"depth": (me + j) % BRICKS}, device_id_type=mesh_id)
        return 0

    def greet_col(j, _):
        pl.semaphore_signal(barrier, inc=1, device_id={"col": (col + j) % COLS}, device_id_type=mesh_id)
        return 0

    lax.fori_loop(1, BRICKS, greet_depth, 0)
    lax.fori_loop(1, COLS, greet_col, 0)

    for s in range(1, STREAMS):
        fetch(s).start()
    for s in range(STREAMS):
        for rp, cp in parts:
            fetch_target(s, rp, cp).start()

    def arrived(ref, sem):
        pltpu.make_async_copy(ref, ref, sem).wait()

    def to_depth(src, dst, send, recv, who):
        return pltpu.make_async_remote_copy(
            src_ref=src, dst_ref=dst, send_sem=send, recv_sem=recv,
            device_id={"depth": who}, device_id_type=mesh_id)

    def spread_start(row, send, recv):
        def one(j, _):
            to_depth(row, row, send, recv, (me + 1 + (j + 6) % (BRICKS - 1)) % BRICKS).start()
            return 0
        lax.fori_loop(1, BRICKS, one, 0)

    def hops(stage, s, rp, cp):
        d, half, block = spot(rp, cp)

        def hop(src, dst, *dims):
            return to_depth(src, dst, s_sem.at[stage], r_sem.at[stage, s], other(*dims))

        if stage == 0:
            return [hop(p_ref.at[s, cp, rp, 1 - half], recv1_ref.at[s, rp, cp], d)]
        if stage == 3:
            ref = r_ref.at[s, cp, rp, half]
            return [hop(ref, ref, d)]
        out = []
        rest = [e for e in range(4) if e != d]
        for k in (7, 6, 5, 3, 4, 2, 1):
            dims = [e for i, e in enumerate(rest) if k // 2 ** i % 2]
            if stage == 1:
                out.append(hop(acc_ref.at[s, rp, cp, spot(rp, cp, dims)[2]],
                               recv2_ref.at[s, rp, cp, k - 1], *dims))
            else:
                ref = r_ref.at[s, cp, rp, half, block]
                out.append(hop(ref, ref, *dims))
        return out

    def send(stage, s, rp, cp):
        for copy in hops(stage, s, rp, cp):
            copy.start()

    def send_mixed(stage, s):
        for group in zip(*(hops(stage, s, rp, cp) for rp, cp in parts)):
            for copy in group:
                copy.start()

    def got_all(stage, s):
        ref = recv1_ref if stage in (0, 3) else recv2_ref
        arrived(ref.at[s], r_sem.at[stage, s])


    def forward(s):
        if s == 0:
            weights[0].wait()
            wint_ref[...] = win_ref[...].astype(F32).T.astype(BF16)
            for copy in weights[1:4]:
                copy.wait()
            wcol_ref[...] = jnp.broadcast_to(wden_ref[...].astype(F32), (LANES, hid)).T
        fetch(s).wait()
        place = lax.broadcasted_iota(jnp.int32, (smp, ray), 0)
        sig = jnp.zeros((smp, ray), F32)
        for i in range(smp):
            pre = mm(wint_ref[...], f_ref[s, i], NT)
            h = jnp.maximum(pre, 0.0).astype(BF16)
            hid_ref[s, i] = h
            dense = jnp.sum(h.astype(F32) * jnp.concatenate([wcol_ref[...]] * (ray // LANES), 1), 0, keepdims=True)
            sig = jnp.where(place == i, dense, sig)
        here = pl.ds(s * ray, ray)
        row = lax.broadcasted_iota(jnp.int32, (smp, ray), 0)
        gate = jnp.where(row < cnt_ref[:, here], jnp.broadcast_to(step_ref[:, here], (smp, ray)), 0.0)
        soft = jnp.maximum(sig, 0.0) + jnp.log1p(jnp.exp(-jnp.abs(sig)))
        tau = soft * gate
        inner = running(tau, False)
        t_all[s, me] = (inner + tau)[smp - 1:smp]
        if s == 0:
            pl.semaphore_wait(barrier, BRICKS - 1 + COLS - 1)
        spread_start(t_all.at[s, me], ts_sem.at[0], tr_sem.at[s])
        keep = jnp.exp(-tau)
        light = jnp.exp(-inner)
        lw = light * (1.0 - keep)
        keep_ref[s, 0] = lw
        keep_ref[s, 1] = light * keep
        keep_ref[s, 2] = sig
        keep_ref[s, 3] = gate

    def weigh(s):
        lw = keep_ref[s, 0]
        for t in range(0, hid, 32):
            total = None
            for i in range(smp):
                term = lw[i:i + 1] * hid_ref[s, i, t:t + 32].astype(F32)
                total = term if i == 0 else total + term
            hbar_ref[s, t:t + 32] = total
        if s == 0:
            weights[4].wait()
        high, low = halves(hbar_ref[s])
        value = mm(high, wout_ref[...], TN) + mm(low, wout_ref[...], TN)
        for cp in range(2):
            p_ref[s, cp] = value[:, cp * half_width:(cp + 1) * half_width].reshape(p_ref.shape[2:])

    def reduce_near(s):
        arrived(t_all.at[s, pl.ds(0, BRICKS - 1)], tr_sem.at[s])
        before = jnp.zeros((1, ray), F32)
        for b in range(BRICKS):
            e_all[s, b] = jnp.exp(-before)
            before = before + t_all[s, b]
        row = lax.broadcasted_iota(jnp.int32, (smp, ray), 0)
        table = jnp.broadcast_to(e_all[s, me], (smp, ray))
        for d in range(4):
            table = jnp.where(row == d + 1, jnp.broadcast_to(e_all[s, other(d)], (smp, ray)), table)
        ecol_ref[s] = table.T.reshape(2, 2, half_rays, smp)
        got_all(0, s)
        for rp, cp in parts:
            d, half, _ = spot(rp, cp)
            e = ecol_ref[s, rp, half]
            own = e[:, :1] * p_ref[s, cp, rp, half].reshape(half_rays, half_width)
            got = e[:, d + 1:d + 2] * recv1_ref[s, rp, cp].reshape(half_rays, half_width)
            ps_ref[s, rp, cp, 0] = own
            ps_ref[s, rp, cp, 1] = got
            acc_ref[s, rp, cp] = (own + got).reshape(acc_ref.shape[3:])
        send_mixed(1, s)

    def reduce_far(s):
        if s == 0:
            arrived(tgt_ref, tgt_sem.at[0])
        got_all(1, s)
        for rp, cp in parts:
            _, half, block = spot(rp, cp)
            total = acc_ref[s, rp, cp, block] - tgt_ref[s, rp, cp]
            for k in range(7):
                total = total + recv2_ref[s, rp, cp, k]
            r_ref[s, cp, rp, half, block] = total
        send_mixed(2, s)

    def gather_far(s):
        got_all(2, s)
        for rp, cp in parts:
            send(3, s, rp, cp)
        for i, (rp, cp) in enumerate(parts):
            r = r_ref[s, cp, rp, spot(rp, cp)[1]].reshape(half_rays, half_width)
            for j in range(2):
                prod_ref[pl.ds((2 * i + j) * half_rays, half_rays)] = ps_ref[s, rp, cp, j] * r
        high, low = halves(prod_ref[...])
        ones = jnp.ones((smp, half_width), BF16)
        own_all[s, me] = (mm(ones, high, NT) + mm(ones, low, NT))[:1]
        spread_start(own_all.at[s, me], os_sem.at[0], or_sem.at[s])

    def put_residual(s, cp):
        return pltpu.make_async_copy(
            r_ref.at[s, cp], res_hbm.at[s, :, :, :, :, pl.ds(cp * half_width, half_width)], out_sem.at[0])

    def gather_near(s):
        got_all(3, s)
        for cp in range(2):
            put_residual(s, cp).start()

    def emissions(s):
        gather_near(s)
        b_high, b_low = halves(hbar_ref[s] * e_all[s, me])
        v = None
        out = []
        for cp in range(2):
            r_high, r_low = halves(r_ref[s, cp].reshape(ray, half_width))
            w = wout_ref[:, cp * half_width:(cp + 1) * half_width]
            term = mm(w, r_high, NT) + mm(w, r_low, NT)
            v = term if cp == 0 else v + term
            out.append(mm(b_high, r_high, NN) + mm(b_low, r_high, NN))
        v_ref[s] = v
        out = jnp.concatenate(out, 1)
        for c in range(COLS):
            mine = out[c * slab:(c + 1) * slab]
            go_ref[c % 2, c // 2] = mine if s == 0 else go_ref[c % 2, c // 2] + mine
        if s == STREAMS - 1:
            pair_copy.start()

        row = lax.broadcasted_iota(jnp.int32, (smp, LANES), 0)
        for at in range(0, ray, LANES):
            here = slice(at, at + LANES)
            v = v_ref[s, :, here]
            em = jnp.zeros((smp, LANES), F32)
            for i in range(smp):
                e = jnp.sum(v * hid_ref[s, i, :, here].astype(F32), 0, keepdims=True)
                em = jnp.where(row == i, e, em)
            keep_ref[s, 4, :, here] = em

    def later_bricks(s):
        arrived(own_all.at[s, pl.ds(0, BRICKS - 1)], or_sem.at[s])
        side = lax.broadcasted_iota(jnp.int32, (1, part_rays), 1) // half_rays
        out = []
        for rp in range(2):
            whole = jnp.zeros((1, part_rays), F32)
            for cp in range(2):
                d = 2 * rp + cp
                totals = [jnp.zeros((1, part_rays), F32) for _ in range(2)]
                for source in range(BRICKS):
                    at = (source % RING, source // RING)
                    code = (at[0] ^ at[0] // 2) + RING * (at[1] ^ at[1] // 2)
                    mate = (moved(at[1], d == 2, d == 3) * RING
                            + moved(at[0], d == 0, d == 1))
                    term = own_all[s, source][:, d * part_rays:(d + 1) * part_rays]
                    brick = jnp.where(side == 0, source, mate)
                    half = code >> d & 1
                    totals[half] = totals[half] + jnp.where(brick > me, term, 0.0)
                totals = [t + pltpu.roll(t, half_rays, 1) for t in totals]
                whole = whole + jnp.where(side == 0, totals[0], totals[1])
            out.append(whole)
        return jnp.concatenate(out, 1)

    def gradients(s):
        e = jnp.broadcast_to(e_all[s, me], (smp, ray))
        em = keep_ref[s, 4]
        wgt = keep_ref[s, 0] * e
        later = running(wgt * em, True) + later_bricks(s)
        dens = (keep_ref[s, 1] * e * em - later) * keep_ref[s, 3]
        dens_ref[:, pl.ds(s * ray, ray)] = dens
        dsig = dens / (1.0 + jnp.exp(-keep_ref[s, 2]))
        for at in range(0, ray, LANES):
            here = slice(at, at + LANES)
            for t in range(0, hid, 64):
                down = slice(t, t + 64)
                v = v_ref[s, down, here]
                wden = wcol_ref[down]
                for i in range(smp):
                    dh = wgt[i:i + 1, here] * v + dsig[i:i + 1, here] * wden
                    dpre_ref[down, i * ray + at:i * ray + at + LANES] = jnp.where(
                        hid_ref[s, i, down, here] > 0, dh.astype(BF16), jnp.zeros((), BF16))
        g_in = mm(dpre_ref[...], f_ref[s].reshape(smp * ray, -1), NN)
        gt_ref[...] = g_in if s == 0 else gt_ref[...] + g_in
        d_high, d_low = halves(dsig)
        stacked = jnp.concatenate([d_high.astype(F32), d_low.astype(F32)], 0)
        row = lax.broadcasted_iota(jnp.int32, stacked.shape, 0)
        g_den = jnp.zeros((hid, 2 * smp), F32)
        for i in range(smp):
            g_den = g_den + mm(hid_ref[s, i], jnp.where(row % smp == i, stacked, 0.0).astype(BF16), NT)
        gd_ref[...] = g_den if s == 0 else gd_ref[...] + g_den
        if s == STREAMS - 1:
            turned = gt_ref[...].T
            den = gd_ref[...].T
            gr_ref[...] = jnp.sum(den, 0, keepdims=True)
            gi_ref[...] = turned.reshape(gi_ref.shape)

    x, core = col // 2, col % 2

    def to_col(src, dst, send, recv, who):
        return pltpu.make_async_remote_copy(
            src_ref=src, dst_ref=dst, send_sem=send, recv_sem=recv,
            device_id={"col": who}, device_id_type=mesh_id)

    pair_copy = to_col(go_ref.at[1 - core], go_pair, gs_sem.at[0], gr_sem.at[0], x * 2 + 1 - core)

    def share_out():
        pair_copy.wait_recv()
        go_sum[...] = go_ref[core] + go_pair[...]
        for j in (2, 1, 3):
            to = (x + j) % RING
            to_col(go_sum.at[to], go_recv.at[j - 1], gs_sem.at[1], gr_sem.at[1], to * 2 + core).start()

    def share_in(j, _):
        to = (col + j) % COLS
        to_col(gi_ref.at[to], gi_recv.at[j - 1], gs_sem.at[2], gr_sem.at[2], to).start()
        to_col(gr_ref, gr_recv.at[j - 1], gs_sem.at[3], gr_sem.at[3], to).start()
        return 0

    for s in range(STREAMS):
        forward(s)
        weigh(s)
        for rp, cp in parts:
            send(0, s, rp, cp)
    for step, s in ORDER:
        (reduce_near, reduce_far, gather_far, emissions, gradients)[step](s)
    for j in (4, 3, 5, 2, 6, 1, 7):
        share_in(j, 0)
    share_out()
    dens_copy = pltpu.make_async_copy(dens_ref, dens_hbm, out_sem.at[1])
    dens_copy.start()
    arrived(go_recv, gr_sem.at[1])
    total = go_sum[x]
    for j in range(RING - 1):
        total = total + go_recv[j]
    gout_ref[...] = total
    gout_copy = pltpu.make_async_copy(gout_ref, gout_hbm, out_sem.at[2])
    gout_copy.start()
    arrived(recv1_ref, s_sem.at[0])
    arrived(recv2_ref, s_sem.at[1])
    arrived(recv2_ref, s_sem.at[2])
    arrived(recv1_ref, s_sem.at[3])
    arrived(t_all.at[:, pl.ds(0, BRICKS - 1)], ts_sem.at[0])
    arrived(own_all.at[:, pl.ds(0, BRICKS - 1)], os_sem.at[0])
    pair_copy.wait_send()
    arrived(go_recv, gs_sem.at[1])
    arrived(r_ref, out_sem.at[0])
    dens_copy.wait()
    arrived(gi_recv, gr_sem.at[2])
    total = gi_ref[col]
    for j in range(COLS - 1):
        total = total + gi_recv[j]
    gin_ref[:slab] = total
    arrived(gr_recv, gr_sem.at[3])
    total = gr_ref[...]
    for j in range(COLS - 1):
        total = total + gr_recv[j]
    gin_ref[slab:] = jnp.broadcast_to(total, (smp, hid))
    gin_copy = pltpu.make_async_copy(gin_ref, gin_hbm, out_sem.at[3])
    gin_copy.start()
    arrived(gi_recv, gs_sem.at[2])
    arrived(gr_recv, gs_sem.at[3])
    gout_copy.wait()
    gin_copy.wait()


def finish(res_in, dens_in, gin_in, gout_in, res_hbm, dens_hbm, gin_hbm, gden_hbm, gout_hbm,
           held, dens_ref, gin_ref, gout_ref, gden_ref, in_sem, out_sem):
    parts = res_in.shape[0]
    slab = gin_hbm.shape[0]
    take = [pltpu.make_async_copy(src, dst, in_sem.at[i]) for i, (src, dst) in enumerate(
        [(gin_in, gin_ref), (dens_in, dens_ref), (gout_in, gout_ref)]
        + [(res_in.at[i], held.at[i]) for i in range(parts)])]
    put = [pltpu.make_async_copy(src, dst, out_sem.at[i]) for i, (src, dst) in enumerate(
        [(gin_ref.at[pl.ds(0, slab)], gin_hbm), (dens_ref, dens_hbm), (gout_ref, gout_hbm)]
        + [(held.at[i], res_hbm.at[i]) for i in range(parts)] + [(gden_ref, gden_hbm)])]
    for copy in take:
        copy.start()
    for got, gone in zip(take, put):
        got.wait()
        gone.start()
    den = gin_ref[slab:slab + 1]
    col = lax.axis_index("col")
    mine = den[:, :slab]
    for c in range(1, COLS):
        mine = jnp.where(col == c, den[:, c * slab:(c + 1) * slab], mine)
    gden_ref[...] = mine
    put[-1].start()
    for copy in put:
        copy.wait()


def per_device(features, counts, steps, target, w_in, w_density, w_out):
    _, smp, nray, din = features.shape
    hid, width = w_out.shape[1:]
    ray = nray // STREAMS
    half_rays = ray // 4
    half_width = width // 2
    block = half_rays // 8
    slab = din // COLS
    hbm = pl.BlockSpec(memory_space=pl.ANY)
    dma = pltpu.SemaphoreType.DMA
    split = (STREAMS, 2, 2, 8, block, width)
    quads = (STREAMS, 2, 2)
    scratch = [
        pltpu.VMEM((1, nray), jnp.int32),
        pltpu.VMEM((1, nray), F32),
        pltpu.VMEM((din, hid), BF16),
        pltpu.VMEM((1, hid), BF16),
        pltpu.VMEM((hid, width), BF16),
        pltpu.VMEM((smp, nray), F32),
        pltpu.VMEM((slab + smp, hid), F32),
        pltpu.VMEM((slab, width), F32),
        pltpu.VMEM((hid, din), BF16),
        pltpu.VMEM((hid, LANES), F32),
        pltpu.VMEM((STREAMS, smp, ray, din), BF16),
        pltpu.VMEM((STREAMS, smp, hid, ray), BF16),
        pltpu.VMEM((STREAMS, hid, ray), F32),
        pltpu.VMEM((*quads, 2, 8, block, half_width), F32),
        pltpu.VMEM((*quads, 2, half_rays, half_width), F32),
        pltpu.VMEM((*quads, 8, block, half_width), F32),
        pltpu.VMEM((*quads, 8, block, half_width), F32),
        pltpu.VMEM((*quads, 7, block, half_width), F32),
        pltpu.VMEM((*quads, 2, 8, block, half_width), F32),
        pltpu.VMEM((2 * ray, half_width), F32),
        pltpu.VMEM((*quads, block, half_width), F32),
        pltpu.VMEM((STREAMS, BRICKS, 1, ray), F32),
        pltpu.VMEM((STREAMS, BRICKS, 1, ray), F32),
        pltpu.VMEM((STREAMS, BRICKS, 1, 2 * ray), F32),
        pltpu.VMEM((STREAMS, 2, 2, half_rays, smp), F32),
        pltpu.VMEM((STREAMS, 5, smp, ray), F32),
        pltpu.VMEM((STREAMS, hid, ray), F32),
        pltpu.VMEM((hid, smp * ray), BF16),
        pltpu.VMEM((hid, din), F32),
        pltpu.VMEM((hid, 2 * smp), F32),
        pltpu.VMEM((COLS, slab, hid), F32),
        pltpu.VMEM((2, RING, slab, width), F32),
        pltpu.VMEM((COLS - 1, slab, hid), F32),
        pltpu.VMEM((1, hid), F32),
        pltpu.VMEM((COLS - 1, 1, hid), F32),
        pltpu.VMEM((RING, slab, width), F32),
        pltpu.VMEM((RING, slab, width), F32),
        pltpu.VMEM((RING - 1, slab, width), F32),
        dma((5,)), dma((STREAMS,)), dma((1,)), dma((4,)),
        dma((4,)), dma((4, STREAMS)),
        dma((1,)), dma((STREAMS,)), dma((1,)), dma((STREAMS,)),
        dma((4,)), dma((4,)),
    ]
    residual, dens, g_in, g_out = pl.pallas_call(
        body,
        out_shape=(
            jax.ShapeDtypeStruct(split, F32),
            jax.ShapeDtypeStruct((smp, nray), F32),
            jax.ShapeDtypeStruct((slab + smp, hid), F32),
            jax.ShapeDtypeStruct((slab, width), F32),
        ),
        in_specs=[hbm] * 7,
        out_specs=(hbm,) * 4,
        scratch_shapes=scratch,
        compiler_params=pltpu.CompilerParams(
            collective_id=0, has_side_effects=True, vmem_limit_bytes=60 * 1024 * 1024),
        name="brick_step",
    )(features[0], counts, steps, target.reshape(split), w_in[0], w_density, w_out[0])
    residual, dens, g_in, g_den, g_out = pl.pallas_call(
        finish,
        out_shape=(
            jax.ShapeDtypeStruct((8, nray // 8, width), F32),
            jax.ShapeDtypeStruct((smp, nray), F32),
            jax.ShapeDtypeStruct((slab, hid), F32),
            jax.ShapeDtypeStruct((1, slab), F32),
            jax.ShapeDtypeStruct((slab, width), F32),
        ),
        in_specs=[hbm] * 4,
        out_specs=(hbm,) * 5,
        scratch_shapes=[
            pltpu.VMEM((8, nray // 8, width), F32),
            pltpu.VMEM((smp, nray), F32),
            pltpu.VMEM((slab + smp, hid), F32),
            pltpu.VMEM((slab, width), F32),
            pltpu.VMEM((1, slab), F32),
            dma((11,)), dma((12,)),
        ],
        name="brick_finish",
    )(residual.reshape(8, nray // 8, width), dens, g_in, g_out)
    return residual.reshape(nray, width), dens[None], g_in[None], g_den, g_out[None]


def solution(mesh):
    return jax.shard_map(
        per_device,
        mesh=mesh,
        in_specs=(
            P("depth", None, "col", None),
            P("depth", "col"),
            P("depth", "col"),
            P("col", None),
            P("depth", None, None),
            P("depth", None),
            P("depth", None, None),
        ),
        out_specs=(
            P("col", None),
            P("depth", None, "col"),
            P("depth", "col", None),
            P("depth", "col"),
            P("depth", "col", None),
        ),
        check_vma=False,
    )
```
